32 devices in a mesh: dp: 16 (over z, x, core), tensor: 2 (over y).
Axes of the slice: x: 2, y: 2, z: 4, core: 2. Of those that a mesh axis runs over, the one named last changes fastest.
Arguments:
- layer_input: bfloat16 [2, 8192, 1024], P(None, ('dp', 'tensor')), may hold values from -6 to 6
- segment_ids: int32 [2, 8192], P(None, 'dp'), may hold values from 0 to 5, as said below
- qkv_weight: bfloat16 [3, 1024, 1024], P(None, 'dp', 'tensor'), may hold values from -0.1875 to 0.1875
- qv_bias: bfloat16 [2, 16, 64], P(None, 'tensor', 'dp'), may hold values from -3 to 3
- out_weight: bfloat16 [1024, 1024], P('tensor', 'dp'), may hold values from -1 to 1
- up_weight: bfloat16 [1024, 4096], P('dp', 'tensor'), may hold values from -0.1875 to 0.1875
- up_bias: bfloat16 [2, 2048], P('tensor', 'dp'), may hold values from -3 to 3
- down_weight: bfloat16 [4096, 1024], P('tensor', 'dp'), may hold values from -0.09375 to 0.09375
- norm_gains: float32 [2, 1024], P(None, ('dp', 'tensor')), may hold values from 0.1 to 1.9
- row_biases: float32 [4, 1024], P(None, ('dp', 'tensor')), may hold values from -2 to 2
- cotangent: bfloat16 [2, 8192, 1024], P(None, ('dp', 'tensor')), may hold values from -6 to 6
Outputs:
- layer_output: bfloat16 [2, 8192, 1024], P(None, ('dp', 'tensor'))
- input_grad: bfloat16 [2, 8192, 1024], P(None, ('dp', 'tensor'))
- qkv_weight_grad: float32 [3, 1024, 1024], P(None, 'dp', 'tensor')
- qv_bias_grad: float32 [2, 16, 64], P(None, 'tensor', 'dp')
- out_weight_grad: float32 [1024, 1024], P('tensor', 'dp')
- up_weight_grad: float32 [1024, 4096], P('dp', 'tensor')
- up_bias_grad: float32 [2, 2048], P('tensor', 'dp')
- down_weight_grad: float32 [4096, 1024], P('tensor', 'dp')
- norm_gains_grad: float32 [2, 1024], P(None, ('dp', 'tensor'))
- row_biases_grad: float32 [4, 1024], P(None, ('dp', 'tensor'))
The draws below stay inside these ranges and needn't reach their ends.
Inputs may be any that keep to these rules, and one draw needn't show every extreme that they name: `segment_ids`: within every sequence of 512 rows, documents 1 to 5 follow one another in order, each 20 to 100 tokens long, and padding with id 0 fills the rest, 12 tokens or more.
All inputs are finite; a program needn't handle non-finite values.
Results may differ from the reference program's by a relative error of at most 0.02.
Values may be sent and summed in bfloat16 or wider, within the bound.
No kernel may reach another device: no remote copies, remote signals or barrier semaphores. Data moves between devices by JAX's collectives and lax.ppermute only.
A program may use at most 192 MiB of HBM per device.

```python
import math
import jax
import jax.numpy as jnp
from jax import lax

D = 1024
HEADS = 16
HEAD_DIM = 64
FF = 4096
LEN = 512
NDOC = 5
MICRO = 2
DOC_MOST = 100
DOC_LEAST = 20
ROWS = 8192
N_DP = 16
N_TENSOR = 2


def draw_segment_ids(key, part):
    sequences = ROWS // LEN
    lengths = jax.random.randint(key, (MICRO, sequences, NDOC), DOC_LEAST, DOC_MOST + 1)
    ends = jnp.cumsum(lengths, axis=-1)
    positions = jnp.arange(LEN)
    counted = 1 + jnp.sum((positions[:, None] >= ends[:, :, None, :]).astype(jnp.int32), axis=-1)
    labels = jnp.where(counted > NDOC, 0, counted)
    return labels.reshape(MICRO, ROWS).astype(jnp.int32)


def spiked(array, own_key, source, target, parts, factor):
    def block_of(dim):
        return (jnp.arange(array.shape[dim]) // (array.shape[dim] // parts)).reshape((-1,) + (1,) * (array.ndim - 1 - dim))

    near = jax.random.permutation(own_key, parts)[block_of(target)]
    other_side = (block_of(target) + parts // 2) % parts
    return jnp.where((block_of(source) == near) | (block_of(source) == other_side), factor * array, array)


def level_of(key, shape, cuts, least, high):
    factor_of = 1.0
    for axis_at, shards_of in cuts:
        heights = jax.random.uniform(jax.random.fold_in(jax.random.fold_in(key, 6), axis_at), (shards_of,), jnp.float32, least / len(cuts), high / len(cuts))
        factor_of = factor_of * jnp.repeat(jnp.exp(heights), shape[axis_at] // shards_of).reshape((-1,) + (1,) * (len(shape) - 1 - axis_at))
    return factor_of


def bell_draw(key, dims, scale, reach, cuts=(), dtype=jnp.bfloat16):
    drawn = jax.random.normal(key, dims, jnp.float32) * scale
    if len(cuts) > 0:
        drawn = level_of(key, dims, cuts, -0.22, 0.18) * drawn
    return jnp.clip(drawn, min=-reach, max=reach).astype(dtype)


def noise_with(key, dims, scale, reach, pieces, heavy, kind=jnp.bfloat16):
    entries = scale * jax.random.normal(key, dims, jnp.float32)
    if pieces:
        entries = entries * level_of(key, dims, pieces, -0.22, 0.18)
    return jnp.clip(spiked(entries, jax.random.fold_in(key, 3), *heavy), -reach, reach).astype(kind)


def setup_inputs(seed: int = 0) -> dict:
    splits = jax.random.split(jax.random.key(seed), 12)
    return {
        "layer_input": noise_with(splits[0], (MICRO, ROWS, D), 1.0, 6.0, ((1, 32),), (1, 2, 32, 2.75)),
        "segment_ids": draw_segment_ids(jax.random.fold_in(splits[11], 71), 0),
        "qkv_weight": bell_draw(splits[2], (3, D, D), D ** -0.5, 0.1875, ((1, 16), (2, 2))),
        "qv_bias": bell_draw(splits[3], (2, HEADS, HEAD_DIM), 0.5, 3.0, ((1, 2), (2, 16))),
        "out_weight": bell_draw(splits[4], (D, D), (D // 32) ** -0.5, 1.0, ((0, 2), (1, 16))),
        "up_weight": bell_draw(splits[5], (D, FF), D ** -0.5, 0.1875, ((0, 16), (1, 2))),
        "up_bias": bell_draw(splits[6], (N_TENSOR, FF // N_TENSOR), 0.5, 3.0, ((0, 2), (1, 16))),
        "down_weight": bell_draw(splits[7], (FF, D), FF ** -0.5, 0.09375, ((0, 2), (1, 16))),
        "norm_gains": jnp.clip(1.0 + 0.18 * jax.random.normal(splits[8], (2, D), jnp.float32), 0.1, 1.9),
        "row_biases": bell_draw(splits[9], (4, D), 0.3, 2.0, ((1, 32),), jnp.float32),
        "cotangent": noise_with(splits[10], (MICRO, ROWS, D), 1.0, 6.0, ((1, 32),), (1, 2, 32, 2.75)),
    }


@jax.custom_vjp
def low(v):
    return lax.optimization_barrier(v.astype(jnp.bfloat16)).astype(jnp.float32)

@jax.custom_vjp
def low_back(v):
    return v

def low_keep(v):
    return (low(v), None)

def low_pass(kept, grad):
    return (grad,)

def back_keep(v):
    return (v, None)

def back_low(kept, grad):
    return (low(grad),)
low.defvjp(low_keep, low_pass)
low_back.defvjp(back_keep, back_low)

def layer_norm(rows, gain, shift):
    centered = rows - lax.optimization_barrier(jnp.mean(rows, axis=-1, keepdims=True))
    variance = lax.optimization_barrier(jnp.mean(centered * centered, axis=-1, keepdims=True))
    return centered * lax.rsqrt(variance + 1e-05) * gain + shift

def forward(weights, rows, segments):
    qkv_weight, qv_bias, out_weight, up_weight, up_bias, down_weight, norm_gains, row_biases = weights
    highest = lax.Precision.HIGHEST
    group, length, width = rows.shape
    projected = jnp.einsum('bld,kde->kble', rows, qkv_weight, precision=highest)
    biases_qv = qv_bias.reshape(2, width)
    query = low(low_back(projected[0] + biases_qv[0]))
    keys = low(low_back(projected[1]))
    values = low(low_back(projected[2] + biases_qv[1]))
    split = (group, length, HEADS, HEAD_DIM)
    scores = jnp.einsum('bqhd,bkhd->bhqk', query.reshape(split), keys.reshape(split), precision=highest) * HEAD_DIM ** (-0.5)
    scores = low_back(scores)
    keep_mask = (segments[:, :, None] == segments[:, None, :])[:, None]
    masked = jnp.where(keep_mask, scores, -1e+30)
    shifted = jnp.exp(masked - lax.optimization_barrier(jnp.max(masked, axis=-1, keepdims=True)))
    probs = low(shifted / lax.optimization_barrier(jnp.sum(shifted, axis=-1, keepdims=True)))
    context = jnp.einsum('bhqk,bkhd->bqhd', probs, values.reshape(split), precision=highest).reshape(group, length, width)
    context = low(low_back(context))
    attention = low_back(jnp.einsum('blc,cd->bld', context, out_weight, precision=highest))
    hidden = layer_norm(rows + attention + row_biases[0], norm_gains[0], row_biases[1])
    upper = low_back(jnp.einsum('bld,df->blf', low(hidden), up_weight, precision=highest) + up_bias.reshape(-1))
    activated = low(jax.nn.gelu(upper, approximate=False))
    branch = low_back(jnp.einsum('blf,fd->bld', activated, down_weight, precision=highest))
    return layer_norm(hidden + branch + row_biases[2], norm_gains[1], row_biases[3])

def reference(layer_input, segment_ids, qkv_weight, qv_bias, out_weight, up_weight, up_bias, down_weight, norm_gains, row_biases, cotangent):
    params = tuple((item.astype(jnp.float32) for item in (qkv_weight, qv_bias, out_weight, up_weight, up_bias, down_weight, norm_gains, row_biases)))
    sequences = MICRO * N_DP
    group = math.gcd(sequences, max(1, 4096 // LEN))
    blocks = sequences // group
    inputs = layer_input.astype(jnp.float32).reshape(blocks, group, LEN, D)
    segments = segment_ids.reshape(blocks, group, LEN)
    grads_in = cotangent.astype(jnp.float32).reshape(blocks, group, LEN, D)

    def step(totals, block):
        rows, block_segments, grads = block
        result, pullback = jax.vjp(lambda weights, values: forward(weights, values, block_segments), params, rows)
        weight_grads, row_grads = pullback(grads)
        totals = jax.tree.map(lambda first, second: first + second, totals, weight_grads)
        return (totals, (result.astype(jnp.bfloat16), row_grads.astype(jnp.bfloat16)))
    zeros = jax.tree.map(jnp.zeros_like, params)
    totals, (outputs, input_grads) = lax.scan(step, zeros, (inputs, segments, grads_in))
    outputs = outputs.reshape(MICRO, N_DP * LEN, D)
    input_grads = input_grads.reshape(MICRO, N_DP * LEN, D)
    return (outputs, input_grads, totals[0], totals[1], totals[2], totals[3], totals[4], totals[5], totals[6], totals[7])
```

```python
import jax
import jax.numpy as jnp
from jax import lax
from jax.experimental import pallas as pl
from jax.experimental.pallas import tpu as pltpu
from jax.sharding import PartitionSpec as P

HEAD_DIM = 64


def gelu_exact(values):
    return jax.nn.gelu(values, approximate=False)


def normalize(rows, gain, shift):
    centered = rows - jnp.mean(rows, axis=-1, keepdims=True)
    variance = jnp.mean(centered * centered, axis=-1, keepdims=True)
    inverse = lax.rsqrt(variance + 1e-05)
    normed = centered * inverse
    return (normed * gain + shift, normed, inverse)


def norm_back(grad, normed, inverse, gain):
    scaled = grad * gain
    return inverse * (
        scaled
        - jnp.mean(scaled, axis=-1, keepdims=True)
        - normed * jnp.mean(scaled * normed, axis=-1, keepdims=True)
    )


def attend(query, keys, values, keep_mask, scale):
    scores = jnp.einsum("qhd,khd->hqk", query, keys, preferred_element_type=jnp.float32) * scale
    masked = jnp.where(keep_mask[None], scores, -1e30)
    highest = jnp.max(masked, axis=-1, keepdims=True)
    shifted = jnp.exp(masked - highest)
    totals = jnp.sum(shifted, axis=-1, keepdims=True)
    probs = (shifted / totals).astype(jnp.bfloat16)
    context = jnp.einsum("hqk,khd->qhd", probs, values, preferred_element_type=jnp.float32)
    return (context, highest + jnp.log(totals))


def attend_back(query, keys, values, keep_mask, logsumexp, grad_context, scale):
    scores = jnp.einsum("qhd,khd->hqk", query, keys, preferred_element_type=jnp.float32) * scale
    masked = jnp.where(keep_mask[None], scores, -1e30)
    probs = jnp.exp(masked - logsumexp)
    probs_low = probs.astype(jnp.bfloat16)
    grad_values = jnp.einsum(
        "hqk,qhd->khd", probs_low, grad_context, preferred_element_type=jnp.float32
    )
    grad_probs = jnp.einsum(
        "qhd,khd->hqk", grad_context, values, preferred_element_type=jnp.float32
    )
    grad_scores = probs * (grad_probs - jnp.sum(probs * grad_probs, axis=-1, keepdims=True))
    grad_low = grad_scores.astype(jnp.bfloat16)
    grad_query = (
        jnp.einsum("hqk,khd->qhd", grad_low, keys, preferred_element_type=jnp.float32) * scale
    )
    grad_keys = (
        jnp.einsum("hqk,qhd->khd", grad_low, query, preferred_element_type=jnp.float32) * scale
    )
    return (grad_query, grad_keys, grad_values)


def tensor_split(
    layer_input,
    segment_ids,
    qkv_weight,
    qv_bias,
    out_weight,
    up_weight,
    up_bias,
    down_weight,
    norm_gains,
    row_biases,
    cotangent,
):
    gains_all, biases_all = (
        lax.all_gather(norm_gains, ("dp", "tensor"), axis=1, tiled=True),
        lax.all_gather(row_biases, ("dp", "tensor"), axis=1, tiled=True),
    )
    shards = (qkv_weight, qv_bias, out_weight, up_weight, up_bias, down_weight)
    dp_count = lax.axis_size("dp")
    seq_len = segment_ids.shape[1]
    heads_local = qv_bias.shape[1]
    width_local = heads_local * HEAD_DIM
    scale = HEAD_DIM ** (-0.5)

    def micro_step(carry, inputs):
        rows_in, segments, grad_rows = inputs
        qkv_full, qv_full, out_full, up_full, upb_full, down_full = (
            lax.all_gather(shards[0], "dp", axis=1, tiled=True),
            lax.all_gather(shards[1], "dp", axis=2, tiled=True),
            lax.all_gather(shards[2], "dp", axis=1, tiled=True),
            lax.all_gather(shards[3], "dp", axis=0, tiled=True),
            lax.all_gather(shards[4], "dp", axis=1, tiled=True),
            lax.all_gather(shards[5], "dp", axis=1, tiled=True),
        )
        gathered = lax.all_gather(rows_in, "tensor", axis=0, tiled=True)
        projected = jnp.einsum(
            "rd,kdc->krc", gathered, qkv_full, preferred_element_type=jnp.float32
        )
        bias_flat = qv_full.reshape(2, width_local).astype(jnp.float32)
        split = (seq_len, heads_local, HEAD_DIM)
        query = (projected[0] + bias_flat[0]).astype(jnp.bfloat16).reshape(split)
        keys = projected[1].astype(jnp.bfloat16).reshape(split)
        values = (projected[2] + bias_flat[1]).astype(jnp.bfloat16).reshape(split)
        keep_mask = segments[:, None] == segments[None, :]
        attended, logsumexp = attend(query, keys, values, keep_mask, scale)
        context = attended.reshape(seq_len, width_local).astype(jnp.bfloat16)
        attention = lax.psum_scatter(
            jnp.dot(context, out_full, preferred_element_type=jnp.float32).astype(jnp.bfloat16),
            "tensor",
            scatter_dimension=0,
            tiled=True,
        ).astype(jnp.float32)
        residual_one = rows_in.astype(jnp.float32) + attention + biases_all[0]
        hidden, normed_one, inverse_one = normalize(residual_one, gains_all[0], biases_all[1])
        hidden_rows = lax.all_gather(hidden.astype(jnp.bfloat16), "tensor", axis=0, tiled=True)
        upper = jnp.dot(
            hidden_rows, up_full, preferred_element_type=jnp.float32
        ) + upb_full.reshape(-1).astype(jnp.float32)
        activated = gelu_exact(upper).astype(jnp.bfloat16)
        branch = lax.psum_scatter(
            jnp.dot(activated, down_full, preferred_element_type=jnp.float32).astype(jnp.bfloat16),
            "tensor",
            scatter_dimension=0,
            tiled=True,
        ).astype(jnp.float32)
        residual_two = hidden + branch + biases_all[2]
        result, normed_two, inverse_two = normalize(residual_two, gains_all[1], biases_all[3])
        qkv_back, qv_back, out_back, up_back, upb_back, down_back = (
            lax.all_gather(shards[0], "dp", axis=1, tiled=True),
            lax.all_gather(shards[1], "dp", axis=2, tiled=True),
            lax.all_gather(shards[2], "dp", axis=1, tiled=True),
            lax.all_gather(shards[3], "dp", axis=0, tiled=True),
            lax.all_gather(shards[4], "dp", axis=1, tiled=True),
            lax.all_gather(shards[5], "dp", axis=1, tiled=True),
        )
        grad_output = grad_rows.astype(jnp.float32)
        gain_two_grad = jnp.sum(grad_output * normed_two, axis=0)
        shift_two_grad = jnp.sum(grad_output, axis=0)
        grad_two = norm_back(grad_output, normed_two, inverse_two, gains_all[1])
        down_bias_grad = jnp.sum(grad_two, axis=0)
        branch_rows = lax.all_gather(grad_two.astype(jnp.bfloat16), "tensor", axis=0, tiled=True)
        down_grad = jnp.einsum(
            "rf,rd->fd", activated, branch_rows, preferred_element_type=jnp.float32
        )
        grad_active = jnp.einsum(
            "rd,fd->rf", branch_rows, down_back, preferred_element_type=jnp.float32
        )
        gelu_pull = jax.vjp(gelu_exact, upper)[1]
        grad_upper = gelu_pull(grad_active)[0].astype(jnp.bfloat16)
        up_bias_grad = jnp.sum(grad_upper.astype(jnp.float32), axis=0).reshape(1, -1)
        up_grad = jnp.einsum(
            "rd,rf->df", hidden_rows, grad_upper, preferred_element_type=jnp.float32
        )
        grad_hidden = grad_two + lax.psum_scatter(
            jnp.einsum("rf,df->rd", grad_upper, up_back, preferred_element_type=jnp.float32).astype(
                jnp.bfloat16
            ),
            "tensor",
            scatter_dimension=0,
            tiled=True,
        ).astype(jnp.float32)
        gain_one_grad = jnp.sum(grad_hidden * normed_one, axis=0)
        shift_one_grad = jnp.sum(grad_hidden, axis=0)
        grad_one = norm_back(grad_hidden, normed_one, inverse_one, gains_all[0])
        out_bias_grad = jnp.sum(grad_one, axis=0)
        attention_rows = lax.all_gather(grad_one.astype(jnp.bfloat16), "tensor", axis=0, tiled=True)
        out_grad = jnp.einsum(
            "rc,rd->cd", context, attention_rows, preferred_element_type=jnp.float32
        )
        grad_context = (
            jnp.einsum("rd,cd->rc", attention_rows, out_back, preferred_element_type=jnp.float32)
            .astype(jnp.bfloat16)
            .reshape(split)
        )
        grad_query, grad_keys, grad_values = attend_back(
            query, keys, values, keep_mask, logsumexp, grad_context, scale
        )
        grad_qkv = (
            jnp.stack([grad_query, grad_keys, grad_values])
            .reshape(3, seq_len, width_local)
            .astype(jnp.bfloat16)
        )
        bias_sums = jnp.sum(jnp.stack([grad_qkv[0], grad_qkv[2]]).astype(jnp.float32), axis=1)
        qv_grad = bias_sums.reshape(2, heads_local, HEAD_DIM)
        qkv_grad = jnp.einsum("rd,krc->kdc", gathered, grad_qkv, preferred_element_type=jnp.float32)
        input_grad = (
            grad_one
            + lax.psum_scatter(
                jnp.einsum(
                    "krc,kdc->rd", grad_qkv, qkv_back, preferred_element_type=jnp.float32
                ).astype(jnp.bfloat16),
                "tensor",
                scatter_dimension=0,
                tiled=True,
            ).astype(jnp.float32)
        ).astype(jnp.bfloat16)
        gains_grad = jnp.stack([gain_one_grad, gain_two_grad])
        biases_grad = jnp.stack([out_bias_grad, shift_one_grad, down_bias_grad, shift_two_grad])
        updates = (
            qkv_grad,
            qv_grad,
            out_grad,
            up_grad,
            up_bias_grad,
            down_grad,
            gains_grad,
            biases_grad,
        )
        carry = tuple((total + update for total, update in zip(carry, updates)))
        return (carry, (result.astype(jnp.bfloat16), input_grad))

    initial = (
        jnp.zeros((3, qkv_weight.shape[1] * dp_count, qkv_weight.shape[2]), jnp.float32),
        jnp.zeros((2, qv_bias.shape[1], qv_bias.shape[2] * dp_count), jnp.float32),
        jnp.zeros((out_weight.shape[0], out_weight.shape[1] * dp_count), jnp.float32),
        jnp.zeros((up_weight.shape[0] * dp_count, up_weight.shape[1]), jnp.float32),
        jnp.zeros((1, up_bias.shape[1] * dp_count), jnp.float32),
        jnp.zeros((down_weight.shape[0], down_weight.shape[1] * dp_count), jnp.float32),
        jnp.zeros(gains_all.shape, jnp.float32),
        jnp.zeros(biases_all.shape, jnp.float32),
    )
    totals, (outputs, input_grads) = lax.scan(
        micro_step, initial, (layer_input, segment_ids, cotangent)
    )
    qkv_sum, qv_sum, out_sum, up_sum, upb_sum, down_sum = (
        lax.psum_scatter(
            totals[0].astype(jnp.bfloat16), "dp", scatter_dimension=1, tiled=True
        ).astype(jnp.float32),
        lax.psum_scatter(
            totals[1].astype(jnp.bfloat16), "dp", scatter_dimension=2, tiled=True
        ).astype(jnp.float32),
        lax.psum_scatter(
            totals[2].astype(jnp.bfloat16), "dp", scatter_dimension=1, tiled=True
        ).astype(jnp.float32),
        lax.psum_scatter(
            totals[3].astype(jnp.bfloat16), "dp", scatter_dimension=0, tiled=True
        ).astype(jnp.float32),
        lax.psum_scatter(
            totals[4].astype(jnp.bfloat16), "dp", scatter_dimension=1, tiled=True
        ).astype(jnp.float32),
        lax.psum_scatter(
            totals[5].astype(jnp.bfloat16), "dp", scatter_dimension=1, tiled=True
        ).astype(jnp.float32),
    )
    gains_sum, biases_sum = (
        lax.psum_scatter(totals[6], ("dp", "tensor"), scatter_dimension=1, tiled=True),
        lax.psum_scatter(totals[7], ("dp", "tensor"), scatter_dimension=1, tiled=True),
    )
    return (
        outputs,
        input_grads,
        qkv_sum,
        qv_sum,
        out_sum,
        up_sum,
        upb_sum,
        down_sum,
        gains_sum,
        biases_sum,
    )


NEGATIVE = -1e30
LANES = 2 * HEAD_DIM


def half_mask(shape, half):
    lane = lax.broadcasted_iota(jnp.int32, shape, 1)
    return (lane // HEAD_DIM) == half


def attend_kernel(q_ref, k_ref, v_ref, row_ref, col_ref, context_ref, stats_ref):
    query, keys, values = q_ref[...], k_ref[...], v_ref[...]
    keep = col_ref[...] == row_ref[...]
    total = jnp.zeros(context_ref.shape, jnp.float32)
    for half in range(2):
        own = half_mask(query.shape, half)
        masked_query = jnp.where(own, query, 0) * jnp.asarray(HEAD_DIM**-0.5, query.dtype)
        scores = lax.dot_general(
            keys, masked_query, (((1,), (1,)), ((), ())), preferred_element_type=jnp.float32
        )
        scores = jnp.where(keep, scores, NEGATIVE)
        highest = jnp.max(scores, axis=0, keepdims=True)
        shifted = jnp.exp(scores - highest)
        sums = jnp.sum(shifted, axis=0, keepdims=True)
        probs = (shifted * (1.0 / sums)).astype(jnp.bfloat16)
        own_values = jnp.where(own, values, 0)
        total += lax.dot_general(
            probs, own_values, (((0,), (0,)), ((), ())), preferred_element_type=jnp.float32
        )
        stats_ref[0, half : half + 1, :] = highest + jnp.log(sums)
    context_ref[...] = total.astype(context_ref.dtype)


def attend_back_kernel(
    q_ref, k_ref, v_ref, grad_ref, row_ref, col_ref, stats_ref, dq_ref, dk_ref, dv_ref
):
    query, keys, values, grad = q_ref[...], k_ref[...], v_ref[...], grad_ref[...]
    scale = jnp.asarray(HEAD_DIM**-0.5, query.dtype)
    keep = col_ref[...] == row_ref[...]
    zero = jnp.zeros(dq_ref.shape, jnp.float32)
    grad_query, grad_keys, grad_values = zero, zero, zero
    for half in range(2):
        own = half_mask(query.shape, half)
        own_query = jnp.where(own, query, 0) * scale
        own_keys = jnp.where(own, keys, 0) * scale
        own_grad = jnp.where(own, grad, 0)
        contract_last = (((1,), (1,)), ((), ()))
        scores = lax.dot_general(
            keys, own_query, contract_last, preferred_element_type=jnp.float32
        )
        scores = jnp.where(keep, scores, NEGATIVE)
        probs = jnp.exp(scores - stats_ref[0, half : half + 1, :])
        grad_values += jnp.dot(
            probs.astype(jnp.bfloat16), own_grad, preferred_element_type=jnp.float32
        )
        grad_probs = lax.dot_general(
            values, own_grad, contract_last, preferred_element_type=jnp.float32
        )
        weighted = probs * grad_probs
        grad_scores = (weighted - probs * jnp.sum(weighted, axis=0, keepdims=True)).astype(
            jnp.bfloat16
        )
        grad_keys += jnp.dot(grad_scores, own_query, preferred_element_type=jnp.float32)
        grad_query += lax.dot_general(
            grad_scores, own_keys, (((0,), (0,)), ((), ())), preferred_element_type=jnp.float32
        )
    dq_ref[...] = grad_query.astype(dq_ref.dtype)
    dk_ref[...] = grad_keys.astype(dk_ref.dtype)
    dv_ref[...] = grad_values.astype(dv_ref.dtype)


def attention_specs(rows, pairs):
    def column(offset):
        return pl.BlockSpec((rows, LANES), lambda i, offset=offset: (0, offset + i))

    row_ids = pl.BlockSpec((1, rows), lambda i: (0, 0))
    column_ids = pl.BlockSpec((rows, 1), lambda i: (0, 0))
    stats = pl.BlockSpec((1, 2, rows), lambda i: (i, 0, 0))
    return column, row_ids, column_ids, stats


def attend_call(projected, segments):
    rows, width = projected.shape[0], projected.shape[1] // 3
    pairs = width // LANES
    column, row_ids, column_ids, stats = attention_specs(rows, pairs)
    return pl.pallas_call(
        attend_kernel,
        grid=(pairs,),
        in_specs=[column(0), column(pairs), column(2 * pairs), row_ids, column_ids],
        out_specs=[column(0), stats],
        out_shape=[
            jax.ShapeDtypeStruct((rows, width), jnp.bfloat16),
            jax.ShapeDtypeStruct((pairs, 2, rows), jnp.float32),
        ],
        compiler_params=pltpu.CompilerParams(vmem_limit_bytes=48 * 1024 * 1024),
        cost_estimate=pl.CostEstimate(
            flops=8 * pairs * rows * rows * LANES,
            bytes_accessed=8 * rows * width,
            transcendentals=2 * pairs * rows * rows,
        ),
        name="attend",
    )(projected, projected, projected, segments[None, :], segments[:, None])


def attend_back_call(projected, grad, segments, stats_in):
    rows, width = grad.shape
    pairs = width // LANES
    column, row_ids, column_ids, stats = attention_specs(rows, pairs)
    shape = jax.ShapeDtypeStruct((rows, width), jnp.bfloat16)
    return pl.pallas_call(
        attend_back_kernel,
        grid=(pairs,),
        in_specs=[
            column(0),
            column(pairs),
            column(2 * pairs),
            column(0),
            row_ids,
            column_ids,
            stats,
        ],
        out_specs=[column(0)] * 3,
        out_shape=[shape] * 3,
        compiler_params=pltpu.CompilerParams(vmem_limit_bytes=48 * 1024 * 1024),
        cost_estimate=pl.CostEstimate(
            flops=20 * pairs * rows * rows * LANES,
            bytes_accessed=14 * rows * width,
            transcendentals=2 * pairs * rows * rows,
        ),
        name="attend_back",
    )(projected, projected, projected, grad, segments[None, :], segments[:, None], stats_in)


def dot_nn(a, b):
    return jnp.dot(a, b, preferred_element_type=jnp.float32)


def dot_nt(a, b):
    return lax.dot_general(a, b, (((1,), (1,)), ((), ())), preferred_element_type=jnp.float32)


def dot_tn(a, b):
    return lax.dot_general(a, b, (((0,), (0,)), ((), ())), preferred_element_type=jnp.float32)


def gelu_pair(values):
    cdf = 0.5 * (1.0 + lax.erf(values * (0.5**0.5)))
    density = jnp.exp(-0.5 * values * values) * (0.5 / jnp.pi) ** 0.5
    return values * cdf, cdf + values * density


def sequence_parallel(
    layer_input,
    segment_ids,
    qkv_weight,
    qv_bias,
    out_weight,
    up_weight,
    up_bias,
    down_weight,
    norm_gains,
    row_biases,
    cotangent,
):
    low = jnp.bfloat16
    parts = lax.axis_size("tensor")
    dp_count = lax.axis_size("dp")
    mine = lax.axis_index("tensor")
    swap = [(i, (i + 1) % parts) for i in range(parts)]
    half = layer_input.shape[1]
    width = layer_input.shape[2]
    heads_local = qv_bias.shape[1]
    width_local = heads_local * HEAD_DIM

    def own_sequence(rows):
        kept = lax.dynamic_index_in_dim(rows, mine, 0, keepdims=False)
        sent = lax.dynamic_index_in_dim(rows, 1 - mine, 0, keepdims=False)
        return jnp.concatenate([kept, lax.ppermute(sent, "tensor", swap)], axis=0)

    def own_rows(rows):
        received = lax.ppermute(rows[half:], "tensor", swap)
        first = jnp.where(mine == 0, rows[:half], received)
        second = jnp.where(mine == 0, received, rows[:half])
        return jnp.stack([first, second])

    everything = ("tensor", "dp")
    rows_in = own_sequence(layer_input)
    segments = lax.dynamic_index_in_dim(segment_ids, mine, 0, keepdims=False)
    segments = jnp.where(mine == 0, segments, jnp.roll(segments, -half))

    small = jnp.concatenate(
        [
            qv_bias.astype(jnp.float32).reshape(-1),
            up_bias.astype(jnp.float32).reshape(-1),
            norm_gains.reshape(-1),
            row_biases.reshape(-1),
        ]
    )
    small_all = lax.all_gather(small, everything, axis=0, tiled=False)
    small_all = small_all.reshape(parts, dp_count, small.shape[0])
    sizes = [qv_bias.size, up_bias.size, norm_gains.size, row_biases.size]
    starts = [0, sizes[0], sum(sizes[:2]), sum(sizes[:3])]
    qv_all, upb_all, gains_all, biases_all = (
        small_all[:, :, a : a + n] for a, n in zip(starts, sizes)
    )
    qv_all = qv_all.reshape((parts, dp_count) + qv_bias.shape).transpose(2, 0, 3, 1, 4)
    qv_all = qv_all.reshape(2, parts, width_local)
    upb_all = upb_all.reshape(parts, -1)

    def whole_rows(values, shard):
        values = values.reshape((parts, dp_count) + shard.shape).transpose(2, 1, 0, 3)
        return values.reshape(shard.shape[0], width)

    gains_all = whole_rows(gains_all, norm_gains)
    biases_all = whole_rows(biases_all, row_biases)

    def gather(piece):
        return lax.all_gather(piece, everything, axis=0, tiled=True).reshape(
            parts, width, piece.shape[1]
        )

    def scatter(blocks):
        flat = blocks.reshape(parts * width, blocks.shape[2])
        return lax.psum_scatter(flat, everything, scatter_dimension=0, tiled=True)

    packed = jnp.concatenate(
        [
            qkv_weight[0],
            qkv_weight[1],
            qkv_weight[2],
            out_weight.T,
            up_weight,
            down_weight.T,
        ],
        axis=1,
    )
    gathered = gather(packed)
    wide = 3 * width_local
    edges = [wide, wide + width_local, wide + width_local + up_weight.shape[1]]
    qkv_full = gathered[:, :, : edges[0]]
    out_full = gathered[:, :, edges[0] : edges[1]]
    up_full = gathered[:, :, edges[1] : edges[2]]
    down_full = gathered[:, :, edges[2] :]
    span = range(parts)

    rows_wide = rows_in.astype(jnp.float32)
    none = jnp.zeros((width_local,), jnp.float32)
    projected, contexts, stats = [], [], []
    for t in span:
        bias = jnp.concatenate([qv_all[0, t], none, qv_all[1, t]])
        projected.append((dot_nn(rows_in, qkv_full[t]) + bias).astype(low))
        context, stat = attend_call(projected[t], segments)
        contexts.append(context)
        stats.append(stat)
    attention = sum(dot_nt(contexts[t], out_full[t]) for t in span)
    residual_one = rows_wide + attention + biases_all[0]
    hidden, normed_one, inverse_one = normalize(residual_one, gains_all[0], biases_all[1])
    hidden_low = hidden.astype(low)
    activated, slopes = [], []
    for t in span:
        value, slope = gelu_pair(dot_nn(hidden_low, up_full[t]) + upb_all[t])
        activated.append(value.astype(low))
        slopes.append(slope)
    branch = sum(dot_nt(activated[t], down_full[t]) for t in span)
    residual_two = hidden + branch + biases_all[2]
    result, normed_two, inverse_two = normalize(residual_two, gains_all[1], biases_all[3])
    outputs = own_rows(result.astype(low))

    grad_output = own_sequence(cotangent).astype(jnp.float32)
    gain_two_grad = jnp.sum(grad_output * normed_two, axis=0)
    shift_two_grad = jnp.sum(grad_output, axis=0)
    grad_two = norm_back(grad_output, normed_two, inverse_two, gains_all[1])
    down_bias_grad = jnp.sum(grad_two, axis=0)
    branch_grad = grad_two.astype(low)
    down_grad = jnp.stack([dot_tn(branch_grad, activated[t]).astype(low) for t in span])
    down_sum = scatter(down_grad)
    grad_upper = [(dot_nn(branch_grad, down_full[t]) * slopes[t]).astype(low) for t in span]
    upb_grad = jnp.stack([jnp.sum(grad_upper[t].astype(jnp.float32), axis=0) for t in span])
    up_grad = jnp.stack([dot_tn(hidden_low, grad_upper[t]).astype(low) for t in span])
    up_sum = scatter(up_grad)
    grad_hidden = grad_two + sum(dot_nt(grad_upper[t], up_full[t]) for t in span)
    gain_one_grad = jnp.sum(grad_hidden * normed_one, axis=0)
    shift_one_grad = jnp.sum(grad_hidden, axis=0)
    grad_one = norm_back(grad_hidden, normed_one, inverse_one, gains_all[0])
    out_bias_grad = jnp.sum(grad_one, axis=0)
    attention_grad = grad_one.astype(low)
    last, qv_grads, input_grad = [], [], grad_one
    for t in span:
        out_grad = dot_tn(attention_grad, contexts[t]).astype(low)
        grad_context = dot_nn(attention_grad, out_full[t]).astype(low)
        triple = attend_back_call(projected[t], grad_context, segments, stats[t])
        grad_qkv = jnp.concatenate(triple, axis=1)
        qv_grads.append(
            jnp.stack([jnp.sum(triple[j].astype(jnp.float32), axis=0) for j in (0, 2)])
        )
        qkv_grad = dot_tn(rows_in, grad_qkv).astype(low)
        last.append(jnp.concatenate([qkv_grad, out_grad], axis=1))
        input_grad = input_grad + dot_nt(grad_qkv, qkv_full[t])
    last_sum = scatter(jnp.stack(last))
    input_grads = own_rows(input_grad.astype(low))

    qv_grads = jnp.stack(qv_grads).reshape(parts, 2, heads_local, dp_count, -1)
    qv_grads = qv_grads.transpose(0, 3, 1, 2, 4).reshape(parts, dp_count, -1)
    upb_grad = upb_grad.reshape(parts, dp_count, -1)

    def split_rows(rows):
        rows = rows.reshape(rows.shape[0], dp_count, parts, -1).transpose(2, 1, 0, 3)
        return rows.reshape(parts, dp_count, -1)

    gains_grad = jnp.stack([gain_one_grad, gain_two_grad])
    biases_grad = jnp.stack([out_bias_grad, shift_one_grad, down_bias_grad, shift_two_grad])
    small_grad = jnp.concatenate(
        [qv_grads, upb_grad, split_rows(gains_grad), split_rows(biases_grad)], axis=2
    )
    small_grad = small_grad.reshape(parts * dp_count, -1)
    exchanged = lax.all_to_all(small_grad, everything, 0, 0, tiled=True)
    small_sum = jnp.sum(exchanged, axis=0)
    qv_sum, upb_sum, gains_sum, biases_sum = (
        small_sum[a : a + n] for a, n in zip(starts, sizes)
    )
    wide_sums = (last_sum.astype(jnp.float32), up_sum, down_sum)
    qkv_sum = wide_sums[0][:, :wide].reshape(-1, 3, width_local).transpose(1, 0, 2)
    return (
        outputs,
        input_grads,
        qkv_sum,
        qv_sum.reshape(qv_bias.shape),
        wide_sums[0][:, wide:].T,
        up_sum.astype(jnp.float32),
        upb_sum.reshape(up_bias.shape),
        down_sum.astype(jnp.float32).T,
        gains_sum.reshape(norm_gains.shape),
        biases_sum.reshape(row_biases.shape),
    )


def solution(mesh):
    whole = ("dp", "tensor")
    rows, vectors = P(None, whole, None), P(None, whole)
    weights = (
        P(None, "dp", "tensor"),
        P(None, "tensor", "dp"),
        P("tensor", "dp"),
        P("dp", "tensor"),
        P("tensor", "dp"),
        P("tensor", "dp"),
        vectors,
        vectors,
    )

    def program(*arrays):
        micro = arrays[0].shape[0]
        fits = micro == 2 and mesh.shape["tensor"] == 2
        return jax.shard_map(
            sequence_parallel if fits else tensor_split,
            mesh=mesh,
            in_specs=(rows, P(None, "dp")) + weights + (rows,),
            out_specs=(rows, rows) + weights,
            check_vma=False,
        )(*arrays)

    return program
```

```python
import functools

import jax
import jax.numpy as jnp
from jax import lax
from jax.experimental import pallas as pl
from jax.experimental.pallas import tpu as pltpu
from jax.sharding import Mesh
from jax.sharding import PartitionSpec as P

HEAD_DIM = 64


def gelu_exact(values):
    return jax.nn.gelu(values, approximate=False)


def normalize(rows, gain, shift):
    centered = rows - jnp.mean(rows, axis=-1, keepdims=True)
    variance = jnp.mean(centered * centered, axis=-1, keepdims=True)
    inverse = lax.rsqrt(variance + 1e-05)
    normed = centered * inverse
    return (normed * gain + shift, normed, inverse)


def norm_back(grad, normed, inverse, gain):
    scaled = grad * gain
    return inverse * (
        scaled
        - jnp.mean(scaled, axis=-1, keepdims=True)
        - normed * jnp.mean(scaled * normed, axis=-1, keepdims=True)
    )


def attend(query, keys, values, keep_mask, scale):
    scores = jnp.einsum("qhd,khd->hqk", query, keys, preferred_element_type=jnp.float32) * scale
    masked = jnp.where(keep_mask[None], scores, -1e30)
    highest = jnp.max(masked, axis=-1, keepdims=True)
    shifted = jnp.exp(masked - highest)
    totals = jnp.sum(shifted, axis=-1, keepdims=True)
    probs = (shifted / totals).astype(jnp.bfloat16)
    context = jnp.einsum("hqk,khd->qhd", probs, values, preferred_element_type=jnp.float32)
    return (context, highest + jnp.log(totals))


def attend_back(query, keys, values, keep_mask, logsumexp, grad_context, scale):
    scores = jnp.einsum("qhd,khd->hqk", query, keys, preferred_element_type=jnp.float32) * scale
    masked = jnp.where(keep_mask[None], scores, -1e30)
    probs = jnp.exp(masked - logsumexp)
    probs_low = probs.astype(jnp.bfloat16)
    grad_values = jnp.einsum(
        "hqk,qhd->khd", probs_low, grad_context, preferred_element_type=jnp.float32
    )
    grad_probs = jnp.einsum(
        "qhd,khd->hqk", grad_context, values, preferred_element_type=jnp.float32
    )
    grad_scores = probs * (grad_probs - jnp.sum(probs * grad_probs, axis=-1, keepdims=True))
    grad_low = grad_scores.astype(jnp.bfloat16)
    grad_query = (
        jnp.einsum("hqk,khd->qhd", grad_low, keys, preferred_element_type=jnp.float32) * scale
    )
    grad_keys = (
        jnp.einsum("hqk,qhd->khd", grad_low, query, preferred_element_type=jnp.float32) * scale
    )
    return (grad_query, grad_keys, grad_values)


def tensor_split(
    layer_input,
    segment_ids,
    qkv_weight,
    qv_bias,
    out_weight,
    up_weight,
    up_bias,
    down_weight,
    norm_gains,
    row_biases,
    cotangent,
):
    gains_all, biases_all = (
        lax.all_gather(norm_gains, ("dp", "tensor"), axis=1, tiled=True),
        lax.all_gather(row_biases, ("dp", "tensor"), axis=1, tiled=True),
    )
    shards = (qkv_weight, qv_bias, out_weight, up_weight, up_bias, down_weight)
    dp_count = lax.axis_size("dp")
    seq_len = segment_ids.shape[1]
    heads_local = qv_bias.shape[1]
    width_local = heads_local * HEAD_DIM
    scale = HEAD_DIM ** (-0.5)

    def micro_step(carry, inputs):
        rows_in, segments, grad_rows = inputs
        qkv_full, qv_full, out_full, up_full, upb_full, down_full = (
            lax.all_gather(shards[0], "dp", axis=1, tiled=True),
            lax.all_gather(shards[1], "dp", axis=2, tiled=True),
            lax.all_gather(shards[2], "dp", axis=1, tiled=True),
            lax.all_gather(shards[3], "dp", axis=0, tiled=True),
            lax.all_gather(shards[4], "dp", axis=1, tiled=True),
            lax.all_gather(shards[5], "dp", axis=1, tiled=True),
        )
        gathered = lax.all_gather(rows_in, "tensor", axis=0, tiled=True)
        projected = jnp.einsum(
            "rd,kdc->krc", gathered, qkv_full, preferred_element_type=jnp.float32
        )
        bias_flat = qv_full.reshape(2, width_local).astype(jnp.float32)
        split = (seq_len, heads_local, HEAD_DIM)
        query = (projected[0] + bias_flat[0]).astype(jnp.bfloat16).reshape(split)
        keys = projected[1].astype(jnp.bfloat16).reshape(split)
        values = (projected[2] + bias_flat[1]).astype(jnp.bfloat16).reshape(split)
        keep_mask = segments[:, None] == segments[None, :]
        attended, logsumexp = attend(query, keys, values, keep_mask, scale)
        context = attended.reshape(seq_len, width_local).astype(jnp.bfloat16)
        attention = lax.psum_scatter(
            jnp.dot(context, out_full, preferred_element_type=jnp.float32).astype(jnp.bfloat16),
            "tensor",
            scatter_dimension=0,
            tiled=True,
        ).astype(jnp.float32)
        residual_one = rows_in.astype(jnp.float32) + attention + biases_all[0]
        hidden, normed_one, inverse_one = normalize(residual_one, gains_all[0], biases_all[1])
        hidden_rows = lax.all_gather(hidden.astype(jnp.bfloat16), "tensor", axis=0, tiled=True)
        upper = jnp.dot(
            hidden_rows, up_full, preferred_element_type=jnp.float32
        ) + upb_full.reshape(-1).astype(jnp.float32)
        activated = gelu_exact(upper).astype(jnp.bfloat16)
        branch = lax.psum_scatter(
            jnp.dot(activated, down_full, preferred_element_type=jnp.float32).astype(jnp.bfloat16),
            "tensor",
            scatter_dimension=0,
            tiled=True,
        ).astype(jnp.float32)
        residual_two = hidden + branch + biases_all[2]
        result, normed_two, inverse_two = normalize(residual_two, gains_all[1], biases_all[3])
        qkv_back, qv_back, out_back, up_back, upb_back, down_back = (
            lax.all_gather(shards[0], "dp", axis=1, tiled=True),
            lax.all_gather(shards[1], "dp", axis=2, tiled=True),
            lax.all_gather(shards[2], "dp", axis=1, tiled=True),
            lax.all_gather(shards[3], "dp", axis=0, tiled=True),
            lax.all_gather(shards[4], "dp", axis=1, tiled=True),
            lax.all_gather(shards[5], "dp", axis=1, tiled=True),
        )
        grad_output = grad_rows.astype(jnp.float32)
        gain_two_grad = jnp.sum(grad_output * normed_two, axis=0)
        shift_two_grad = jnp.sum(grad_output, axis=0)
        grad_two = norm_back(grad_output, normed_two, inverse_two, gains_all[1])
        down_bias_grad = jnp.sum(grad_two, axis=0)
        branch_rows = lax.all_gather(grad_two.astype(jnp.bfloat16), "tensor", axis=0, tiled=True)
        down_grad = jnp.einsum(
            "rf,rd->fd", activated, branch_rows, preferred_element_type=jnp.float32
        )
        grad_active = jnp.einsum(
            "rd,fd->rf", branch_rows, down_back, preferred_element_type=jnp.float32
        )
        gelu_pull = jax.vjp(gelu_exact, upper)[1]
        grad_upper = gelu_pull(grad_active)[0].astype(jnp.bfloat16)
        up_bias_grad = jnp.sum(grad_upper.astype(jnp.float32), axis=0).reshape(1, -1)
        up_grad = jnp.einsum(
            "rd,rf->df", hidden_rows, grad_upper, preferred_element_type=jnp.float32
        )
        grad_hidden = grad_two + lax.psum_scatter(
            jnp.einsum("rf,df->rd", grad_upper, up_back, preferred_element_type=jnp.float32).astype(
                jnp.bfloat16
            ),
            "tensor",
            scatter_dimension=0,
            tiled=True,
        ).astype(jnp.float32)
        gain_one_grad = jnp.sum(grad_hidden * normed_one, axis=0)
        shift_one_grad = jnp.sum(grad_hidden, axis=0)
        grad_one = norm_back(grad_hidden, normed_one, inverse_one, gains_all[0])
        out_bias_grad = jnp.sum(grad_one, axis=0)
        attention_rows = lax.all_gather(grad_one.astype(jnp.bfloat16), "tensor", axis=0, tiled=True)
        out_grad = jnp.einsum(
            "rc,rd->cd", context, attention_rows, preferred_element_type=jnp.float32
        )
        grad_context = (
            jnp.einsum("rd,cd->rc", attention_rows, out_back, preferred_element_type=jnp.float32)
            .astype(jnp.bfloat16)
            .reshape(split)
        )
        grad_query, grad_keys, grad_values = attend_back(
            query, keys, values, keep_mask, logsumexp, grad_context, scale
        )
        grad_qkv = (
            jnp.stack([grad_query, grad_keys, grad_values])
            .reshape(3, seq_len, width_local)
            .astype(jnp.bfloat16)
        )
        bias_sums = jnp.sum(jnp.stack([grad_qkv[0], grad_qkv[2]]).astype(jnp.float32), axis=1)
        qv_grad = bias_sums.reshape(2, heads_local, HEAD_DIM)
        qkv_grad = jnp.einsum("rd,krc->kdc", gathered, grad_qkv, preferred_element_type=jnp.float32)
        input_grad = (
            grad_one
            + lax.psum_scatter(
                jnp.einsum(
                    "krc,kdc->rd", grad_qkv, qkv_back, preferred_element_type=jnp.float32
                ).astype(jnp.bfloat16),
                "tensor",
                scatter_dimension=0,
                tiled=True,
            ).astype(jnp.float32)
        ).astype(jnp.bfloat16)
        gains_grad = jnp.stack([gain_one_grad, gain_two_grad])
        biases_grad = jnp.stack([out_bias_grad, shift_one_grad, down_bias_grad, shift_two_grad])
        updates = (
            qkv_grad,
            qv_grad,
            out_grad,
            up_grad,
            up_bias_grad,
            down_grad,
            gains_grad,
            biases_grad,
        )
        carry = tuple((total + update for total, update in zip(carry, updates)))
        return (carry, (result.astype(jnp.bfloat16), input_grad))

    initial = (
        jnp.zeros((3, qkv_weight.shape[1] * dp_count, qkv_weight.shape[2]), jnp.float32),
        jnp.zeros((2, qv_bias.shape[1], qv_bias.shape[2] * dp_count), jnp.float32),
        jnp.zeros((out_weight.shape[0], out_weight.shape[1] * dp_count), jnp.float32),
        jnp.zeros((up_weight.shape[0] * dp_count, up_weight.shape[1]), jnp.float32),
        jnp.zeros((1, up_bias.shape[1] * dp_count), jnp.float32),
        jnp.zeros((down_weight.shape[0], down_weight.shape[1] * dp_count), jnp.float32),
        jnp.zeros(gains_all.shape, jnp.float32),
        jnp.zeros(biases_all.shape, jnp.float32),
    )
    totals, (outputs, input_grads) = lax.scan(
        micro_step, initial, (layer_input, segment_ids, cotangent)
    )
    qkv_sum, qv_sum, out_sum, up_sum, upb_sum, down_sum = (
        lax.psum_scatter(
            totals[0].astype(jnp.bfloat16), "dp", scatter_dimension=1, tiled=True
        ).astype(jnp.float32),
        lax.psum_scatter(
            totals[1].astype(jnp.bfloat16), "dp", scatter_dimension=2, tiled=True
        ).astype(jnp.float32),
        lax.psum_scatter(
            totals[2].astype(jnp.bfloat16), "dp", scatter_dimension=1, tiled=True
        ).astype(jnp.float32),
        lax.psum_scatter(
            totals[3].astype(jnp.bfloat16), "dp", scatter_dimension=0, tiled=True
        ).astype(jnp.float32),
        lax.psum_scatter(
            totals[4].astype(jnp.bfloat16), "dp", scatter_dimension=1, tiled=True
        ).astype(jnp.float32),
        lax.psum_scatter(
            totals[5].astype(jnp.bfloat16), "dp", scatter_dimension=1, tiled=True
        ).astype(jnp.float32),
    )
    gains_sum, biases_sum = (
        lax.psum_scatter(totals[6], ("dp", "tensor"), scatter_dimension=1, tiled=True),
        lax.psum_scatter(totals[7], ("dp", "tensor"), scatter_dimension=1, tiled=True),
    )
    return (
        outputs,
        input_grads,
        qkv_sum,
        qv_sum,
        out_sum,
        up_sum,
        upb_sum,
        down_sum,
        gains_sum,
        biases_sum,
    )


NEGATIVE = -1e30
LANES = 2 * HEAD_DIM


def half_mask(shape, half):
    lane = lax.broadcasted_iota(jnp.int32, shape, 1)
    return (lane // HEAD_DIM) == half


def attend_kernel(q_ref, k_ref, v_ref, row_ref, col_ref, context_ref, stats_ref):
    query, keys, values = q_ref[...], k_ref[...], v_ref[...]
    keep = col_ref[...] == row_ref[...]
    total = jnp.zeros(context_ref.shape, jnp.float32)
    for half in range(2):
        own = half_mask(query.shape, half)
        masked_query = jnp.where(own, query, 0) * jnp.asarray(HEAD_DIM**-0.5, query.dtype)
        scores = lax.dot_general(
            keys, masked_query, (((1,), (1,)), ((), ())), preferred_element_type=jnp.float32
        )
        scores = jnp.where(keep, scores, NEGATIVE)
        highest = jnp.max(scores, axis=0, keepdims=True)
        shifted = jnp.exp(scores - highest)
        sums = jnp.sum(shifted, axis=0, keepdims=True)
        probs = (shifted * (1.0 / sums)).astype(jnp.bfloat16)
        own_values = jnp.where(own, values, 0)
        total += lax.dot_general(
            probs, own_values, (((0,), (0,)), ((), ())), preferred_element_type=jnp.float32
        )
        stats_ref[0, half : half + 1, :] = highest + jnp.log(sums)
    context_ref[...] = total.astype(context_ref.dtype)


def attend_back_kernel(
    q_ref, k_ref, v_ref, grad_ref, row_ref, col_ref, stats_ref, d_ref
):
    query, keys, values, grad = q_ref[...], k_ref[...], v_ref[...], grad_ref[...]
    scale = jnp.asarray(HEAD_DIM**-0.5, query.dtype)
    keep = col_ref[...] == row_ref[...]
    zero = jnp.zeros(query.shape, jnp.float32)
    grad_query, grad_keys, grad_values = zero, zero, zero
    for half in range(2):
        own = half_mask(query.shape, half)
        own_query = jnp.where(own, query, 0) * scale
        own_keys = jnp.where(own, keys, 0) * scale
        own_grad = jnp.where(own, grad, 0)
        contract_last = (((1,), (1,)), ((), ()))
        scores = lax.dot_general(
            keys, own_query, contract_last, preferred_element_type=jnp.float32
        )
        scores = jnp.where(keep, scores, NEGATIVE)
        probs = jnp.exp(scores - stats_ref[0, half : half + 1, :])
        grad_values += jnp.dot(
            probs.astype(jnp.bfloat16), own_grad, preferred_element_type=jnp.float32
        )
        grad_probs = lax.dot_general(
            values, own_grad, contract_last, preferred_element_type=jnp.float32
        )
        weighted = probs * grad_probs
        grad_scores = (weighted - probs * jnp.sum(weighted, axis=0, keepdims=True)).astype(
            jnp.bfloat16
        )
        grad_keys += jnp.dot(grad_scores, own_query, preferred_element_type=jnp.float32)
        grad_query += lax.dot_general(
            grad_scores, own_keys, (((0,), (0,)), ((), ())), preferred_element_type=jnp.float32
        )
    pair, width = pl.program_id(0), d_ref.shape[1] // 3
    for place, value in enumerate((grad_query, grad_keys, grad_values)):
        start = pl.multiple_of(place * width + pair * LANES, LANES)
        d_ref[:, pl.ds(start, LANES)] = value.astype(d_ref.dtype)


def attention_specs(rows, pairs):
    def column(offset):
        return pl.BlockSpec((rows, LANES), lambda i, offset=offset: (0, offset + i))

    row_ids = pl.BlockSpec((1, rows), lambda i: (0, 0))
    column_ids = pl.BlockSpec((rows, 1), lambda i: (0, 0))
    stats = pl.BlockSpec((1, 2, rows), lambda i: (i, 0, 0))
    return column, row_ids, column_ids, stats


def attend_call(projected, segments):
    rows, width = projected.shape[0], projected.shape[1] // 3
    pairs = width // LANES
    column, row_ids, column_ids, stats = attention_specs(rows, pairs)
    return pl.pallas_call(
        attend_kernel,
        grid=(pairs,),
        in_specs=[column(0), column(pairs), column(2 * pairs), row_ids, column_ids],
        out_specs=[column(0), stats],
        out_shape=[
            jax.ShapeDtypeStruct((rows, width), jnp.bfloat16),
            jax.ShapeDtypeStruct((pairs, 2, rows), jnp.float32),
        ],
        compiler_params=pltpu.CompilerParams(vmem_limit_bytes=48 * 1024 * 1024),
        cost_estimate=pl.CostEstimate(
            flops=8 * pairs * rows * rows * LANES,
            bytes_accessed=8 * rows * width,
            transcendentals=2 * pairs * rows * rows,
        ),
        name="attend",
    )(projected, projected, projected, segments[None, :], segments[:, None])


def attend_back_call(projected, grad, segments, stats_in):
    rows, width = grad.shape
    pairs = width // LANES
    column, row_ids, column_ids, stats = attention_specs(rows, pairs)
    whole = pl.BlockSpec((rows, 3 * width), lambda i: (0, 0))
    return pl.pallas_call(
        attend_back_kernel,
        grid=(pairs,),
        in_specs=[
            column(0),
            column(pairs),
            column(2 * pairs),
            column(0),
            row_ids,
            column_ids,
            stats,
        ],
        out_specs=whole,
        out_shape=jax.ShapeDtypeStruct((rows, 3 * width), jnp.bfloat16),
        compiler_params=pltpu.CompilerParams(vmem_limit_bytes=48 * 1024 * 1024),
        cost_estimate=pl.CostEstimate(
            flops=20 * pairs * rows * rows * LANES,
            bytes_accessed=14 * rows * width,
            transcendentals=2 * pairs * rows * rows,
        ),
        name="attend_back",
    )(projected, projected, projected, grad, segments[None, :], segments[:, None], stats_in)


def dot_nn(a, b):
    return jnp.dot(a, b, preferred_element_type=jnp.float32)


def dot_nt(a, b):
    return lax.dot_general(a, b, (((1,), (1,)), ((), ())), preferred_element_type=jnp.float32)


def dot_tn(a, b):
    return lax.dot_general(a, b, (((0,), (0,)), ((), ())), preferred_element_type=jnp.float32)


def gelu_pair(values):
    cdf = 0.5 * (1.0 + lax.erf(values * (0.5**0.5)))
    density = jnp.exp(-0.5 * values * values) * (0.5 / jnp.pi) ** 0.5
    return values * cdf, cdf + values * density


VMEM_BYTES = 56 * 1024 * 1024


def gradient_kernel(row_ref, part_ref, *refs, blocks, pairs, added):
    lefts, rights = refs[:pairs], refs[pairs : 3 * pairs]
    received = refs[3 * pairs : 3 * pairs + added]
    outs = refs[3 * pairs + added :]
    step = pl.program_id(0)
    size = outs[0].shape[0]
    start = pl.multiple_of(row_ref[step] * size, size)

    def products(part):
        pieces = [
            dot_tn(lefts[i][:, pl.ds(start, size)], rights[2 * i + part][...])
            for i in range(pairs)
        ]
        total = pieces[0] if pairs == 1 else jnp.concatenate(pieces, axis=1)
        if added:
            total = total + received[0][...].astype(jnp.float32)
        total = total.astype(jnp.bfloat16)
        if len(outs) == 1:
            outs[0][...] = total
        else:
            for out, (low, high) in zip(outs, blocks):
                @pl.when((step >= low) & (step < high))
                def _(out=out):
                    out[...] = total

    for part in range(2):
        pl.when(part_ref[step] == part)(functools.partial(products, part))


def gradient_blocks(rows, parts, lefts, rights, received=None):
    count = rows.shape[0]
    size = lefts[0].shape[1] // count
    width = sum(pair[0].shape[1] for pair in rights)
    flat = [item for pair in rights for item in pair]
    spans = ((0, 2), (2, 3), (3, 4))
    whole = [
        pl.BlockSpec(item.shape, lambda i, *_: (0, 0), pipeline_mode=pl.Buffered(1))
        for item in list(lefts) + flat
    ]
    block = pl.BlockSpec((size, width), lambda i, *_: (i, 0))
    in_specs, operands = whole, list(lefts) + flat
    if received is None:
        out_shape = [jax.ShapeDtypeStruct((count * size, width), jnp.bfloat16)]
        out_specs = [block]
    else:
        in_specs, operands = whole + [block], operands + [received]
        out_shape = [
            jax.ShapeDtypeStruct(((high - low) * size, width), jnp.bfloat16)
            for low, high in spans
        ]
        out_specs = [
            pl.BlockSpec(
                (size, width),
                lambda i, *_, low=low, high=high: (jnp.clip(i, low, high - 1) - low, 0),
            )
            for low, high in spans
        ]
    return pl.pallas_call(
        functools.partial(
            gradient_kernel,
            blocks=spans,
            pairs=len(lefts),
            added=0 if received is None else 1,
        ),
        grid_spec=pltpu.PrefetchScalarGridSpec(
            num_scalar_prefetch=2,
            grid=(count,),
            in_specs=in_specs,
            out_specs=out_specs,
        ),
        out_shape=out_shape,
        compiler_params=pltpu.CompilerParams(vmem_limit_bytes=VMEM_BYTES),
        cost_estimate=pl.CostEstimate(
            flops=2 * count * size * lefts[0].shape[0] * width,
            bytes_accessed=6 * count * size * width,
            transcendentals=0,
        ),
        name="gradient_blocks",
    )(rows, parts, *operands)


def permutes():
    def index(x, c, y):
        return (x * 2 + c) * 2 + y

    cells = [(x, y) for x in range(2) for y in range(2)]
    along = [(index(x, 0, y), index(1 - x, 0, y)) for x, y in cells]
    along += [(index(x, 1, y), index(x, 1, 1 - y)) for x, y in cells]
    cross = [(index(x, 0, y), index(1 - x, 1, y)) for x, y in cells]
    cross += [(index(x, 1, y), index(x, 0, 1 - y)) for x, y in cells]
    return along, cross


PLANE = ("x", "c", "y")
EVERY = ("y", "x", "c", "z")
SWAP = [(0, 1), (1, 0)]


def block_tables(x, c, y):
    def kept(core):
        first = jnp.stack([2 - 2 * x, 3 - 2 * x, 2 - 2 * x, 2 * x])
        second = jnp.stack([2 * x, 2 * x + 1, 3 - 2 * x, 2 * x + 1])
        parts_first = jnp.stack([y, y, 1 - y, y])
        parts_second = jnp.stack([1 - y, 1 - y, 1 - y, y])
        return jnp.where(core == 0, first, second), jnp.where(
            core == 0, parts_first, parts_second
        )

    return kept(c), kept(1 - c)


def reduce_gradient(lefts, rights, tables, core):
    own, other = tables
    sent = gradient_blocks(*other, lefts, rights)[0]
    received = lax.ppermute(sent, "c", SWAP)
    main, diagonal, home = gradient_blocks(*own, lefts, rights, received)
    along, cross = permutes()
    arrived = lax.ppermute(diagonal, PLANE, cross)
    size, width = diagonal.shape
    halves = main.reshape(2, size, width)
    aimed = lax.broadcasted_iota(jnp.int32, (2, 1, 1), 0) == 1 - core
    halves = jnp.where(
        aimed, (halves.astype(jnp.float32) + arrived.astype(jnp.float32)).astype(main.dtype), halves
    )
    landed = lax.ppermute(halves, PLANE, along)
    passed = lax.ppermute(lax.dynamic_index_in_dim(landed, 1 - core, 0, False), "c", SWAP)
    kept = lax.dynamic_index_in_dim(landed, core, 0, False)
    total = home.astype(jnp.float32) + kept.astype(jnp.float32) + passed.astype(jnp.float32)
    return lax.psum_scatter(total.astype(jnp.bfloat16), "z", scatter_dimension=0, tiled=True)


def sequence_parallel(
    layer_input,
    segment_ids,
    qkv_weight,
    qv_bias,
    out_weight,
    up_weight,
    up_bias,
    down_weight,
    norm_gains,
    row_biases,
    cotangent,
):
    low = jnp.bfloat16
    parts = lax.axis_size("y")
    grid = tuple(lax.axis_size(name) for name in ("x", "c", "z"))
    dp_count = grid[0] * grid[1] * grid[2]
    mine = lax.axis_index("y")
    core = lax.axis_index("c")
    tables = block_tables(lax.axis_index("x"), core, mine)
    half, width = layer_input.shape[1:]
    heads_local = qv_bias.shape[1]
    width_local = heads_local * HEAD_DIM
    span = range(parts)

    source = jnp.arange(width).reshape(grid[2], grid[0], grid[1], -1)
    source = source.transpose(1, 2, 0, 3).reshape(-1)
    chosen = lax.broadcasted_iota(jnp.int32, (width, width), 0) == source[None, :]
    order = chosen.astype(low)

    def own_sequence(rows):
        kept = lax.dynamic_index_in_dim(rows, mine, 0, keepdims=False)
        sent = lax.dynamic_index_in_dim(rows, 1 - mine, 0, keepdims=False)
        rows = jnp.concatenate([kept, lax.ppermute(sent, "y", SWAP)], axis=0)
        return dot_nn(rows, order).astype(low)

    def own_rows(rows):
        rows = dot_nt(rows.astype(low), order).astype(low)
        received = lax.ppermute(rows[half:], "y", SWAP)
        first = jnp.where(mine == 0, rows[:half], received)
        second = jnp.where(mine == 0, received, rows[:half])
        return jnp.stack([first, second])

    packed = jnp.concatenate(
        [
            qkv_weight[0],
            qkv_weight[1],
            qkv_weight[2],
            out_weight.T,
            up_weight,
            down_weight.T,
        ],
        axis=1,
    )
    gathered = lax.all_gather(packed, EVERY, axis=0, tiled=True).reshape(parts, width, -1)
    wide = 3 * width_local
    edges = [wide, wide + width_local, wide + width_local + up_weight.shape[1]]
    qkv_full = gathered[:, :, : edges[0]]
    out_full = gathered[:, :, edges[0] : edges[1]]
    up_full = gathered[:, :, edges[1] : edges[2]]
    down_full = gathered[:, :, edges[2] :]

    rows_in = own_sequence(layer_input)
    segments = lax.dynamic_index_in_dim(segment_ids, mine, 0, keepdims=False)
    segments = jnp.where(mine == 0, segments, jnp.roll(segments, -half))

    small = jnp.concatenate(
        [
            qv_bias.astype(jnp.float32).reshape(-1),
            up_bias.astype(jnp.float32).reshape(-1),
            norm_gains.reshape(-1),
            row_biases.reshape(-1),
        ]
    )
    copies = jnp.broadcast_to(small[None], (parts * dp_count, small.shape[0]))
    small_all = lax.all_to_all(copies, EVERY, 0, 0, tiled=True)
    small_all = small_all.reshape((parts,) + grid + (small.shape[0],))
    sizes = [qv_bias.size, up_bias.size, norm_gains.size, row_biases.size]
    starts = [0, sizes[0], sum(sizes[:2]), sum(sizes[:3])]

    def section(i, shard):
        values = small_all[..., starts[i] : starts[i] + sizes[i]]
        return values.reshape((parts,) + grid + shard.shape)

    qv_all = section(0, qv_bias).transpose(4, 0, 5, 3, 1, 2, 6).reshape(2, parts, width_local)
    upb_all = section(1, up_bias).transpose(0, 3, 1, 2, 4, 5).reshape(parts, -1)

    def whole_rows(i, shard):
        values = section(i, shard).transpose(4, 1, 2, 3, 0, 5)
        return values.reshape(shard.shape[0], width)

    gains_all, biases_all = whole_rows(2, norm_gains), whole_rows(3, row_biases)

    rows_wide = rows_in.astype(jnp.float32)
    none = jnp.zeros((width_local,), jnp.float32)
    projected, contexts, stats = [], [], []
    for t in span:
        bias = jnp.concatenate([qv_all[0, t], none, qv_all[1, t]])
        projected.append((dot_nn(rows_in, qkv_full[t]) + bias).astype(low))
        context, stat = attend_call(projected[t], segments)
        contexts.append(context)
        stats.append(stat)
    attention = sum(dot_nt(contexts[t], out_full[t]) for t in span)
    residual_one = rows_wide + attention + biases_all[0]
    hidden, normed_one, inverse_one = normalize(residual_one, gains_all[0], biases_all[1])
    hidden_low = hidden.astype(low)
    activated, slopes = [], []
    for t in span:
        value, slope = gelu_pair(dot_nn(hidden_low, up_full[t]) + upb_all[t])
        activated.append(value.astype(low))
        slopes.append(slope)
    branch = sum(dot_nt(activated[t], down_full[t]) for t in span)
    residual_two = hidden + branch + biases_all[2]
    result, normed_two, inverse_two = normalize(residual_two, gains_all[1], biases_all[3])

    grad_output = own_sequence(cotangent).astype(jnp.float32)
    gain_two_grad = jnp.sum(grad_output * normed_two, axis=0)
    shift_two_grad = jnp.sum(grad_output, axis=0)
    grad_two = norm_back(grad_output, normed_two, inverse_two, gains_all[1])
    down_bias_grad = jnp.sum(grad_two, axis=0)
    branch_grad = grad_two.astype(low)
    down_sum = reduce_gradient([branch_grad], [activated], tables, core)
    outputs = own_rows(result)
    grad_upper = [(dot_nn(branch_grad, down_full[t]) * slopes[t]).astype(low) for t in span]
    upb_grad = jnp.stack([jnp.sum(grad_upper[t].astype(jnp.float32), axis=0) for t in span])
    up_sum = reduce_gradient([hidden_low], [grad_upper], tables, core)
    grad_hidden = grad_two + sum(dot_nt(grad_upper[t], up_full[t]) for t in span)
    gain_one_grad = jnp.sum(grad_hidden * normed_one, axis=0)
    shift_one_grad = jnp.sum(grad_hidden, axis=0)
    grad_one = norm_back(grad_hidden, normed_one, inverse_one, gains_all[0])
    out_bias_grad = jnp.sum(grad_one, axis=0)
    attention_grad = grad_one.astype(low)
    grad_projected, qv_grads, input_grad = [], [], grad_one
    for t in span:
        grad_context = dot_nn(attention_grad, out_full[t]).astype(low)
        grad_projected.append(attend_back_call(projected[t], grad_context, segments, stats[t]))
        sums = jnp.sum(grad_projected[t].astype(jnp.float32), axis=0).reshape(3, width_local)
        qv_grads.append(jnp.stack([sums[0], sums[2]]))
    last_sum = reduce_gradient(
        [rows_in, attention_grad], [grad_projected, contexts], tables, core
    )
    for t in span:
        input_grad = input_grad + dot_nt(grad_projected[t], qkv_full[t])
    input_grads = own_rows(input_grad)

    dp_order = (grid[2], grid[0], grid[1])
    qv_grads = jnp.stack(qv_grads).reshape((parts, 2, heads_local) + dp_order + (-1,))
    qv_grads = qv_grads.transpose(0, 4, 5, 3, 1, 2, 6).reshape(parts * dp_count, -1)
    upb_grad = upb_grad.reshape((parts,) + dp_order + (-1,))
    upb_grad = upb_grad.transpose(0, 2, 3, 1, 4).reshape(parts * dp_count, -1)

    def split_rows(rows):
        count = len(rows)
        rows = jnp.stack(rows).reshape((count,) + grid + (parts, -1))
        return rows.transpose(4, 1, 2, 3, 0, 5).reshape(parts * dp_count, -1)

    small_grad = jnp.concatenate(
        [
            qv_grads,
            upb_grad,
            split_rows([gain_one_grad, gain_two_grad]),
            split_rows([out_bias_grad, shift_one_grad, down_bias_grad, shift_two_grad]),
        ],
        axis=1,
    )
    exchanged = lax.all_to_all(small_grad, EVERY, 0, 0, tiled=True)
    small_sum = jnp.sum(exchanged, axis=0)
    qv_sum, upb_sum, gains_sum, biases_sum = (
        small_sum[a : a + n] for a, n in zip(starts, sizes)
    )
    last_sum = last_sum.astype(jnp.float32)
    qkv_sum = last_sum[:, :wide].reshape(-1, 3, width_local).transpose(1, 0, 2)
    return (
        outputs,
        input_grads,
        qkv_sum,
        qv_sum.reshape(qv_bias.shape),
        last_sum[:, wide:].T,
        up_sum.astype(jnp.float32),
        upb_sum.reshape(up_bias.shape),
        down_sum.astype(jnp.float32).T,
        gains_sum.reshape(norm_gains.shape),
        biases_sum.reshape(row_biases.shape),
    )


def solution(mesh):
    groups = mesh.shape["dp"]
    parts = mesh.shape["tensor"]

    def program(*arrays):
        micro, width = arrays[0].shape[0], arrays[0].shape[2]
        fits = micro == 2 and parts == 2 and groups % 4 == 0 and width % (groups * 16) == 0
        if fits:
            dp, place = ("z", "x", "c"), "y"
            shape = (groups // 4, 2, 2, 2)
            used = Mesh(mesh.devices.reshape(shape), dp + (place,))
        else:
            dp, place, used = ("dp",), "tensor", mesh
        whole = dp + (place,)
        rows, vectors = P(None, whole, None), P(None, whole)
        weights = (
            P(None, dp, place),
            P(None, place, dp),
            P(place, dp),
            P(dp, place),
            P(place, dp),
            P(place, dp),
            vectors,
            vectors,
        )
        return jax.shard_map(
            sequence_parallel if fits else tensor_split,
            mesh=used,
            in_specs=(rows, P(None, dp)) + weights + (rows,),
            out_specs=(rows, rows) + weights,
            check_vma=False,
        )(*arrays)

    return program
```

```python
import functools

import jax
import jax.numpy as jnp
from jax import lax
from jax.experimental import pallas as pl
from jax.experimental.pallas import tpu as pltpu
from jax.sharding import Mesh
from jax.sharding import PartitionSpec as P

HEAD_DIM = 64


def gelu_exact(values):
    return jax.nn.gelu(values, approximate=False)


def normalize(rows, gain, shift):
    centered = rows - jnp.mean(rows, axis=-1, keepdims=True)
    variance = jnp.mean(centered * centered, axis=-1, keepdims=True)
    inverse = lax.rsqrt(variance + 1e-05)
    normed = centered * inverse
    return (normed * gain + shift, normed, inverse)


def norm_back(grad, normed, inverse, gain):
    scaled = grad * gain
    return inverse * (
        scaled
        - jnp.mean(scaled, axis=-1, keepdims=True)
        - normed * jnp.mean(scaled * normed, axis=-1, keepdims=True)
    )


def attend(query, keys, values, keep_mask, scale):
    scores = jnp.einsum("qhd,khd->hqk", query, keys, preferred_element_type=jnp.float32) * scale
    masked = jnp.where(keep_mask[None], scores, -1e30)
    highest = jnp.max(masked, axis=-1, keepdims=True)
    shifted = jnp.exp(masked - highest)
    totals = jnp.sum(shifted, axis=-1, keepdims=True)
    probs = (shifted / totals).astype(jnp.bfloat16)
    context = jnp.einsum("hqk,khd->qhd", probs, values, preferred_element_type=jnp.float32)
    return (context, highest + jnp.log(totals))


def attend_back(query, keys, values, keep_mask, logsumexp, grad_context, scale):
    scores = jnp.einsum("qhd,khd->hqk", query, keys, preferred_element_type=jnp.float32) * scale
    masked = jnp.where(keep_mask[None], scores, -1e30)
    probs = jnp.exp(masked - logsumexp)
    probs_low = probs.astype(jnp.bfloat16)
    grad_values = jnp.einsum(
        "hqk,qhd->khd", probs_low, grad_context, preferred_element_type=jnp.float32
    )
    grad_probs = jnp.einsum(
        "qhd,khd->hqk", grad_context, values, preferred_element_type=jnp.float32
    )
    grad_scores = probs * (grad_probs - jnp.sum(probs * grad_probs, axis=-1, keepdims=True))
    grad_low = grad_scores.astype(jnp.bfloat16)
    grad_query = (
        jnp.einsum("hqk,khd->qhd", grad_low, keys, preferred_element_type=jnp.float32) * scale
    )
    grad_keys = (
        jnp.einsum("hqk,qhd->khd", grad_low, query, preferred_element_type=jnp.float32) * scale
    )
    return (grad_query, grad_keys, grad_values)


def tensor_split(
    layer_input,
    segment_ids,
    qkv_weight,
    qv_bias,
    out_weight,
    up_weight,
    up_bias,
    down_weight,
    norm_gains,
    row_biases,
    cotangent,
):
    gains_all, biases_all = (
        lax.all_gather(norm_gains, ("dp", "tensor"), axis=1, tiled=True),
        lax.all_gather(row_biases, ("dp", "tensor"), axis=1, tiled=True),
    )
    shards = (qkv_weight, qv_bias, out_weight, up_weight, up_bias, down_weight)
    dp_count = lax.axis_size("dp")
    seq_len = segment_ids.shape[1]
    heads_local = qv_bias.shape[1]
    width_local = heads_local * HEAD_DIM
    scale = HEAD_DIM ** (-0.5)

    def micro_step(carry, inputs):
        rows_in, segments, grad_rows = inputs
        qkv_full, qv_full, out_full, up_full, upb_full, down_full = (
            lax.all_gather(shards[0], "dp", axis=1, tiled=True),
            lax.all_gather(shards[1], "dp", axis=2, tiled=True),
            lax.all_gather(shards[2], "dp", axis=1, tiled=True),
            lax.all_gather(shards[3], "dp", axis=0, tiled=True),
            lax.all_gather(shards[4], "dp", axis=1, tiled=True),
            lax.all_gather(shards[5], "dp", axis=1, tiled=True),
        )
        gathered = lax.all_gather(rows_in, "tensor", axis=0, tiled=True)
        projected = jnp.einsum(
            "rd,kdc->krc", gathered, qkv_full, preferred_element_type=jnp.float32
        )
        bias_flat = qv_full.reshape(2, width_local).astype(jnp.float32)
        split = (seq_len, heads_local, HEAD_DIM)
        query = (projected[0] + bias_flat[0]).astype(jnp.bfloat16).reshape(split)
        keys = projected[1].astype(jnp.bfloat16).reshape(split)
        values = (projected[2] + bias_flat[1]).astype(jnp.bfloat16).reshape(split)
        keep_mask = segments[:, None] == segments[None, :]
        attended, logsumexp = attend(query, keys, values, keep_mask, scale)
        context = attended.reshape(seq_len, width_local).astype(jnp.bfloat16)
        attention = lax.psum_scatter(
            jnp.dot(context, out_full, preferred_element_type=jnp.float32).astype(jnp.bfloat16),
            "tensor",
            scatter_dimension=0,
            tiled=True,
        ).astype(jnp.float32)
        residual_one = rows_in.astype(jnp.float32) + attention + biases_all[0]
        hidden, normed_one, inverse_one = normalize(residual_one, gains_all[0], biases_all[1])
        hidden_rows = lax.all_gather(hidden.astype(jnp.bfloat16), "tensor", axis=0, tiled=True)
        upper = jnp.dot(
            hidden_rows, up_full, preferred_element_type=jnp.float32
        ) + upb_full.reshape(-1).astype(jnp.float32)
        activated = gelu_exact(upper).astype(jnp.bfloat16)
        branch = lax.psum_scatter(
            jnp.dot(activated, down_full, preferred_element_type=jnp.float32).astype(jnp.bfloat16),
            "tensor",
            scatter_dimension=0,
            tiled=True,
        ).astype(jnp.float32)
        residual_two = hidden + branch + biases_all[2]
        result, normed_two, inverse_two = normalize(residual_two, gains_all[1], biases_all[3])
        qkv_back, qv_back, out_back, up_back, upb_back, down_back = (
            lax.all_gather(shards[0], "dp", axis=1, tiled=True),
            lax.all_gather(shards[1], "dp", axis=2, tiled=True),
            lax.all_gather(shards[2], "dp", axis=1, tiled=True),
            lax.all_gather(shards[3], "dp", axis=0, tiled=True),
            lax.all_gather(shards[4], "dp", axis=1, tiled=True),
            lax.all_gather(shards[5], "dp", axis=1, tiled=True),
        )
        grad_output = grad_rows.astype(jnp.float32)
        gain_two_grad = jnp.sum(grad_output * normed_two, axis=0)
        shift_two_grad = jnp.sum(grad_output, axis=0)
        grad_two = norm_back(grad_output, normed_two, inverse_two, gains_all[1])
        down_bias_grad = jnp.sum(grad_two, axis=0)
        branch_rows = lax.all_gather(grad_two.astype(jnp.bfloat16), "tensor", axis=0, tiled=True)
        down_grad = jnp.einsum(
            "rf,rd->fd", activated, branch_rows, preferred_element_type=jnp.float32
        )
        grad_active = jnp.einsum(
            "rd,fd->rf", branch_rows, down_back, preferred_element_type=jnp.float32
        )
        gelu_pull = jax.vjp(gelu_exact, upper)[1]
        grad_upper = gelu_pull(grad_active)[0].astype(jnp.bfloat16)
        up_bias_grad = jnp.sum(grad_upper.astype(jnp.float32), axis=0).reshape(1, -1)
        up_grad = jnp.einsum(
            "rd,rf->df", hidden_rows, grad_upper, preferred_element_type=jnp.float32
        )
        grad_hidden = grad_two + lax.psum_scatter(
            jnp.einsum("rf,df->rd", grad_upper, up_back, preferred_element_type=jnp.float32).astype(
                jnp.bfloat16
            ),
            "tensor",
            scatter_dimension=0,
            tiled=True,
        ).astype(jnp.float32)
        gain_one_grad = jnp.sum(grad_hidden * normed_one, axis=0)
        shift_one_grad = jnp.sum(grad_hidden, axis=0)
        grad_one = norm_back(grad_hidden, normed_one, inverse_one, gains_all[0])
        out_bias_grad = jnp.sum(grad_one, axis=0)
        attention_rows = lax.all_gather(grad_one.astype(jnp.bfloat16), "tensor", axis=0, tiled=True)
        out_grad = jnp.einsum(
            "rc,rd->cd", context, attention_rows, preferred_element_type=jnp.float32
        )
        grad_context = (
            jnp.einsum("rd,cd->rc", attention_rows, out_back, preferred_element_type=jnp.float32)
            .astype(jnp.bfloat16)
            .reshape(split)
        )
        grad_query, grad_keys, grad_values = attend_back(
            query, keys, values, keep_mask, logsumexp, grad_context, scale
        )
        grad_qkv = (
            jnp.stack([grad_query, grad_keys, grad_values])
            .reshape(3, seq_len, width_local)
            .astype(jnp.bfloat16)
        )
        bias_sums = jnp.sum(jnp.stack([grad_qkv[0], grad_qkv[2]]).astype(jnp.float32), axis=1)
        qv_grad = bias_sums.reshape(2, heads_local, HEAD_DIM)
        qkv_grad = jnp.einsum("rd,krc->kdc", gathered, grad_qkv, preferred_element_type=jnp.float32)
        input_grad = (
            grad_one
            + lax.psum_scatter(
                jnp.einsum(
                    "krc,kdc->rd", grad_qkv, qkv_back, preferred_element_type=jnp.float32
                ).astype(jnp.bfloat16),
                "tensor",
                scatter_dimension=0,
                tiled=True,
            ).astype(jnp.float32)
        ).astype(jnp.bfloat16)
        gains_grad = jnp.stack([gain_one_grad, gain_two_grad])
        biases_grad = jnp.stack([out_bias_grad, shift_one_grad, down_bias_grad, shift_two_grad])
        updates = (
            qkv_grad,
            qv_grad,
            out_grad,
            up_grad,
            up_bias_grad,
            down_grad,
            gains_grad,
            biases_grad,
        )
        carry = tuple((total + update for total, update in zip(carry, updates)))
        return (carry, (result.astype(jnp.bfloat16), input_grad))

    initial = (
        jnp.zeros((3, qkv_weight.shape[1] * dp_count, qkv_weight.shape[2]), jnp.float32),
        jnp.zeros((2, qv_bias.shape[1], qv_bias.shape[2] * dp_count), jnp.float32),
        jnp.zeros((out_weight.shape[0], out_weight.shape[1] * dp_count), jnp.float32),
        jnp.zeros((up_weight.shape[0] * dp_count, up_weight.shape[1]), jnp.float32),
        jnp.zeros((1, up_bias.shape[1] * dp_count), jnp.float32),
        jnp.zeros((down_weight.shape[0], down_weight.shape[1] * dp_count), jnp.float32),
        jnp.zeros(gains_all.shape, jnp.float32),
        jnp.zeros(biases_all.shape, jnp.float32),
    )
    totals, (outputs, input_grads) = lax.scan(
        micro_step, initial, (layer_input, segment_ids, cotangent)
    )
    qkv_sum, qv_sum, out_sum, up_sum, upb_sum, down_sum = (
        lax.psum_scatter(
            totals[0].astype(jnp.bfloat16), "dp", scatter_dimension=1, tiled=True
        ).astype(jnp.float32),
        lax.psum_scatter(
            totals[1].astype(jnp.bfloat16), "dp", scatter_dimension=2, tiled=True
        ).astype(jnp.float32),
        lax.psum_scatter(
            totals[2].astype(jnp.bfloat16), "dp", scatter_dimension=1, tiled=True
        ).astype(jnp.float32),
        lax.psum_scatter(
            totals[3].astype(jnp.bfloat16), "dp", scatter_dimension=0, tiled=True
        ).astype(jnp.float32),
        lax.psum_scatter(
            totals[4].astype(jnp.bfloat16), "dp", scatter_dimension=1, tiled=True
        ).astype(jnp.float32),
        lax.psum_scatter(
            totals[5].astype(jnp.bfloat16), "dp", scatter_dimension=1, tiled=True
        ).astype(jnp.float32),
    )
    gains_sum, biases_sum = (
        lax.psum_scatter(totals[6], ("dp", "tensor"), scatter_dimension=1, tiled=True),
        lax.psum_scatter(totals[7], ("dp", "tensor"), scatter_dimension=1, tiled=True),
    )
    return (
        outputs,
        input_grads,
        qkv_sum,
        qv_sum,
        out_sum,
        up_sum,
        upb_sum,
        down_sum,
        gains_sum,
        biases_sum,
    )


NEGATIVE = -1e30
LANES = 2 * HEAD_DIM


def half_mask(shape, half):
    lane = lax.broadcasted_iota(jnp.int32, shape, 1)
    return (lane // HEAD_DIM) == half


def attend_kernel(q_ref, k_ref, v_ref, row_ref, col_ref, context_ref, stats_ref):
    query, keys, values = q_ref[...], k_ref[...], v_ref[...]
    keep = col_ref[...] == row_ref[...]
    total = jnp.zeros(context_ref.shape, jnp.float32)
    for half in range(2):
        own = half_mask(query.shape, half)
        masked_query = jnp.where(own, query, 0) * jnp.asarray(HEAD_DIM**-0.5, query.dtype)
        scores = lax.dot_general(
            keys, masked_query, (((1,), (1,)), ((), ())), preferred_element_type=jnp.float32
        )
        scores = jnp.where(keep, scores, NEGATIVE)
        highest = jnp.max(scores, axis=0, keepdims=True)
        shifted = jnp.exp(scores - highest)
        sums = jnp.sum(shifted, axis=0, keepdims=True)
        probs = (shifted * (1.0 / sums)).astype(jnp.bfloat16)
        own_values = jnp.where(own, values, 0)
        total += lax.dot_general(
            probs, own_values, (((0,), (0,)), ((), ())), preferred_element_type=jnp.float32
        )
        stats_ref[0, half : half + 1, :] = highest + jnp.log(sums)
    context_ref[...] = total.astype(context_ref.dtype)


def attend_back_kernel(
    q_ref, k_ref, v_ref, grad_ref, row_ref, col_ref, stats_ref, *rest
):
    query, keys, values, grad = q_ref[...], k_ref[...], v_ref[...], grad_ref[...]
    scale = jnp.asarray(HEAD_DIM**-0.5, query.dtype)
    keep = col_ref[...] == row_ref[...]
    zero = jnp.zeros(query.shape, jnp.float32)
    grad_query, grad_keys, grad_values = zero, zero, zero
    for half in range(2):
        own = half_mask(query.shape, half)
        own_query = jnp.where(own, query, 0) * scale
        own_keys = jnp.where(own, keys, 0) * scale
        own_grad = jnp.where(own, grad, 0)
        contract_last = (((1,), (1,)), ((), ()))
        scores = lax.dot_general(
            keys, own_query, contract_last, preferred_element_type=jnp.float32
        )
        scores = jnp.where(keep, scores, NEGATIVE)
        probs = jnp.exp(scores - stats_ref[0, half : half + 1, :])
        grad_values += jnp.dot(
            probs.astype(jnp.bfloat16), own_grad, preferred_element_type=jnp.float32
        )
        grad_probs = lax.dot_general(
            values, own_grad, contract_last, preferred_element_type=jnp.float32
        )
        weighted = probs * grad_probs
        grad_scores = (weighted - probs * jnp.sum(weighted, axis=0, keepdims=True)).astype(
            jnp.bfloat16
        )
        grad_keys += jnp.dot(grad_scores, own_query, preferred_element_type=jnp.float32)
        grad_query += lax.dot_general(
            grad_scores, own_keys, (((0,), (0,)), ((), ())), preferred_element_type=jnp.float32
        )
    pair, out_ref = pl.program_id(0), rest[-1]
    width = out_ref.shape[1] // 3
    for place, value in enumerate((grad_query, grad_keys, grad_values)):
        start = pl.multiple_of(place * width + pair * LANES, LANES)
        out_ref[:, pl.ds(start, LANES)] = value.astype(out_ref.dtype)


def attention_specs(rows, pairs, parts):
    inner = pairs // parts

    def column(place):
        return pl.BlockSpec(
            (rows, LANES),
            lambda i: (0, (i // inner) * (3 * inner) + place * inner + lax.rem(i, inner)),
        )

    plain = pl.BlockSpec((rows, LANES), lambda i: (0, i))
    row_ids = pl.BlockSpec((1, rows), lambda i: (0, 0))
    column_ids = pl.BlockSpec((rows, 1), lambda i: (0, 0))
    stats = pl.BlockSpec((1, 2, rows), lambda i: (i, 0, 0))
    return [column(place) for place in range(3)], plain, [row_ids, column_ids], stats


def attend_call(projected, segments, parts):
    rows, width = projected.shape[0], projected.shape[1] // 3
    pairs = width // LANES
    columns, plain, ids, stats = attention_specs(rows, pairs, parts)
    return pl.pallas_call(
        attend_kernel,
        grid=(pairs,),
        in_specs=columns + ids,
        out_specs=[plain, stats],
        out_shape=[
            jax.ShapeDtypeStruct((rows, width), jnp.bfloat16),
            jax.ShapeDtypeStruct((pairs, 2, rows), jnp.float32),
        ],
        compiler_params=pltpu.CompilerParams(vmem_limit_bytes=24 * 1024 * 1024),
        cost_estimate=pl.CostEstimate(
            flops=16 * pairs * rows * rows * LANES,
            bytes_accessed=8 * rows * width,
            transcendentals=2 * pairs * rows * rows,
        ),
        name="attend",
    )(projected, projected, projected, segments[None, :], segments[:, None])


def attend_back_call(projected, grad, segments, stats_in, parts, part, others=None):
    rows, width = grad.shape
    inner = width // LANES // parts

    def column(place):
        return pl.BlockSpec(
            (rows, LANES), lambda i: (0, part * (3 * inner) + place * inner + i)
        )

    ids = [pl.BlockSpec((1, rows), lambda i: (0, 0)), pl.BlockSpec((rows, 1), lambda i: (0, 0))]
    stats = pl.BlockSpec((1, 2, rows), lambda i: (part * inner + i, 0, 0))
    plain = pl.BlockSpec((rows, LANES), lambda i: (0, part * inner + i))
    rest = [] if others is None else [others]
    return pl.pallas_call(
        attend_back_kernel,
        grid=(inner,),
        in_specs=[column(place) for place in range(3)]
        + [plain]
        + ids
        + [stats]
        + [pl.BlockSpec(memory_space=pl.ANY)] * len(rest),
        out_specs=pl.BlockSpec((rows, 3 * width // parts), lambda i: (0, part)),
        out_shape=jax.ShapeDtypeStruct((rows, 3 * width), jnp.bfloat16),
        input_output_aliases={7: 0} if rest else {},
        compiler_params=pltpu.CompilerParams(vmem_limit_bytes=24 * 1024 * 1024),
        cost_estimate=pl.CostEstimate(
            flops=40 * inner * rows * rows * LANES,
            bytes_accessed=14 * rows * width // parts,
            transcendentals=2 * inner * rows * rows,
        ),
        name="attend_back",
    )(
        projected,
        projected,
        projected,
        grad,
        segments[None, :],
        segments[:, None],
        stats_in,
        *rest,
    )


def dot_nn(a, b):
    return jnp.dot(a, b, preferred_element_type=jnp.float32)


def dot_nt(a, b):
    return lax.dot_general(a, b, (((1,), (1,)), ((), ())), preferred_element_type=jnp.float32)


def dot_tn(a, b):
    return lax.dot_general(a, b, (((0,), (0,)), ((), ())), preferred_element_type=jnp.float32)


def gelu_pair(values):
    cdf = 0.5 * (1.0 + lax.erf(values * (0.5**0.5)))
    density = jnp.exp(-0.5 * values * values) * (0.5 / jnp.pi) ** 0.5
    return values * cdf, cdf + values * density


PLANE = ("x", "c", "y")
EVERY = ("y", "x", "c", "z")
SWAP = [(0, 1), (1, 0)]


def plane_permutes():
    def index(x, c, y):
        return (x * 2 + c) * 2 + y

    cells = [(x, y) for x in range(2) for y in range(2)]
    along = [(index(x, 0, y), index(1 - x, 0, y)) for x, y in cells]
    along += [(index(x, 1, y), index(x, 1, 1 - y)) for x, y in cells]
    cross = [(index(x, 0, y), index(1 - x, 1, y)) for x, y in cells]
    cross += [(index(x, 1, y), index(x, 0, 1 - y)) for x, y in cells]
    return along, cross, [(target, source) for source, target in cross]


def after(value, *done):
    return lax.optimization_barrier((value,) + done)[0]


def barrier(*values):
    return lax.optimization_barrier(values)


def place_kernel(table_ref, *refs, widths):
    pieces = refs[:8]
    outs, held, arrived, left = refs[8:-3], refs[-3], refs[-2], refs[-1]
    loads, stores = [], []
    for i, piece in enumerate(pieces):
        loads.append(pltpu.make_async_copy(piece, held.at[i], arrived.at[i]))
        loads[-1].start()
    for i, piece in enumerate(pieces):
        size, start = piece.shape[0], 0
        row = pl.multiple_of(table_ref[i] * size, size)
        loads[i].wait()
        for j, (out, width) in enumerate(zip(outs, widths)):
            column = pl.multiple_of(table_ref[8 + i] * width, width)
            stores.append(
                pltpu.make_async_copy(
                    held.at[i, :, pl.ds(start, width)],
                    out.at[pl.ds(row, size), pl.ds(column, width)],
                    left.at[i, j],
                )
            )
            stores[-1].start()
            start += width
    for store in stores:
        store.wait()


def place(pieces, table, widths):
    size = pieces[0].shape[0]
    anywhere = pl.BlockSpec(memory_space=pl.ANY)
    return pl.pallas_call(
        functools.partial(place_kernel, widths=widths),
        grid_spec=pltpu.PrefetchScalarGridSpec(
            num_scalar_prefetch=1,
            grid=(1,),
            in_specs=[anywhere] * 8,
            out_specs=[anywhere] * len(widths),
            scratch_shapes=[
                pltpu.VMEM((8, size, sum(widths)), jnp.bfloat16),
                pltpu.SemaphoreType.DMA((8,)),
                pltpu.SemaphoreType.DMA((8, len(widths))),
            ],
        ),
        out_shape=[jax.ShapeDtypeStruct((4 * size, 2 * w), jnp.bfloat16) for w in widths],
        compiler_params=pltpu.CompilerParams(vmem_limit_bytes=16 * 1024 * 1024),
        cost_estimate=pl.CostEstimate(
            flops=0, bytes_accessed=32 * size * sum(widths), transcendentals=0
        ),
        name="place",
    )(table, *pieces)


def plane_spots(core, x, y):
    main = jnp.where(core == 0, 2 - 2 * x, 2 * x)
    part = jnp.where(core == 0, y, 1 - y)
    rows = [2 * x + core, main + core, main + 1 - core, 3 - 2 * x - core]
    return rows, [y, part, part, 1 - y]


def gather_weight(pieces, coords, widths):
    x, c, y, _ = coords
    pieces = pieces + [lax.ppermute(item, "c", SWAP) for item in pieces[2:]]
    (rows, parts), (partner_rows, partner_parts) = (plane_spots(k, x, y) for k in (c, 1 - c))
    order = [rows[0], partner_rows[0]] + rows[1:] + partner_rows[1:]
    order += [parts[0], partner_parts[0]] + parts[1:] + partner_parts[1:]
    return place(pieces, jnp.stack(order).astype(jnp.int32), widths)


def scatter_kernel(table_ref, *refs, blocks):
    pieces, (out, held, arrived, left) = refs[:-4], refs[-4:]
    size = pieces[0].shape[0] // blocks
    width = pieces[0].shape[1]
    loads, stores = [], []
    for i, piece in enumerate(pieces):
        for j in range(blocks):
            rows = pl.ds(j * size, size)
            loads.append(
                pltpu.make_async_copy(piece.at[rows], held.at[i, rows], arrived.at[i, j])
            )
            loads[-1].start()
    for i in range(len(pieces)):
        for j in range(blocks):
            at = 2 * (i * blocks + j)
            row = pl.multiple_of(table_ref[at] * size, size)
            column = pl.multiple_of(table_ref[at + 1] * width, width)
            loads[i * blocks + j].wait()
            stores.append(
                pltpu.make_async_copy(
                    held.at[i, pl.ds(j * size, size)],
                    out.at[pl.ds(row, size), pl.ds(column, width)],
                    left.at[i, j],
                )
            )
            stores[-1].start()
    for store in stores:
        store.wait()


def finish_plane_first(pieces, coords, count):
    x, c, y, _ = coords
    rows, width = pieces[0].shape
    blocks = 4 * count
    table = []
    for core in (c, 1 - c):
        spots = list(zip(*plane_spots(core, x, y)))
        for level in range(count):
            for row, part in spots:
                table += [row * count + level, part]
    anywhere = pl.BlockSpec(memory_space=pl.ANY)
    return pl.pallas_call(
        functools.partial(scatter_kernel, blocks=blocks),
        grid_spec=pltpu.PrefetchScalarGridSpec(
            num_scalar_prefetch=1,
            grid=(1,),
            in_specs=[anywhere] * 2,
            out_specs=anywhere,
            scratch_shapes=[
                pltpu.VMEM((2, rows, width), jnp.bfloat16),
                pltpu.SemaphoreType.DMA((2, blocks)),
                pltpu.SemaphoreType.DMA((2, blocks)),
            ],
        ),
        out_shape=jax.ShapeDtypeStruct((rows, 2 * width), jnp.bfloat16),
        compiler_params=pltpu.CompilerParams(vmem_limit_bytes=16 * 1024 * 1024),
        cost_estimate=pl.CostEstimate(
            flops=0, bytes_accessed=8 * rows * width, transcendentals=0
        ),
        name="scatter",
    )(jnp.stack(table).astype(jnp.int32), *pieces)


def three_parts(values, rows):
    parts = []
    for _ in range(3):
        parts.append(lax.reduce_precision(values, exponent_bits=8, mantissa_bits=7))
        values = values - parts[-1]
    tile = jnp.concatenate(parts).astype(jnp.bfloat16).reshape(-1, LANES)
    return jnp.pad(tile, ((0, rows - tile.shape[0]), (0, 0)))


class Reduction:
    def __init__(self, pairs, coords):
        self.pairs = pairs
        self.x, self.c, self.y, _ = coords
        self.along, self.cross, _ = plane_permutes()
        x, c, y = self.x, self.c, self.y
        self.main_row = jnp.where(c == 0, 2 - 2 * x, 2 * x)
        self.main_part = jnp.where(c == 0, y, 1 - y)
        self.partner_row = jnp.where(c == 0, 2 * x, 2 - 2 * x)
        self.partner_part = 1 - self.main_part

    def block(self, row, count, part, extras=()):
        pieces, start = [], 0
        pairs, extras = barrier(self.pairs, list(extras))
        for left, right in pairs:
            size, width = left.shape[1] // 4, right.shape[1] // 2
            picked = lax.dynamic_slice_in_dim(left, row * size, count * size, 1)
            total = dot_tn(picked, lax.dynamic_slice_in_dim(right, part * width, width, 1))
            for extra, at in extras:
                if at is not None:
                    extra = lax.dynamic_slice_in_dim(extra, at * size, count * size, 0)
                total = total + extra[:, start : start + width].astype(jnp.float32)
            pieces.append(total.astype(jnp.bfloat16))
            start += width
        return pieces[0] if len(pieces) == 1 else jnp.concatenate(pieces, axis=1)

    def send(self):
        corner = self.block(3 - 2 * self.x - self.c, 1, 1 - self.y)
        main = self.block(self.partner_row, 2, self.partner_part)
        self.corner_in = lax.ppermute(corner, "c", SWAP)
        self.main_in = lax.ppermute(main, "c", SWAP)
        return corner, main

    def spread(self):
        x, c, y = self.x, self.c, self.y
        corner = self.block(2 - 2 * x + c, 1, 1 - y, [(self.corner_in, None)])
        self.corner_got = lax.ppermute(corner, PLANE, self.cross)
        main = self.block(self.main_row + c, 1, self.main_part, [(self.main_in, c)])
        self.kept_got = lax.ppermute(main, PLANE, self.along)
        return corner, main

    def forward(self):
        extras = [(self.main_in, 1 - self.c), (self.corner_got, None)]
        main = self.block(self.main_row + 1 - self.c, 1, self.main_part, extras)
        self.passed_got = lax.ppermute(main, PLANE, self.along)
        return main

    def hand_over(self):
        home = self.block(2 * self.x + 1 - self.c, 1, self.y, [(self.passed_got, None)])
        self.home_in = lax.ppermute(home, "c", SWAP)
        return home

    def finish(self):
        home = self.block(2 * self.x + self.c, 1, self.y, [(self.kept_got, None), (self.home_in, None)])
        return home, lax.psum_scatter(home, "z", scatter_dimension=0, tiled=True)


def sequence_parallel(
    layer_input,
    segment_ids,
    qkv_weight,
    qv_bias,
    out_weight,
    up_weight,
    up_bias,
    down_weight,
    norm_gains,
    row_biases,
    cotangent,
):
    low = jnp.bfloat16
    parts = lax.axis_size("y")
    grid = tuple(lax.axis_size(name) for name in ("x", "c", "z"))
    dp_count = grid[0] * grid[1] * grid[2]
    mine = lax.axis_index("y")
    coords = tuple(lax.axis_index(name) for name in ("x", "c", "y", "z"))
    half, width = layer_input.shape[1:]
    heads_local = qv_bias.shape[1]
    width_local = heads_local * HEAD_DIM
    hidden_local = up_weight.shape[1]
    wide = 3 * width_local
    span = range(parts)

    source = jnp.arange(width).reshape(grid[2], grid[0], grid[1], -1)
    source = source.transpose(1, 2, 0, 3).reshape(-1)
    chosen = lax.broadcasted_iota(jnp.int32, (width, width), 0) == source[None, :]
    order = chosen.astype(low)

    def own_sequence(rows):
        kept = lax.dynamic_index_in_dim(rows, mine, 0, keepdims=False)
        sent = lax.dynamic_index_in_dim(rows, 1 - mine, 0, keepdims=False)
        return jnp.concatenate([kept, lax.ppermute(sent, "y", SWAP)], axis=0)

    def own_rows(rows):
        rows = dot_nt(rows.astype(low), order).astype(low)
        received = lax.ppermute(rows[half:], "y", SWAP)
        first = jnp.where(mine == 0, rows[:half], received)
        second = jnp.where(mine == 0, received, rows[:half])
        return jnp.stack([first, second])

    small = jnp.concatenate(
        [
            qv_bias.astype(jnp.float32).reshape(-1),
            up_bias.astype(jnp.float32).reshape(-1),
            norm_gains.reshape(-1),
            row_biases.reshape(-1),
        ]
    )
    packed = jnp.concatenate(
        [
            qkv_weight[0],
            qkv_weight[1],
            qkv_weight[2],
            out_weight.T,
            three_parts(small, up_weight.shape[0]),
        ],
        axis=1,
    )

    def lane_of(piece):
        return lax.all_gather(piece, "z", axis=0, tiled=True)

    along, _, back = plane_permutes()

    def start_plane(lane):
        other = lax.ppermute(lane, "c", SWAP)
        main_other = lax.ppermute(other, PLANE, along)
        return [lane, other, lax.ppermute(lane, PLANE, along), main_other]

    lane = lane_of(packed)
    up_piece, down_piece, layer_input, cotangent = after(
        (up_weight, down_weight.T, layer_input, cotangent), packed
    )
    lane_up = lane_of(up_piece)
    down_pieces = start_plane(down_piece)
    rows_in, grad_output = own_sequence(layer_input), own_sequence(cotangent)
    down_pieces.append(lax.ppermute(down_pieces[2], PLANE, back))
    down_own = jnp.concatenate(
        [down_pieces[0], down_pieces[2], down_pieces[3], down_pieces[4]], axis=0
    )
    lane, down_own, rows_in, grad_output = barrier(lane, down_own, rows_in, grad_output)
    pieces = start_plane(lane)
    rows_in, grad_output = after((rows_in, grad_output), pieces[1])
    rows_in, grad_output = (dot_nn(item, order).astype(low) for item in (rows_in, grad_output))
    pieces[2], pieces[3], lane_up, rows_in, grad_output, down_own = barrier(
        pieces[2], pieces[3], lane_up, rows_in, grad_output, down_own
    )
    lane_down = lane_of(down_own)
    pieces.append(lax.ppermute(pieces[2], PLANE, back))
    up_pieces = start_plane(lane_up)
    pieces[4], up_pieces[1] = barrier(pieces[4], up_pieces[1])
    qkv_full, out_full, small_all = gather_weight(pieces, coords, (wide, width_local, LANES))
    segments = lax.dynamic_index_in_dim(segment_ids, mine, 0, keepdims=False)
    segments = jnp.where(mine == 0, segments, jnp.roll(segments, -half))

    small_all = small_all.reshape(grid + (-1, parts, LANES))[:, :, :, : 3 * small.size // LANES]
    small_all = small_all.astype(jnp.float32).transpose(4, 0, 1, 2, 3, 5)
    small_all = small_all.reshape((parts,) + grid + (3, small.size))
    small_all = small_all[..., 0, :] + small_all[..., 1, :] + small_all[..., 2, :]
    sizes = [qv_bias.size, up_bias.size, norm_gains.size, row_biases.size]
    starts = [0, sizes[0], sum(sizes[:2]), sum(sizes[:3])]

    def section(i, shard):
        values = small_all[..., starts[i] : starts[i] + sizes[i]]
        return values.reshape((parts,) + grid + shard.shape)

    qv_all = section(0, qv_bias).transpose(4, 0, 5, 3, 1, 2, 6).reshape(2, parts, width_local)
    upb_all = section(1, up_bias).transpose(0, 3, 1, 2, 4, 5).reshape(-1)

    def whole_rows(i, shard):
        values = section(i, shard).transpose(4, 1, 2, 3, 0, 5)
        return values.reshape(shard.shape[0], width)

    gains_all, biases_all = whole_rows(2, norm_gains), whole_rows(3, row_biases)
    none = jnp.zeros((width_local,), jnp.float32)
    qkv_bias = jnp.concatenate(
        [item for t in span for item in (qv_all[0, t], none, qv_all[1, t])]
    )

    up_pieces[2], qkv_full = barrier(up_pieces[2], qkv_full)
    projected = (dot_nn(rows_in, qkv_full) + qkv_bias).astype(low)
    up_pieces[3], projected = barrier(up_pieces[3], projected)
    up_pieces.append(lax.ppermute(after(up_pieces[2], projected), PLANE, back))
    context, stats = attend_call(projected, segments, parts)
    attention = dot_nt(context, out_full)
    residual_one = rows_in.astype(jnp.float32) + attention + biases_all[0]
    hidden, normed_one, inverse_one = normalize(residual_one, gains_all[0], biases_all[1])
    hidden_low = hidden.astype(low)
    (up_full,) = gather_weight(up_pieces, coords, (hidden_local,))
    activated, slope = gelu_pair(
        dot_nn(hidden_low, up_full) + upb_all
    )
    activated, slope = activated.astype(low), slope.astype(low)
    lane_down = after(lane_down, activated)
    lane_other = lax.ppermute(lane_down, "c", SWAP)
    down_full = finish_plane_first([lane_down, lane_other], coords, grid[2])
    branch = dot_nt(activated, down_full)
    residual_two = hidden + branch + biases_all[2]
    result, normed_two, inverse_two = normalize(residual_two, gains_all[1], biases_all[3])

    grad_output = grad_output.astype(jnp.float32)
    grad_two = norm_back(grad_output, normed_two, inverse_two, gains_all[1])
    branch_grad = grad_two.astype(low)

    down = Reduction([(branch_grad, activated)], coords)
    sent = down.send()
    columns = [slice(t * hidden_local, (t + 1) * hidden_local) for t in span]
    branch_late = after(branch_grad, *sent)
    grad_first = (dot_nn(branch_late, down_full[:, columns[0]]) * slope[:, columns[0]]).astype(low)
    down.corner_in = after(down.corner_in, grad_first)
    moved = down.spread()
    branch_late = after(branch_grad, *moved)
    grad_second = (dot_nn(branch_late, down_full[:, columns[1]]) * slope[:, columns[1]]).astype(low)
    grad_upper = jnp.concatenate([grad_first, grad_second], axis=1)
    up = Reduction([(hidden_low, grad_upper)], coords)
    sent = up.send()
    down.corner_got = after(down.corner_got, *sent)
    moved = down.forward()
    grad_hidden = grad_two + dot_nt(after(grad_upper, moved), up_full)
    grad_one = norm_back(grad_hidden, normed_one, inverse_one, gains_all[0])
    attention_grad = grad_one.astype(low)
    grad_context = dot_nn(attention_grad, out_full).astype(low)
    up.corner_in = after(up.corner_in, grad_context, down.kept_got)
    moved = up.spread()
    grad_projected = attend_back_call(
        projected, after(grad_context, *moved), segments, stats, parts, 0
    )
    down.passed_got = after(down.passed_got, grad_projected)
    moved = down.hand_over()
    up.corner_got = after(up.corner_got, moved)
    moved = up.forward()
    down.home_in = after(down.home_in, moved)
    moved, down_sum = down.finish()
    grad_projected = attend_back_call(
        projected, after(grad_context, moved), segments, stats, parts, 1, grad_projected
    )
    last = Reduction([(rows_in, grad_projected), (attention_grad, context)], coords)
    sent = last.send()
    up.passed_got = after(up.passed_got, *sent)
    moved = up.hand_over()
    last.corner_in = after(last.corner_in, moved, up.kept_got)
    moved = last.spread()
    up.home_in = after(up.home_in, *moved)
    moved, up_sum = up.finish()
    input_grad = grad_one + dot_nt(after(grad_projected, moved), qkv_full)
    last.corner_got = after(last.corner_got, input_grad)
    moved = last.forward()
    grad_output, grad_two, grad_hidden, grad_one, grad_upper, grad_projected = after(
        (grad_output, grad_two, grad_hidden, grad_one, grad_upper, grad_projected), moved
    )
    gain_two_grad = jnp.sum(grad_output * normed_two, axis=0)
    shift_two_grad = jnp.sum(grad_output, axis=0)
    down_bias_grad = jnp.sum(grad_two, axis=0)
    gain_one_grad = jnp.sum(grad_hidden * normed_one, axis=0)
    shift_one_grad = jnp.sum(grad_hidden, axis=0)
    out_bias_grad = jnp.sum(grad_one, axis=0)
    upb_grad = jnp.sum(grad_upper.astype(jnp.float32), axis=0)
    qkv_sums = jnp.sum(grad_projected.astype(jnp.float32), axis=0)
    last.passed_got = after(
        last.passed_got,
        *(gain_two_grad, shift_two_grad, down_bias_grad, gain_one_grad),
        *(shift_one_grad, out_bias_grad, upb_grad, qkv_sums, last.kept_got),
    )
    moved = last.hand_over()
    moved, last_sum = last.finish()
    input_grads = own_rows(after(input_grad, moved))
    outputs = own_rows(after(result, moved))

    qkv_sums = qkv_sums.reshape(parts, 3, width_local)
    dp_order = (grid[2], grid[0], grid[1])
    qv_grads = jnp.stack([qkv_sums[:, 0], qkv_sums[:, 2]], axis=1)
    qv_grads = qv_grads.reshape((parts, 2, heads_local) + dp_order + (-1,))
    qv_grads = qv_grads.transpose(0, 4, 5, 3, 1, 2, 6).reshape(parts * dp_count, -1)
    upb_grad = upb_grad.reshape((parts,) + dp_order + (-1,))
    upb_grad = upb_grad.transpose(0, 2, 3, 1, 4).reshape(parts * dp_count, -1)

    def split_rows(rows):
        count = len(rows)
        rows = jnp.stack(rows).reshape((count,) + grid + (parts, -1))
        return rows.transpose(4, 1, 2, 3, 0, 5).reshape(parts * dp_count, -1)

    small_grad = jnp.concatenate(
        [
            qv_grads,
            upb_grad,
            split_rows([gain_one_grad, gain_two_grad]),
            split_rows([out_bias_grad, shift_one_grad, down_bias_grad, shift_two_grad]),
        ],
        axis=1,
    )
    exchanged = lax.all_to_all(small_grad, EVERY, 0, 0, tiled=True)
    small_sum = jnp.sum(exchanged, axis=0)
    qv_sum, upb_sum, gains_sum, biases_sum = (
        small_sum[a : a + n] for a, n in zip(starts, sizes)
    )
    last_sum = last_sum.astype(jnp.float32)
    qkv_sum = last_sum[:, :wide].reshape(-1, 3, width_local).transpose(1, 0, 2)
    return (
        outputs,
        input_grads,
        qkv_sum,
        qv_sum.reshape(qv_bias.shape),
        last_sum[:, wide:].T,
        up_sum.astype(jnp.float32),
        upb_sum.reshape(up_bias.shape),
        down_sum.astype(jnp.float32).T,
        gains_sum.reshape(norm_gains.shape),
        biases_sum.reshape(row_biases.shape),
    )


def solution(mesh):
    groups = mesh.shape["dp"]
    parts = mesh.shape["tensor"]

    def program(*arrays):
        micro, width = arrays[0].shape[0], arrays[0].shape[2]
        fits = micro == 2 and parts == 2 and groups % 4 == 0 and width % (groups * 16) == 0
        if fits:
            dp, place = ("z", "x", "c"), "y"
            shape = (groups // 4, 2, 2, 2)
            used = Mesh(mesh.devices.reshape(shape), dp + (place,))
        else:
            dp, place, used = ("dp",), "tensor", mesh
        whole = dp + (place,)
        rows, vectors = P(None, whole, None), P(None, whole)
        weights = (
            P(None, dp, place),
            P(None, place, dp),
            P(place, dp),
            P(dp, place),
            P(place, dp),
            P(place, dp),
            vectors,
            vectors,
        )
        return jax.shard_map(
            sequence_parallel if fits else tensor_split,
            mesh=used,
            in_specs=(rows, P(None, dp)) + weights + (rows,),
            out_specs=(rows, rows) + weights,
            check_vma=False,
        )(*arrays)

    return program
```

```python
import functools

import jax
import jax.numpy as jnp
from jax import lax
from jax.experimental import pallas as pl
from jax.experimental.pallas import tpu as pltpu
from jax.sharding import Mesh
from jax.sharding import PartitionSpec as P

HEAD_DIM = 64


def gelu_exact(values):
    return jax.nn.gelu(values, approximate=False)


def normalize(rows, gain, shift):
    centered = rows - jnp.mean(rows, axis=-1, keepdims=True)
    variance = jnp.mean(centered * centered, axis=-1, keepdims=True)
    inverse = lax.rsqrt(variance + 1e-05)
    normed = centered * inverse
    return (normed * gain + shift, normed, inverse)


def norm_back(grad, normed, inverse, gain):
    scaled = grad * gain
    return inverse * (
        scaled
        - jnp.mean(scaled, axis=-1, keepdims=True)
        - normed * jnp.mean(scaled * normed, axis=-1, keepdims=True)
    )


def attend(query, keys, values, keep_mask, scale):
    scores = jnp.einsum("qhd,khd->hqk", query, keys, preferred_element_type=jnp.float32) * scale
    masked = jnp.where(keep_mask[None], scores, -1e30)
    highest = jnp.max(masked, axis=-1, keepdims=True)
    shifted = jnp.exp(masked - highest)
    totals = jnp.sum(shifted, axis=-1, keepdims=True)
    probs = (shifted / totals).astype(jnp.bfloat16)
    context = jnp.einsum("hqk,khd->qhd", probs, values, preferred_element_type=jnp.float32)
    return (context, highest + jnp.log(totals))


def attend_back(query, keys, values, keep_mask, logsumexp, grad_context, scale):
    scores = jnp.einsum("qhd,khd->hqk", query, keys, preferred_element_type=jnp.float32) * scale
    masked = jnp.where(keep_mask[None], scores, -1e30)
    probs = jnp.exp(masked - logsumexp)
    probs_low = probs.astype(jnp.bfloat16)
    grad_values = jnp.einsum(
        "hqk,qhd->khd", probs_low, grad_context, preferred_element_type=jnp.float32
    )
    grad_probs = jnp.einsum(
        "qhd,khd->hqk", grad_context, values, preferred_element_type=jnp.float32
    )
    grad_scores = probs * (grad_probs - jnp.sum(probs * grad_probs, axis=-1, keepdims=True))
    grad_low = grad_scores.astype(jnp.bfloat16)
    grad_query = (
        jnp.einsum("hqk,khd->qhd", grad_low, keys, preferred_element_type=jnp.float32) * scale
    )
    grad_keys = (
        jnp.einsum("hqk,qhd->khd", grad_low, query, preferred_element_type=jnp.float32) * scale
    )
    return (grad_query, grad_keys, grad_values)


def tensor_split(
    layer_input,
    segment_ids,
    qkv_weight,
    qv_bias,
    out_weight,
    up_weight,
    up_bias,
    down_weight,
    norm_gains,
    row_biases,
    cotangent,
):
    gains_all, biases_all = (
        lax.all_gather(norm_gains, ("dp", "tensor"), axis=1, tiled=True),
        lax.all_gather(row_biases, ("dp", "tensor"), axis=1, tiled=True),
    )
    shards = (qkv_weight, qv_bias, out_weight, up_weight, up_bias, down_weight)
    dp_count = lax.axis_size("dp")
    seq_len = segment_ids.shape[1]
    heads_local = qv_bias.shape[1]
    width_local = heads_local * HEAD_DIM
    scale = HEAD_DIM ** (-0.5)

    def micro_step(carry, inputs):
        rows_in, segments, grad_rows = inputs
        qkv_full, qv_full, out_full, up_full, upb_full, down_full = (
            lax.all_gather(shards[0], "dp", axis=1, tiled=True),
            lax.all_gather(shards[1], "dp", axis=2, tiled=True),
            lax.all_gather(shards[2], "dp", axis=1, tiled=True),
            lax.all_gather(shards[3], "dp", axis=0, tiled=True),
            lax.all_gather(shards[4], "dp", axis=1, tiled=True),
            lax.all_gather(shards[5], "dp", axis=1, tiled=True),
        )
        gathered = lax.all_gather(rows_in, "tensor", axis=0, tiled=True)
        projected = jnp.einsum(
            "rd,kdc->krc", gathered, qkv_full, preferred_element_type=jnp.float32
        )
        bias_flat = qv_full.reshape(2, width_local).astype(jnp.float32)
        split = (seq_len, heads_local, HEAD_DIM)
        query = (projected[0] + bias_flat[0]).astype(jnp.bfloat16).reshape(split)
        keys = projected[1].astype(jnp.bfloat16).reshape(split)
        values = (projected[2] + bias_flat[1]).astype(jnp.bfloat16).reshape(split)
        keep_mask = segments[:, None] == segments[None, :]
        attended, logsumexp = attend(query, keys, values, keep_mask, scale)
        context = attended.reshape(seq_len, width_local).astype(jnp.bfloat16)
        attention = lax.psum_scatter(
            jnp.dot(context, out_full, preferred_element_type=jnp.float32).astype(jnp.bfloat16),
            "tensor",
            scatter_dimension=0,
            tiled=True,
        ).astype(jnp.float32)
        residual_one = rows_in.astype(jnp.float32) + attention + biases_all[0]
        hidden, normed_one, inverse_one = normalize(residual_one, gains_all[0], biases_all[1])
        hidden_rows = lax.all_gather(hidden.astype(jnp.bfloat16), "tensor", axis=0, tiled=True)
        upper = jnp.dot(
            hidden_rows, up_full, preferred_element_type=jnp.float32
        ) + upb_full.reshape(-1).astype(jnp.float32)
        activated = gelu_exact(upper).astype(jnp.bfloat16)
        branch = lax.psum_scatter(
            jnp.dot(activated, down_full, preferred_element_type=jnp.float32).astype(jnp.bfloat16),
            "tensor",
            scatter_dimension=0,
            tiled=True,
        ).astype(jnp.float32)
        residual_two = hidden + branch + biases_all[2]
        result, normed_two, inverse_two = normalize(residual_two, gains_all[1], biases_all[3])
        qkv_back, qv_back, out_back, up_back, upb_back, down_back = (
            lax.all_gather(shards[0], "dp", axis=1, tiled=True),
            lax.all_gather(shards[1], "dp", axis=2, tiled=True),
            lax.all_gather(shards[2], "dp", axis=1, tiled=True),
            lax.all_gather(shards[3], "dp", axis=0, tiled=True),
            lax.all_gather(shards[4], "dp", axis=1, tiled=True),
            lax.all_gather(shards[5], "dp", axis=1, tiled=True),
        )
        grad_output = grad_rows.astype(jnp.float32)
        gain_two_grad = jnp.sum(grad_output * normed_two, axis=0)
        shift_two_grad = jnp.sum(grad_output, axis=0)
        grad_two = norm_back(grad_output, normed_two, inverse_two, gains_all[1])
        down_bias_grad = jnp.sum(grad_two, axis=0)
        branch_rows = lax.all_gather(grad_two.astype(jnp.bfloat16), "tensor", axis=0, tiled=True)
        down_grad = jnp.einsum(
            "rf,rd->fd", activated, branch_rows, preferred_element_type=jnp.float32
        )
        grad_active = jnp.einsum(
            "rd,fd->rf", branch_rows, down_back, preferred_element_type=jnp.float32
        )
        gelu_pull = jax.vjp(gelu_exact, upper)[1]
        grad_upper = gelu_pull(grad_active)[0].astype(jnp.bfloat16)
        up_bias_grad = jnp.sum(grad_upper.astype(jnp.float32), axis=0).reshape(1, -1)
        up_grad = jnp.einsum(
            "rd,rf->df", hidden_rows, grad_upper, preferred_element_type=jnp.float32
        )
        grad_hidden = grad_two + lax.psum_scatter(
            jnp.einsum("rf,df->rd", grad_upper, up_back, preferred_element_type=jnp.float32).astype(
                jnp.bfloat16
            ),
            "tensor",
            scatter_dimension=0,
            tiled=True,
        ).astype(jnp.float32)
        gain_one_grad = jnp.sum(grad_hidden * normed_one, axis=0)
        shift_one_grad = jnp.sum(grad_hidden, axis=0)
        grad_one = norm_back(grad_hidden, normed_one, inverse_one, gains_all[0])
        out_bias_grad = jnp.sum(grad_one, axis=0)
        attention_rows = lax.all_gather(grad_one.astype(jnp.bfloat16), "tensor", axis=0, tiled=True)
        out_grad = jnp.einsum(
            "rc,rd->cd", context, attention_rows, preferred_element_type=jnp.float32
        )
        grad_context = (
            jnp.einsum("rd,cd->rc", attention_rows, out_back, preferred_element_type=jnp.float32)
            .astype(jnp.bfloat16)
            .reshape(split)
        )
        grad_query, grad_keys, grad_values = attend_back(
            query, keys, values, keep_mask, logsumexp, grad_context, scale
        )
        grad_qkv = (
            jnp.stack([grad_query, grad_keys, grad_values])
            .reshape(3, seq_len, width_local)
            .astype(jnp.bfloat16)
        )
        bias_sums = jnp.sum(jnp.stack([grad_qkv[0], grad_qkv[2]]).astype(jnp.float32), axis=1)
        qv_grad = bias_sums.reshape(2, heads_local, HEAD_DIM)
        qkv_grad = jnp.einsum("rd,krc->kdc", gathered, grad_qkv, preferred_element_type=jnp.float32)
        input_grad = (
            grad_one
            + lax.psum_scatter(
                jnp.einsum(
                    "krc,kdc->rd", grad_qkv, qkv_back, preferred_element_type=jnp.float32
                ).astype(jnp.bfloat16),
                "tensor",
                scatter_dimension=0,
                tiled=True,
            ).astype(jnp.float32)
        ).astype(jnp.bfloat16)
        gains_grad = jnp.stack([gain_one_grad, gain_two_grad])
        biases_grad = jnp.stack([out_bias_grad, shift_one_grad, down_bias_grad, shift_two_grad])
        updates = (
            qkv_grad,
            qv_grad,
            out_grad,
            up_grad,
            up_bias_grad,
            down_grad,
            gains_grad,
            biases_grad,
        )
        carry = tuple((total + update for total, update in zip(carry, updates)))
        return (carry, (result.astype(jnp.bfloat16), input_grad))

    initial = (
        jnp.zeros((3, qkv_weight.shape[1] * dp_count, qkv_weight.shape[2]), jnp.float32),
        jnp.zeros((2, qv_bias.shape[1], qv_bias.shape[2] * dp_count), jnp.float32),
        jnp.zeros((out_weight.shape[0], out_weight.shape[1] * dp_count), jnp.float32),
        jnp.zeros((up_weight.shape[0] * dp_count, up_weight.shape[1]), jnp.float32),
        jnp.zeros((1, up_bias.shape[1] * dp_count), jnp.float32),
        jnp.zeros((down_weight.shape[0], down_weight.shape[1] * dp_count), jnp.float32),
        jnp.zeros(gains_all.shape, jnp.float32),
        jnp.zeros(biases_all.shape, jnp.float32),
    )
    totals, (outputs, input_grads) = lax.scan(
        micro_step, initial, (layer_input, segment_ids, cotangent)
    )
    qkv_sum, qv_sum, out_sum, up_sum, upb_sum, down_sum = (
        lax.psum_scatter(
            totals[0].astype(jnp.bfloat16), "dp", scatter_dimension=1, tiled=True
        ).astype(jnp.float32),
        lax.psum_scatter(
            totals[1].astype(jnp.bfloat16), "dp", scatter_dimension=2, tiled=True
        ).astype(jnp.float32),
        lax.psum_scatter(
            totals[2].astype(jnp.bfloat16), "dp", scatter_dimension=1, tiled=True
        ).astype(jnp.float32),
        lax.psum_scatter(
            totals[3].astype(jnp.bfloat16), "dp", scatter_dimension=0, tiled=True
        ).astype(jnp.float32),
        lax.psum_scatter(
            totals[4].astype(jnp.bfloat16), "dp", scatter_dimension=1, tiled=True
        ).astype(jnp.float32),
        lax.psum_scatter(
            totals[5].astype(jnp.bfloat16), "dp", scatter_dimension=1, tiled=True
        ).astype(jnp.float32),
    )
    gains_sum, biases_sum = (
        lax.psum_scatter(totals[6], ("dp", "tensor"), scatter_dimension=1, tiled=True),
        lax.psum_scatter(totals[7], ("dp", "tensor"), scatter_dimension=1, tiled=True),
    )
    return (
        outputs,
        input_grads,
        qkv_sum,
        qv_sum,
        out_sum,
        up_sum,
        upb_sum,
        down_sum,
        gains_sum,
        biases_sum,
    )


NEGATIVE = -1e30
LANES = 2 * HEAD_DIM


def half_mask(shape, half):
    lane = lax.broadcasted_iota(jnp.int32, shape, 1)
    return (lane // HEAD_DIM) == half


def attend_kernel(q_ref, k_ref, v_ref, row_ref, col_ref, context_ref, stats_ref):
    query, keys, values = q_ref[...], k_ref[...], v_ref[...]
    keep = col_ref[...] == row_ref[...]
    total = jnp.zeros(context_ref.shape, jnp.float32)
    for half in range(2):
        own = half_mask(query.shape, half)
        masked_query = jnp.where(own, query, 0) * jnp.asarray(HEAD_DIM**-0.5, query.dtype)
        scores = lax.dot_general(
            keys, masked_query, (((1,), (1,)), ((), ())), preferred_element_type=jnp.float32
        )
        scores = jnp.where(keep, scores, NEGATIVE)
        highest = jnp.max(scores, axis=0, keepdims=True)
        shifted = jnp.exp(scores - highest)
        sums = jnp.sum(shifted, axis=0, keepdims=True)
        probs = (shifted * (1.0 / sums)).astype(jnp.bfloat16)
        own_values = jnp.where(own, values, 0)
        total += lax.dot_general(
            probs, own_values, (((0,), (0,)), ((), ())), preferred_element_type=jnp.float32
        )
        stats_ref[0, half : half + 1, :] = highest + jnp.log(sums)
    context_ref[...] = total.astype(context_ref.dtype)


def attend_back_kernel(
    q_ref, k_ref, v_ref, grad_ref, row_ref, col_ref, stats_ref, *rest
):
    query, keys, values, grad = q_ref[...], k_ref[...], v_ref[...], grad_ref[...]
    scale = jnp.asarray(HEAD_DIM**-0.5, query.dtype)
    keep = col_ref[...] == row_ref[...]
    zero = jnp.zeros(query.shape, jnp.float32)
    grad_query, grad_keys, grad_values = zero, zero, zero
    for half in range(2):
        own = half_mask(query.shape, half)
        own_query = jnp.where(own, query, 0) * scale
        own_keys = jnp.where(own, keys, 0) * scale
        own_grad = jnp.where(own, grad, 0)
        contract_last = (((1,), (1,)), ((), ()))
        scores = lax.dot_general(
            keys, own_query, contract_last, preferred_element_type=jnp.float32
        )
        scores = jnp.where(keep, scores, NEGATIVE)
        probs = jnp.exp(scores - stats_ref[0, half : half + 1, :])
        grad_values += jnp.dot(
            probs.astype(jnp.bfloat16), own_grad, preferred_element_type=jnp.float32
        )
        grad_probs = lax.dot_general(
            values, own_grad, contract_last, preferred_element_type=jnp.float32
        )
        weighted = probs * grad_probs
        grad_scores = (weighted - probs * jnp.sum(weighted, axis=0, keepdims=True)).astype(
            jnp.bfloat16
        )
        grad_keys += jnp.dot(grad_scores, own_query, preferred_element_type=jnp.float32)
        grad_query += lax.dot_general(
            grad_scores, own_keys, (((0,), (0,)), ((), ())), preferred_element_type=jnp.float32
        )
    pair, out_ref = pl.program_id(0), rest[-1]
    width = out_ref.shape[1] // 3
    for place, value in enumerate((grad_query, grad_keys, grad_values)):
        start = pl.multiple_of(place * width + pair * LANES, LANES)
        out_ref[:, pl.ds(start, LANES)] = value.astype(out_ref.dtype)


def attention_specs(rows, pairs, parts):
    inner = pairs // parts

    def column(place):
        return pl.BlockSpec(
            (rows, LANES),
            lambda i: (0, (i // inner) * (3 * inner) + place * inner + lax.rem(i, inner)),
        )

    plain = pl.BlockSpec((rows, LANES), lambda i: (0, i))
    row_ids = pl.BlockSpec((1, rows), lambda i: (0, 0))
    column_ids = pl.BlockSpec((rows, 1), lambda i: (0, 0))
    stats = pl.BlockSpec((1, 2, rows), lambda i: (i, 0, 0))
    return [column(place) for place in range(3)], plain, [row_ids, column_ids], stats


def attend_call(projected, segments, parts):
    rows, width = projected.shape[0], projected.shape[1] // 3
    pairs = width // LANES
    columns, plain, ids, stats = attention_specs(rows, pairs, parts)
    return pl.pallas_call(
        attend_kernel,
        grid=(pairs,),
        in_specs=columns + ids,
        out_specs=[plain, stats],
        out_shape=[
            jax.ShapeDtypeStruct((rows, width), jnp.bfloat16),
            jax.ShapeDtypeStruct((pairs, 2, rows), jnp.float32),
        ],
        compiler_params=pltpu.CompilerParams(vmem_limit_bytes=14 * 1024 * 1024),
        cost_estimate=pl.CostEstimate(
            flops=16 * pairs * rows * rows * LANES,
            bytes_accessed=8 * rows * width,
            transcendentals=2 * pairs * rows * rows,
        ),
        name="attend",
    )(projected, projected, projected, segments[None, :], segments[:, None])


def attend_back_call(projected, grad, segments, stats_in, parts, part, others=None):
    rows, width = grad.shape
    inner = width // LANES // parts

    def column(place):
        return pl.BlockSpec(
            (rows, LANES), lambda i: (0, part * (3 * inner) + place * inner + i)
        )

    ids = [pl.BlockSpec((1, rows), lambda i: (0, 0)), pl.BlockSpec((rows, 1), lambda i: (0, 0))]
    stats = pl.BlockSpec((1, 2, rows), lambda i: (part * inner + i, 0, 0))
    plain = pl.BlockSpec((rows, LANES), lambda i: (0, part * inner + i))
    rest = [] if others is None else [others]
    return pl.pallas_call(
        attend_back_kernel,
        grid=(inner,),
        in_specs=[column(place) for place in range(3)]
        + [plain]
        + ids
        + [stats]
        + [pl.BlockSpec(memory_space=pl.ANY)] * len(rest),
        out_specs=pl.BlockSpec((rows, 3 * width // parts), lambda i: (0, part)),
        out_shape=jax.ShapeDtypeStruct((rows, 3 * width), jnp.bfloat16),
        input_output_aliases={7: 0} if rest else {},
        compiler_params=pltpu.CompilerParams(vmem_limit_bytes=14 * 1024 * 1024),
        cost_estimate=pl.CostEstimate(
            flops=40 * inner * rows * rows * LANES,
            bytes_accessed=14 * rows * width // parts,
            transcendentals=2 * inner * rows * rows,
        ),
        name="attend_back",
    )(
        projected,
        projected,
        projected,
        grad,
        segments[None, :],
        segments[:, None],
        stats_in,
        *rest,
    )


def dot_nn(a, b):
    return jnp.dot(a, b, preferred_element_type=jnp.float32)


def dot_nt(a, b):
    return lax.dot_general(a, b, (((1,), (1,)), ((), ())), preferred_element_type=jnp.float32)


def dot_tn(a, b):
    return lax.dot_general(a, b, (((0,), (0,)), ((), ())), preferred_element_type=jnp.float32)


def gelu_pair(values):
    cdf = 0.5 * (1.0 + lax.erf(values * (0.5**0.5)))
    density = jnp.exp(-0.5 * values * values) * (0.5 / jnp.pi) ** 0.5
    return values * cdf, cdf + values * density


PLANE = ("x", "c", "y")
EVERY = ("y", "x", "c", "z")
SWAP = [(0, 1), (1, 0)]


def plane_permutes():
    def index(x, c, y):
        return (x * 2 + c) * 2 + y

    cells = [(x, y) for x in range(2) for y in range(2)]
    along = [(index(x, 0, y), index(1 - x, 0, y)) for x, y in cells]
    along += [(index(x, 1, y), index(x, 1, 1 - y)) for x, y in cells]
    cross = [(index(x, 0, y), index(1 - x, 1, y)) for x, y in cells]
    cross += [(index(x, 1, y), index(x, 0, 1 - y)) for x, y in cells]
    return along, cross, [(target, source) for source, target in cross]


def after(value, *done):
    return lax.optimization_barrier((value,) + done)[0]


def barrier(*values):
    return lax.optimization_barrier(values)


def place_kernel(table_ref, *refs, widths):
    pieces = refs[:8]
    outs, held, arrived, left = refs[8:-3], refs[-3], refs[-2], refs[-1]
    loads, stores = [], []
    for i, piece in enumerate(pieces):
        loads.append(pltpu.make_async_copy(piece, held.at[i], arrived.at[i]))
        loads[-1].start()
    for i, piece in enumerate(pieces):
        size, start = piece.shape[0], 0
        row = pl.multiple_of(table_ref[i] * size, size)
        loads[i].wait()
        for j, (out, width) in enumerate(zip(outs, widths)):
            column = pl.multiple_of(table_ref[8 + i] * width, width)
            stores.append(
                pltpu.make_async_copy(
                    held.at[i, :, pl.ds(start, width)],
                    out.at[pl.ds(row, size), pl.ds(column, width)],
                    left.at[i, j],
                )
            )
            stores[-1].start()
            start += width
    for store in stores:
        store.wait()


def place(pieces, table, widths):
    size = pieces[0].shape[0]
    anywhere = pl.BlockSpec(memory_space=pl.ANY)
    return pl.pallas_call(
        functools.partial(place_kernel, widths=widths),
        grid_spec=pltpu.PrefetchScalarGridSpec(
            num_scalar_prefetch=1,
            grid=(1,),
            in_specs=[anywhere] * 8,
            out_specs=[anywhere] * len(widths),
            scratch_shapes=[
                pltpu.VMEM((8, size, sum(widths)), jnp.bfloat16),
                pltpu.SemaphoreType.DMA((8,)),
                pltpu.SemaphoreType.DMA((8, len(widths))),
            ],
        ),
        out_shape=[jax.ShapeDtypeStruct((4 * size, 2 * w), jnp.bfloat16) for w in widths],
        compiler_params=pltpu.CompilerParams(vmem_limit_bytes=16 * 1024 * 1024),
        cost_estimate=pl.CostEstimate(
            flops=0, bytes_accessed=32 * size * sum(widths), transcendentals=0
        ),
        name="place",
    )(table, *pieces)


def plane_spots(core, x, y):
    main = jnp.where(core == 0, 2 - 2 * x, 2 * x)
    part = jnp.where(core == 0, y, 1 - y)
    rows = [2 * x + core, main + core, main + 1 - core, 3 - 2 * x - core]
    return rows, [y, part, part, 1 - y]


def gather_weight(pieces, coords, widths):
    x, c, y, _ = coords
    pieces = pieces + [lax.ppermute(item, "c", SWAP) for item in pieces[2:]]
    (rows, parts), (partner_rows, partner_parts) = (plane_spots(k, x, y) for k in (c, 1 - c))
    order = [rows[0], partner_rows[0]] + rows[1:] + partner_rows[1:]
    order += [parts[0], partner_parts[0]] + parts[1:] + partner_parts[1:]
    return place(pieces, jnp.stack(order).astype(jnp.int32), widths)


def three_parts(values, rows):
    parts = []
    for _ in range(3):
        parts.append(lax.reduce_precision(values, exponent_bits=8, mantissa_bits=7))
        values = values - parts[-1]
    tile = jnp.concatenate(parts).astype(jnp.bfloat16).reshape(-1, LANES)
    return jnp.pad(tile, ((0, rows - tile.shape[0]), (0, 0)))


class Reduction:
    def __init__(self, pairs, coords):
        self.pairs = pairs
        self.x, self.c, self.y, _ = coords
        self.along, self.cross, _ = plane_permutes()
        x, c, y = self.x, self.c, self.y
        self.main_row = jnp.where(c == 0, 2 - 2 * x, 2 * x)
        self.main_part = jnp.where(c == 0, y, 1 - y)
        self.partner_row = jnp.where(c == 0, 2 * x, 2 - 2 * x)
        self.partner_part = 1 - self.main_part

    def block(self, row, count, part, extras=()):
        pieces, start = [], 0
        pairs, extras = barrier(self.pairs, list(extras))
        for left, right in pairs:
            size, width = left.shape[1] // 4, right.shape[1] // 2
            picked = lax.dynamic_slice_in_dim(left, row * size, count * size, 1)
            total = dot_tn(picked, lax.dynamic_slice_in_dim(right, part * width, width, 1))
            for extra, at in extras:
                if at is not None:
                    extra = lax.dynamic_slice_in_dim(extra, at * size, count * size, 0)
                total = total + extra[:, start : start + width].astype(jnp.float32)
            pieces.append(total.astype(jnp.bfloat16))
            start += width
        return pieces[0] if len(pieces) == 1 else jnp.concatenate(pieces, axis=1)

    def send(self):
        corner = self.block(3 - 2 * self.x - self.c, 1, 1 - self.y)
        main = self.block(self.partner_row, 2, self.partner_part)
        self.corner_in = lax.ppermute(corner, "c", SWAP)
        self.main_in = lax.ppermute(main, "c", SWAP)
        return corner, main

    def spread(self):
        x, c, y = self.x, self.c, self.y
        corner = self.block(2 - 2 * x + c, 1, 1 - y, [(self.corner_in, None)])
        self.corner_got = lax.ppermute(corner, PLANE, self.cross)
        main = self.block(self.main_row + c, 1, self.main_part, [(self.main_in, c)])
        self.kept_got = lax.ppermute(main, PLANE, self.along)
        return corner, main

    def forward(self):
        extras = [(self.main_in, 1 - self.c), (self.corner_got, None)]
        main = self.block(self.main_row + 1 - self.c, 1, self.main_part, extras)
        self.passed_got = lax.ppermute(main, PLANE, self.along)
        return main

    def hand_over(self):
        home = self.block(2 * self.x + 1 - self.c, 1, self.y, [(self.passed_got, None)])
        self.home_in = lax.ppermute(home, "c", SWAP)
        return home

    def finish(self):
        home = self.block(2 * self.x + self.c, 1, self.y, [(self.kept_got, None), (self.home_in, None)])
        return home, lax.psum_scatter(home, "z", scatter_dimension=0, tiled=True)


def sequence_parallel(
    layer_input,
    segment_ids,
    qkv_weight,
    qv_bias,
    out_weight,
    up_weight,
    up_bias,
    down_weight,
    norm_gains,
    row_biases,
    cotangent,
):
    low = jnp.bfloat16
    parts = lax.axis_size("y")
    grid = tuple(lax.axis_size(name) for name in ("x", "c", "z"))
    dp_count = grid[0] * grid[1] * grid[2]
    mine = lax.axis_index("y")
    coords = tuple(lax.axis_index(name) for name in ("x", "c", "y", "z"))
    half, width = layer_input.shape[1:]
    heads_local = qv_bias.shape[1]
    width_local = heads_local * HEAD_DIM
    hidden_local = up_weight.shape[1]
    wide = 3 * width_local
    span = range(parts)

    source = jnp.arange(width).reshape(grid[2], grid[0], grid[1], -1)
    source = source.transpose(1, 2, 0, 3).reshape(-1)
    chosen = lax.broadcasted_iota(jnp.int32, (width, width), 0) == source[None, :]
    order = chosen.astype(low)

    def own_sequence(rows):
        kept = lax.dynamic_index_in_dim(rows, mine, 0, keepdims=False)
        sent = lax.dynamic_index_in_dim(rows, 1 - mine, 0, keepdims=False)
        return jnp.concatenate([kept, lax.ppermute(sent, "y", SWAP)], axis=0)

    def own_rows(rows):
        rows = dot_nt(rows.astype(low), order).astype(low)
        received = lax.ppermute(rows[half:], "y", SWAP)
        first = jnp.where(mine == 0, rows[:half], received)
        second = jnp.where(mine == 0, received, rows[:half])
        return jnp.stack([first, second])

    small = jnp.concatenate(
        [
            qv_bias.astype(jnp.float32).reshape(-1),
            up_bias.astype(jnp.float32).reshape(-1),
            norm_gains.reshape(-1),
            row_biases.reshape(-1),
        ]
    )
    packed = jnp.concatenate(
        [
            qkv_weight[0],
            qkv_weight[1],
            qkv_weight[2],
            out_weight.T,
            three_parts(small, up_weight.shape[0]),
        ],
        axis=1,
    )

    def lane_of(piece):
        return lax.all_gather(piece, "z", axis=0, tiled=True)

    along, _, back = plane_permutes()

    def start_plane(lane):
        other = lax.ppermute(lane, "c", SWAP)
        main_other = lax.ppermute(other, PLANE, along)
        return [lane, other, lax.ppermute(lane, PLANE, along), main_other]

    lane = lane_of(packed)
    lane_up = lane_of(after(up_weight, packed))
    lane_down = lane_of(after(down_weight.T, packed))
    layer_input, cotangent = after((layer_input, cotangent), packed)
    rows_in, grad_output = own_sequence(layer_input), own_sequence(cotangent)
    lane, rows_in, grad_output = barrier(lane, rows_in, grad_output)
    pieces = start_plane(lane)
    rows_in, grad_output = after((rows_in, grad_output), pieces[1])
    rows_in, grad_output = (dot_nn(item, order).astype(low) for item in (rows_in, grad_output))
    pieces[2], pieces[3], rows_in, grad_output = barrier(
        pieces[2], pieces[3], rows_in, grad_output
    )
    pieces.append(lax.ppermute(pieces[2], PLANE, back))
    up_pieces = start_plane(after(lane_up, pieces[2]))
    pieces[4], up_pieces[1] = barrier(pieces[4], up_pieces[1])
    qkv_full, out_full, small_all = gather_weight(pieces, coords, (wide, width_local, LANES))
    segments = lax.dynamic_index_in_dim(segment_ids, mine, 0, keepdims=False)
    segments = jnp.where(mine == 0, segments, jnp.roll(segments, -half))

    small_all = small_all.reshape(grid + (-1, parts, LANES))[:, :, :, : 3 * small.size // LANES]
    small_all = small_all.astype(jnp.float32).transpose(4, 0, 1, 2, 3, 5)
    small_all = small_all.reshape((parts,) + grid + (3, small.size))
    small_all = small_all[..., 0, :] + small_all[..., 1, :] + small_all[..., 2, :]
    sizes = [qv_bias.size, up_bias.size, norm_gains.size, row_biases.size]
    starts = [0, sizes[0], sum(sizes[:2]), sum(sizes[:3])]

    def section(i, shard):
        values = small_all[..., starts[i] : starts[i] + sizes[i]]
        return values.reshape((parts,) + grid + shard.shape)

    qv_all = section(0, qv_bias).transpose(4, 0, 5, 3, 1, 2, 6).reshape(2, parts, width_local)
    upb_all = section(1, up_bias).transpose(0, 3, 1, 2, 4, 5).reshape(-1)

    def whole_rows(i, shard):
        values = section(i, shard).transpose(4, 1, 2, 3, 0, 5)
        return values.reshape(shard.shape[0], width)

    gains_all, biases_all = whole_rows(2, norm_gains), whole_rows(3, row_biases)
    none = jnp.zeros((width_local,), jnp.float32)
    qkv_bias = jnp.concatenate(
        [item for t in span for item in (qv_all[0, t], none, qv_all[1, t])]
    )

    up_pieces[2], qkv_full = barrier(up_pieces[2], qkv_full)
    projected = (dot_nn(rows_in, qkv_full) + qkv_bias).astype(low)
    up_pieces[3], projected = barrier(up_pieces[3], projected)
    up_pieces.append(lax.ppermute(after(up_pieces[2], projected), PLANE, back))
    down_pieces = start_plane(after(lane_down, projected))
    context, stats = attend_call(after(projected, down_pieces[1]), segments, parts)
    down_pieces[2], context = barrier(down_pieces[2], context)
    down_pieces.append(lax.ppermute(down_pieces[2], PLANE, back))
    attention = dot_nt(context, out_full)
    residual_one = rows_in.astype(jnp.float32) + attention + biases_all[0]
    hidden, normed_one, inverse_one = normalize(residual_one, gains_all[0], biases_all[1])
    hidden_low = hidden.astype(low)
    (up_full,) = gather_weight(up_pieces, coords, (hidden_local,))
    activated, slope = gelu_pair(
        dot_nn(hidden_low, up_full) + upb_all
    )
    activated, slope = activated.astype(low), slope.astype(low)
    (down_full,) = gather_weight(down_pieces, coords, (hidden_local,))
    branch = dot_nt(activated, down_full)
    residual_two = hidden + branch + biases_all[2]
    result, normed_two, inverse_two = normalize(residual_two, gains_all[1], biases_all[3])

    result_low = barrier(result.astype(low))[0]
    grad_output = grad_output.astype(jnp.float32)
    grad_two = norm_back(grad_output, normed_two, inverse_two, gains_all[1])
    branch_grad = grad_two.astype(low)

    down = Reduction([(branch_grad, activated)], coords)
    sent = down.send()
    columns = [slice(t * hidden_local, (t + 1) * hidden_local) for t in span]
    branch_late = after(branch_grad, *sent)
    grad_first = (dot_nn(branch_late, down_full[:, columns[0]]) * slope[:, columns[0]]).astype(low)
    down.corner_in = after(down.corner_in, grad_first)
    moved = down.spread()
    branch_late = after(branch_grad, *moved)
    grad_second = (dot_nn(branch_late, down_full[:, columns[1]]) * slope[:, columns[1]]).astype(low)
    grad_upper = jnp.concatenate([grad_first, grad_second], axis=1)
    up = Reduction([(hidden_low, grad_upper)], coords)
    sent = up.send()
    down.corner_got = after(down.corner_got, *sent)
    moved = down.forward()
    grad_hidden = grad_two + dot_nt(after(grad_upper, moved), up_full)
    grad_one = norm_back(grad_hidden, normed_one, inverse_one, gains_all[0])
    attention_grad = grad_one.astype(low)
    grad_context = dot_nn(attention_grad, out_full).astype(low)
    up.corner_in = after(up.corner_in, grad_context, down.kept_got)
    moved = up.spread()
    grad_projected = attend_back_call(
        projected, after(grad_context, *moved), segments, stats, parts, 0
    )
    down.passed_got = after(down.passed_got, grad_projected)
    moved = down.hand_over()
    up.corner_got = after(up.corner_got, moved)
    moved = up.forward()
    down.home_in = after(down.home_in, moved)
    moved, down_sum = down.finish()
    grad_projected = attend_back_call(
        projected, after(grad_context, moved), segments, stats, parts, 1, grad_projected
    )
    last = Reduction([(rows_in, grad_projected), (attention_grad, context)], coords)
    sent = last.send()
    up.passed_got = after(up.passed_got, *sent)
    moved = up.hand_over()
    last.corner_in = after(last.corner_in, moved, up.kept_got)
    moved = last.spread()
    up.home_in = after(up.home_in, *moved)
    moved, up_sum = up.finish()
    input_grad = grad_one + dot_nt(after(grad_projected, moved), qkv_full)
    last.corner_got = after(last.corner_got, input_grad)
    moved = last.forward()
    grad_output, grad_two, grad_hidden, grad_one, grad_upper, grad_projected = after(
        (grad_output, grad_two, grad_hidden, grad_one, grad_upper, grad_projected), moved
    )
    gain_two_grad = jnp.sum(grad_output * normed_two, axis=0)
    shift_two_grad = jnp.sum(grad_output, axis=0)
    down_bias_grad = jnp.sum(grad_two, axis=0)
    gain_one_grad = jnp.sum(grad_hidden * normed_one, axis=0)
    shift_one_grad = jnp.sum(grad_hidden, axis=0)
    out_bias_grad = jnp.sum(grad_one, axis=0)
    upb_grad = jnp.sum(grad_upper.astype(jnp.float32), axis=0)
    qkv_sums = jnp.sum(grad_projected.astype(jnp.float32), axis=0)
    last.passed_got = after(
        last.passed_got,
        *(gain_two_grad, shift_two_grad, down_bias_grad, gain_one_grad),
        *(shift_one_grad, out_bias_grad, upb_grad, qkv_sums, last.kept_got),
    )
    moved = last.hand_over()
    moved, last_sum = last.finish()
    input_grads = own_rows(after(input_grad, moved))
    outputs = own_rows(after(result_low, moved))

    qkv_sums = qkv_sums.reshape(parts, 3, width_local)
    dp_order = (grid[2], grid[0], grid[1])
    qv_grads = jnp.stack([qkv_sums[:, 0], qkv_sums[:, 2]], axis=1)
    qv_grads = qv_grads.reshape((parts, 2, heads_local) + dp_order + (-1,))
    qv_grads = qv_grads.transpose(0, 4, 5, 3, 1, 2, 6).reshape(parts * dp_count, -1)
    upb_grad = upb_grad.reshape((parts,) + dp_order + (-1,))
    upb_grad = upb_grad.transpose(0, 2, 3, 1, 4).reshape(parts * dp_count, -1)

    def split_rows(rows):
        count = len(rows)
        rows = jnp.stack(rows).reshape((count,) + grid + (parts, -1))
        return rows.transpose(4, 1, 2, 3, 0, 5).reshape(parts * dp_count, -1)

    small_grad = jnp.concatenate(
        [
            qv_grads,
            upb_grad,
            split_rows([gain_one_grad, gain_two_grad]),
            split_rows([out_bias_grad, shift_one_grad, down_bias_grad, shift_two_grad]),
        ],
        axis=1,
    )
    small_grad = after(small_grad, moved)
    exchanged = lax.all_to_all(small_grad, EVERY, 0, 0, tiled=True)
    small_sum = jnp.sum(exchanged, axis=0)
    qv_sum, upb_sum, gains_sum, biases_sum = (
        small_sum[a : a + n] for a, n in zip(starts, sizes)
    )
    last_sum = last_sum.astype(jnp.float32)
    qkv_sum = last_sum[:, :wide].reshape(-1, 3, width_local).transpose(1, 0, 2)
    return (
        outputs,
        input_grads,
        qkv_sum,
        qv_sum.reshape(qv_bias.shape),
        last_sum[:, wide:].T,
        up_sum.astype(jnp.float32),
        upb_sum.reshape(up_bias.shape),
        down_sum.astype(jnp.float32).T,
        gains_sum.reshape(norm_gains.shape),
        biases_sum.reshape(row_biases.shape),
    )


def solution(mesh):
    groups = mesh.shape["dp"]
    parts = mesh.shape["tensor"]

    def program(*arrays):
        micro, width = arrays[0].shape[0], arrays[0].shape[2]
        fits = micro == 2 and parts == 2 and groups % 4 == 0 and width % (groups * 16) == 0
        if fits:
            dp, place = ("z", "x", "c"), "y"
            shape = (groups // 4, 2, 2, 2)
            used = Mesh(mesh.devices.reshape(shape), dp + (place,))
        else:
            dp, place, used = ("dp",), "tensor", mesh
        whole = dp + (place,)
        rows, vectors = P(None, whole, None), P(None, whole)
        weights = (
            P(None, dp, place),
            P(None, place, dp),
            P(place, dp),
            P(dp, place),
            P(place, dp),
            P(place, dp),
            vectors,
            vectors,
        )
        return jax.shard_map(
            sequence_parallel if fits else tensor_split,
            mesh=used,
            in_specs=(rows, P(None, dp)) + weights + (rows,),
            out_specs=(rows, rows) + weights,
            check_vma=False,
        )(*arrays)

    return program
```

```python
import functools

import jax
import jax.numpy as jnp
from jax import lax
from jax.experimental import pallas as pl
from jax.experimental.pallas import tpu as pltpu
from jax.sharding import Mesh
from jax.sharding import PartitionSpec as P

HEAD_DIM = 64


def gelu_exact(values):
    return jax.nn.gelu(values, approximate=False)


def normalize(rows, gain, shift):
    centered = rows - jnp.mean(rows, axis=-1, keepdims=True)
    variance = jnp.mean(centered * centered, axis=-1, keepdims=True)
    inverse = lax.rsqrt(variance + 1e-05)
    normed = centered * inverse
    return (normed * gain + shift, normed, inverse)


def norm_back(grad, normed, inverse, gain):
    scaled = grad * gain
    return inverse * (
        scaled
        - jnp.mean(scaled, axis=-1, keepdims=True)
        - normed * jnp.mean(scaled * normed, axis=-1, keepdims=True)
    )


def attend(query, keys, values, keep_mask, scale):
    scores = jnp.einsum("qhd,khd->hqk", query, keys, preferred_element_type=jnp.float32) * scale
    masked = jnp.where(keep_mask[None], scores, -1e30)
    highest = jnp.max(masked, axis=-1, keepdims=True)
    shifted = jnp.exp(masked - highest)
    totals = jnp.sum(shifted, axis=-1, keepdims=True)
    probs = (shifted / totals).astype(jnp.bfloat16)
    context = jnp.einsum("hqk,khd->qhd", probs, values, preferred_element_type=jnp.float32)
    return (context, highest + jnp.log(totals))


def attend_back(query, keys, values, keep_mask, logsumexp, grad_context, scale):
    scores = jnp.einsum("qhd,khd->hqk", query, keys, preferred_element_type=jnp.float32) * scale
    masked = jnp.where(keep_mask[None], scores, -1e30)
    probs = jnp.exp(masked - logsumexp)
    probs_low = probs.astype(jnp.bfloat16)
    grad_values = jnp.einsum(
        "hqk,qhd->khd", probs_low, grad_context, preferred_element_type=jnp.float32
    )
    grad_probs = jnp.einsum(
        "qhd,khd->hqk", grad_context, values, preferred_element_type=jnp.float32
    )
    grad_scores = probs * (grad_probs - jnp.sum(probs * grad_probs, axis=-1, keepdims=True))
    grad_low = grad_scores.astype(jnp.bfloat16)
    grad_query = (
        jnp.einsum("hqk,khd->qhd", grad_low, keys, preferred_element_type=jnp.float32) * scale
    )
    grad_keys = (
        jnp.einsum("hqk,qhd->khd", grad_low, query, preferred_element_type=jnp.float32) * scale
    )
    return (grad_query, grad_keys, grad_values)


def tensor_split(
    layer_input,
    segment_ids,
    qkv_weight,
    qv_bias,
    out_weight,
    up_weight,
    up_bias,
    down_weight,
    norm_gains,
    row_biases,
    cotangent,
):
    gains_all, biases_all = (
        lax.all_gather(norm_gains, ("dp", "tensor"), axis=1, tiled=True),
        lax.all_gather(row_biases, ("dp", "tensor"), axis=1, tiled=True),
    )
    shards = (qkv_weight, qv_bias, out_weight, up_weight, up_bias, down_weight)
    dp_count = lax.axis_size("dp")
    seq_len = segment_ids.shape[1]
    heads_local = qv_bias.shape[1]
    width_local = heads_local * HEAD_DIM
    scale = HEAD_DIM ** (-0.5)

    def micro_step(carry, inputs):
        rows_in, segments, grad_rows = inputs
        qkv_full, qv_full, out_full, up_full, upb_full, down_full = (
            lax.all_gather(shards[0], "dp", axis=1, tiled=True),
            lax.all_gather(shards[1], "dp", axis=2, tiled=True),
            lax.all_gather(shards[2], "dp", axis=1, tiled=True),
            lax.all_gather(shards[3], "dp", axis=0, tiled=True),
            lax.all_gather(shards[4], "dp", axis=1, tiled=True),
            lax.all_gather(shards[5], "dp", axis=1, tiled=True),
        )
        gathered = lax.all_gather(rows_in, "tensor", axis=0, tiled=True)
        projected = jnp.einsum(
            "rd,kdc->krc", gathered, qkv_full, preferred_element_type=jnp.float32
        )
        bias_flat = qv_full.reshape(2, width_local).astype(jnp.float32)
        split = (seq_len, heads_local, HEAD_DIM)
        query = (projected[0] + bias_flat[0]).astype(jnp.bfloat16).reshape(split)
        keys = projected[1].astype(jnp.bfloat16).reshape(split)
        values = (projected[2] + bias_flat[1]).astype(jnp.bfloat16).reshape(split)
        keep_mask = segments[:, None] == segments[None, :]
        attended, logsumexp = attend(query, keys, values, keep_mask, scale)
        context = attended.reshape(seq_len, width_local).astype(jnp.bfloat16)
        attention = lax.psum_scatter(
            jnp.dot(context, out_full, preferred_element_type=jnp.float32).astype(jnp.bfloat16),
            "tensor",
            scatter_dimension=0,
            tiled=True,
        ).astype(jnp.float32)
        residual_one = rows_in.astype(jnp.float32) + attention + biases_all[0]
        hidden, normed_one, inverse_one = normalize(residual_one, gains_all[0], biases_all[1])
        hidden_rows = lax.all_gather(hidden.astype(jnp.bfloat16), "tensor", axis=0, tiled=True)
        upper = jnp.dot(
            hidden_rows, up_full, preferred_element_type=jnp.float32
        ) + upb_full.reshape(-1).astype(jnp.float32)
        activated = gelu_exact(upper).astype(jnp.bfloat16)
        branch = lax.psum_scatter(
            jnp.dot(activated, down_full, preferred_element_type=jnp.float32).astype(jnp.bfloat16),
            "tensor",
            scatter_dimension=0,
            tiled=True,
        ).astype(jnp.float32)
        residual_two = hidden + branch + biases_all[2]
        result, normed_two, inverse_two = normalize(residual_two, gains_all[1], biases_all[3])
        qkv_back, qv_back, out_back, up_back, upb_back, down_back = (
            lax.all_gather(shards[0], "dp", axis=1, tiled=True),
            lax.all_gather(shards[1], "dp", axis=2, tiled=True),
            lax.all_gather(shards[2], "dp", axis=1, tiled=True),
            lax.all_gather(shards[3], "dp", axis=0, tiled=True),
            lax.all_gather(shards[4], "dp", axis=1, tiled=True),
            lax.all_gather(shards[5], "dp", axis=1, tiled=True),
        )
        grad_output = grad_rows.astype(jnp.float32)
        gain_two_grad = jnp.sum(grad_output * normed_two, axis=0)
        shift_two_grad = jnp.sum(grad_output, axis=0)
        grad_two = norm_back(grad_output, normed_two, inverse_two, gains_all[1])
        down_bias_grad = jnp.sum(grad_two, axis=0)
        branch_rows = lax.all_gather(grad_two.astype(jnp.bfloat16), "tensor", axis=0, tiled=True)
        down_grad = jnp.einsum(
            "rf,rd->fd", activated, branch_rows, preferred_element_type=jnp.float32
        )
        grad_active = jnp.einsum(
            "rd,fd->rf", branch_rows, down_back, preferred_element_type=jnp.float32
        )
        gelu_pull = jax.vjp(gelu_exact, upper)[1]
        grad_upper = gelu_pull(grad_active)[0].astype(jnp.bfloat16)
        up_bias_grad = jnp.sum(grad_upper.astype(jnp.float32), axis=0).reshape(1, -1)
        up_grad = jnp.einsum(
            "rd,rf->df", hidden_rows, grad_upper, preferred_element_type=jnp.float32
        )
        grad_hidden = grad_two + lax.psum_scatter(
            jnp.einsum("rf,df->rd", grad_upper, up_back, preferred_element_type=jnp.float32).astype(
                jnp.bfloat16
            ),
            "tensor",
            scatter_dimension=0,
            tiled=True,
        ).astype(jnp.float32)
        gain_one_grad = jnp.sum(grad_hidden * normed_one, axis=0)
        shift_one_grad = jnp.sum(grad_hidden, axis=0)
        grad_one = norm_back(grad_hidden, normed_one, inverse_one, gains_all[0])
        out_bias_grad = jnp.sum(grad_one, axis=0)
        attention_rows = lax.all_gather(grad_one.astype(jnp.bfloat16), "tensor", axis=0, tiled=True)
        out_grad = jnp.einsum(
            "rc,rd->cd", context, attention_rows, preferred_element_type=jnp.float32
        )
        grad_context = (
            jnp.einsum("rd,cd->rc", attention_rows, out_back, preferred_element_type=jnp.float32)
            .astype(jnp.bfloat16)
            .reshape(split)
        )
        grad_query, grad_keys, grad_values = attend_back(
            query, keys, values, keep_mask, logsumexp, grad_context, scale
        )
        grad_qkv = (
            jnp.stack([grad_query, grad_keys, grad_values])
            .reshape(3, seq_len, width_local)
            .astype(jnp.bfloat16)
        )
        bias_sums = jnp.sum(jnp.stack([grad_qkv[0], grad_qkv[2]]).astype(jnp.float32), axis=1)
        qv_grad = bias_sums.reshape(2, heads_local, HEAD_DIM)
        qkv_grad = jnp.einsum("rd,krc->kdc", gathered, grad_qkv, preferred_element_type=jnp.float32)
        input_grad = (
            grad_one
            + lax.psum_scatter(
                jnp.einsum(
                    "krc,kdc->rd", grad_qkv, qkv_back, preferred_element_type=jnp.float32
                ).astype(jnp.bfloat16),
                "tensor",
                scatter_dimension=0,
                tiled=True,
            ).astype(jnp.float32)
        ).astype(jnp.bfloat16)
        gains_grad = jnp.stack([gain_one_grad, gain_two_grad])
        biases_grad = jnp.stack([out_bias_grad, shift_one_grad, down_bias_grad, shift_two_grad])
        updates = (
            qkv_grad,
            qv_grad,
            out_grad,
            up_grad,
            up_bias_grad,
            down_grad,
            gains_grad,
            biases_grad,
        )
        carry = tuple((total + update for total, update in zip(carry, updates)))
        return (carry, (result.astype(jnp.bfloat16), input_grad))

    initial = (
        jnp.zeros((3, qkv_weight.shape[1] * dp_count, qkv_weight.shape[2]), jnp.float32),
        jnp.zeros((2, qv_bias.shape[1], qv_bias.shape[2] * dp_count), jnp.float32),
        jnp.zeros((out_weight.shape[0], out_weight.shape[1] * dp_count), jnp.float32),
        jnp.zeros((up_weight.shape[0] * dp_count, up_weight.shape[1]), jnp.float32),
        jnp.zeros((1, up_bias.shape[1] * dp_count), jnp.float32),
        jnp.zeros((down_weight.shape[0], down_weight.shape[1] * dp_count), jnp.float32),
        jnp.zeros(gains_all.shape, jnp.float32),
        jnp.zeros(biases_all.shape, jnp.float32),
    )
    totals, (outputs, input_grads) = lax.scan(
        micro_step, initial, (layer_input, segment_ids, cotangent)
    )
    qkv_sum, qv_sum, out_sum, up_sum, upb_sum, down_sum = (
        lax.psum_scatter(
            totals[0].astype(jnp.bfloat16), "dp", scatter_dimension=1, tiled=True
        ).astype(jnp.float32),
        lax.psum_scatter(
            totals[1].astype(jnp.bfloat16), "dp", scatter_dimension=2, tiled=True
        ).astype(jnp.float32),
        lax.psum_scatter(
            totals[2].astype(jnp.bfloat16), "dp", scatter_dimension=1, tiled=True
        ).astype(jnp.float32),
        lax.psum_scatter(
            totals[3].astype(jnp.bfloat16), "dp", scatter_dimension=0, tiled=True
        ).astype(jnp.float32),
        lax.psum_scatter(
            totals[4].astype(jnp.bfloat16), "dp", scatter_dimension=1, tiled=True
        ).astype(jnp.float32),
        lax.psum_scatter(
            totals[5].astype(jnp.bfloat16), "dp", scatter_dimension=1, tiled=True
        ).astype(jnp.float32),
    )
    gains_sum, biases_sum = (
        lax.psum_scatter(totals[6], ("dp", "tensor"), scatter_dimension=1, tiled=True),
        lax.psum_scatter(totals[7], ("dp", "tensor"), scatter_dimension=1, tiled=True),
    )
    return (
        outputs,
        input_grads,
        qkv_sum,
        qv_sum,
        out_sum,
        up_sum,
        upb_sum,
        down_sum,
        gains_sum,
        biases_sum,
    )


NEGATIVE = -1e30
LANES = 2 * HEAD_DIM


def half_mask(shape, half):
    lane = lax.broadcasted_iota(jnp.int32, shape, 1)
    return (lane // HEAD_DIM) == half


def attend_kernel(q_ref, k_ref, v_ref, row_ref, col_ref, context_ref, stats_ref):
    query, keys, values = q_ref[...], k_ref[...], v_ref[...]
    keep = col_ref[...] == row_ref[...]
    total = jnp.zeros(context_ref.shape, jnp.float32)
    for half in range(2):
        own = half_mask(query.shape, half)
        masked_query = jnp.where(own, query, 0) * jnp.asarray(HEAD_DIM**-0.5, query.dtype)
        scores = lax.dot_general(
            keys, masked_query, (((1,), (1,)), ((), ())), preferred_element_type=jnp.float32
        )
        scores = jnp.where(keep, scores, NEGATIVE)
        highest = jnp.max(scores, axis=0, keepdims=True)
        shifted = jnp.exp(scores - highest)
        sums = jnp.sum(shifted, axis=0, keepdims=True)
        probs = (shifted * (1.0 / sums)).astype(jnp.bfloat16)
        own_values = jnp.where(own, values, 0)
        total += lax.dot_general(
            probs, own_values, (((0,), (0,)), ((), ())), preferred_element_type=jnp.float32
        )
        stats_ref[0, half : half + 1, :] = highest + jnp.log(sums)
    context_ref[...] = total.astype(context_ref.dtype)


def attend_back_kernel(
    q_ref, k_ref, v_ref, grad_ref, row_ref, col_ref, stats_ref, *rest
):
    query, keys, values, grad = q_ref[...], k_ref[...], v_ref[...], grad_ref[...]
    scale = jnp.asarray(HEAD_DIM**-0.5, query.dtype)
    keep = col_ref[...] == row_ref[...]
    zero = jnp.zeros(query.shape, jnp.float32)
    grad_query, grad_keys, grad_values = zero, zero, zero
    for half in range(2):
        own = half_mask(query.shape, half)
        own_query = jnp.where(own, query, 0) * scale
        own_keys = jnp.where(own, keys, 0) * scale
        own_grad = jnp.where(own, grad, 0)
        contract_last = (((1,), (1,)), ((), ()))
        scores = lax.dot_general(
            keys, own_query, contract_last, preferred_element_type=jnp.float32
        )
        scores = jnp.where(keep, scores, NEGATIVE)
        probs = jnp.exp(scores - stats_ref[0, half : half + 1, :])
        grad_values += jnp.dot(
            probs.astype(jnp.bfloat16), own_grad, preferred_element_type=jnp.float32
        )
        grad_probs = lax.dot_general(
            values, own_grad, contract_last, preferred_element_type=jnp.float32
        )
        weighted = probs * grad_probs
        grad_scores = (weighted - probs * jnp.sum(weighted, axis=0, keepdims=True)).astype(
            jnp.bfloat16
        )
        grad_keys += jnp.dot(grad_scores, own_query, preferred_element_type=jnp.float32)
        grad_query += lax.dot_general(
            grad_scores, own_keys, (((0,), (0,)), ((), ())), preferred_element_type=jnp.float32
        )
    pair, out_ref = pl.program_id(0), rest[-1]
    width = out_ref.shape[1] // 3
    for place, value in enumerate((grad_query, grad_keys, grad_values)):
        start = pl.multiple_of(place * width + pair * LANES, LANES)
        out_ref[:, pl.ds(start, LANES)] = value.astype(out_ref.dtype)


def attention_specs(rows, pairs, parts):
    inner = pairs // parts

    def column(place):
        return pl.BlockSpec(
            (rows, LANES),
            lambda i: (0, (i // inner) * (3 * inner) + place * inner + lax.rem(i, inner)),
        )

    plain = pl.BlockSpec((rows, LANES), lambda i: (0, i))
    row_ids = pl.BlockSpec((1, rows), lambda i: (0, 0))
    column_ids = pl.BlockSpec((rows, 1), lambda i: (0, 0))
    stats = pl.BlockSpec((1, 2, rows), lambda i: (i, 0, 0))
    return [column(place) for place in range(3)], plain, [row_ids, column_ids], stats


def attend_call(projected, segments, parts):
    rows, width = projected.shape[0], projected.shape[1] // 3
    pairs = width // LANES
    columns, plain, ids, stats = attention_specs(rows, pairs, parts)
    return pl.pallas_call(
        attend_kernel,
        grid=(pairs,),
        in_specs=columns + ids,
        out_specs=[plain, stats],
        out_shape=[
            jax.ShapeDtypeStruct((rows, width), jnp.bfloat16),
            jax.ShapeDtypeStruct((pairs, 2, rows), jnp.float32),
        ],
        compiler_params=pltpu.CompilerParams(vmem_limit_bytes=14 * 1024 * 1024),
        cost_estimate=pl.CostEstimate(
            flops=16 * pairs * rows * rows * LANES,
            bytes_accessed=8 * rows * width,
            transcendentals=2 * pairs * rows * rows,
        ),
        name="attend",
    )(projected, projected, projected, segments[None, :], segments[:, None])


def attend_back_call(projected, grad, segments, stats_in, parts, part, others=None):
    rows, width = grad.shape
    inner = width // LANES // parts

    def column(place):
        return pl.BlockSpec(
            (rows, LANES), lambda i: (0, part * (3 * inner) + place * inner + i)
        )

    ids = [pl.BlockSpec((1, rows), lambda i: (0, 0)), pl.BlockSpec((rows, 1), lambda i: (0, 0))]
    stats = pl.BlockSpec((1, 2, rows), lambda i: (part * inner + i, 0, 0))
    plain = pl.BlockSpec((rows, LANES), lambda i: (0, part * inner + i))
    rest = [] if others is None else [others]
    return pl.pallas_call(
        attend_back_kernel,
        grid=(inner,),
        in_specs=[column(place) for place in range(3)]
        + [plain]
        + ids
        + [stats]
        + [pl.BlockSpec(memory_space=pl.ANY)] * len(rest),
        out_specs=pl.BlockSpec((rows, 3 * width // parts), lambda i: (0, part)),
        out_shape=jax.ShapeDtypeStruct((rows, 3 * width), jnp.bfloat16),
        input_output_aliases={7: 0} if rest else {},
        compiler_params=pltpu.CompilerParams(vmem_limit_bytes=14 * 1024 * 1024),
        cost_estimate=pl.CostEstimate(
            flops=40 * inner * rows * rows * LANES,
            bytes_accessed=14 * rows * width // parts,
            transcendentals=2 * inner * rows * rows,
        ),
        name="attend_back",
    )(
        projected,
        projected,
        projected,
        grad,
        segments[None, :],
        segments[:, None],
        stats_in,
        *rest,
    )


def dot_nn(a, b):
    return jnp.dot(a, b, preferred_element_type=jnp.float32)


def dot_nt(a, b):
    return lax.dot_general(a, b, (((1,), (1,)), ((), ())), preferred_element_type=jnp.float32)


def dot_tn(a, b):
    return lax.dot_general(a, b, (((0,), (0,)), ((), ())), preferred_element_type=jnp.float32)


def gelu_pair(values):
    cdf = 0.5 * (1.0 + lax.erf(values * (0.5**0.5)))
    density = jnp.exp(-0.5 * values * values) * (0.5 / jnp.pi) ** 0.5
    return values * cdf, cdf + values * density


PLANE = ("x", "c", "y")
EVERY = ("y", "x", "c", "z")
SWAP = [(0, 1), (1, 0)]


def plane_permutes():
    def index(x, c, y):
        return (x * 2 + c) * 2 + y

    cells = [(x, y) for x in range(2) for y in range(2)]
    along = [(index(x, 0, y), index(1 - x, 0, y)) for x, y in cells]
    along += [(index(x, 1, y), index(x, 1, 1 - y)) for x, y in cells]
    cross = [(index(x, 0, y), index(1 - x, 1, y)) for x, y in cells]
    cross += [(index(x, 1, y), index(x, 0, 1 - y)) for x, y in cells]
    return along, cross, [(target, source) for source, target in cross]


def after(value, *done):
    return lax.optimization_barrier((value,) + done)[0]


def barrier(*values):
    return lax.optimization_barrier(values)


def place_kernel(table_ref, *refs, widths):
    pieces = refs[:8]
    outs, held, arrived, left = refs[8:-3], refs[-3], refs[-2], refs[-1]
    loads, stores = [], []
    for i, piece in enumerate(pieces):
        loads.append(pltpu.make_async_copy(piece, held.at[i], arrived.at[i]))
        loads[-1].start()
    for i, piece in enumerate(pieces):
        size, start = piece.shape[0], 0
        row = pl.multiple_of(table_ref[i] * size, size)
        loads[i].wait()
        for j, (out, width) in enumerate(zip(outs, widths)):
            column = pl.multiple_of(table_ref[8 + i] * width, width)
            stores.append(
                pltpu.make_async_copy(
                    held.at[i, :, pl.ds(start, width)],
                    out.at[pl.ds(row, size), pl.ds(column, width)],
                    left.at[i, j],
                )
            )
            stores[-1].start()
            start += width
    for store in stores:
        store.wait()


def place(pieces, table, widths):
    size = pieces[0].shape[0]
    anywhere = pl.BlockSpec(memory_space=pl.ANY)
    return pl.pallas_call(
        functools.partial(place_kernel, widths=widths),
        grid_spec=pltpu.PrefetchScalarGridSpec(
            num_scalar_prefetch=1,
            grid=(1,),
            in_specs=[anywhere] * 8,
            out_specs=[anywhere] * len(widths),
            scratch_shapes=[
                pltpu.VMEM((8, size, sum(widths)), jnp.bfloat16),
                pltpu.SemaphoreType.DMA((8,)),
                pltpu.SemaphoreType.DMA((8, len(widths))),
            ],
        ),
        out_shape=[jax.ShapeDtypeStruct((4 * size, 2 * w), jnp.bfloat16) for w in widths],
        compiler_params=pltpu.CompilerParams(vmem_limit_bytes=16 * 1024 * 1024),
        cost_estimate=pl.CostEstimate(
            flops=0, bytes_accessed=32 * size * sum(widths), transcendentals=0
        ),
        name="place",
    )(table, *pieces)


def plane_spots(core, x, y):
    main = jnp.where(core == 0, 2 - 2 * x, 2 * x)
    part = jnp.where(core == 0, y, 1 - y)
    rows = [2 * x + core, main + core, main + 1 - core, 3 - 2 * x - core]
    return rows, [y, part, part, 1 - y]


def gather_weight(pieces, coords, widths):
    x, c, y, _ = coords
    pieces = pieces + [lax.ppermute(item, "c", SWAP) for item in pieces[2:]]
    (rows, parts), (partner_rows, partner_parts) = (plane_spots(k, x, y) for k in (c, 1 - c))
    order = [rows[0], partner_rows[0]] + rows[1:] + partner_rows[1:]
    order += [parts[0], partner_parts[0]] + parts[1:] + partner_parts[1:]
    return place(pieces, jnp.stack(order).astype(jnp.int32), widths)


def three_parts(values, rows):
    parts = []
    for _ in range(3):
        parts.append(lax.reduce_precision(values, exponent_bits=8, mantissa_bits=7))
        values = values - parts[-1]
    tile = jnp.concatenate(parts).astype(jnp.bfloat16).reshape(-1, LANES)
    return jnp.pad(tile, ((0, rows - tile.shape[0]), (0, 0)))


class Reduction:
    def __init__(self, pairs, coords):
        self.pairs = pairs
        self.x, self.c, self.y, _ = coords
        self.along, self.cross, _ = plane_permutes()
        x, c, y = self.x, self.c, self.y
        self.main_row = jnp.where(c == 0, 2 - 2 * x, 2 * x)
        self.main_part = jnp.where(c == 0, y, 1 - y)
        self.partner_row = jnp.where(c == 0, 2 * x, 2 - 2 * x)
        self.partner_part = 1 - self.main_part

    def block(self, row, count, part, extras=()):
        pieces, start = [], 0
        pairs, extras = barrier(self.pairs, list(extras))
        for left, right in pairs:
            size, width = left.shape[1] // 4, right.shape[1] // 2
            picked = lax.dynamic_slice_in_dim(left, row * size, count * size, 1)
            total = dot_tn(picked, lax.dynamic_slice_in_dim(right, part * width, width, 1))
            for extra, at in extras:
                if at is not None:
                    extra = lax.dynamic_slice_in_dim(extra, at * size, count * size, 0)
                total = total + extra[:, start : start + width].astype(jnp.float32)
            pieces.append(total.astype(jnp.bfloat16))
            start += width
        return pieces[0] if len(pieces) == 1 else jnp.concatenate(pieces, axis=1)

    def send(self):
        corner = self.block(3 - 2 * self.x - self.c, 1, 1 - self.y)
        main = self.block(self.partner_row, 2, self.partner_part)
        self.corner_in = lax.ppermute(corner, "c", SWAP)
        self.main_in = lax.ppermute(main, "c", SWAP)
        return corner, main

    def spread(self):
        x, c, y = self.x, self.c, self.y
        corner = self.block(2 - 2 * x + c, 1, 1 - y, [(self.corner_in, None)])
        self.corner_got = lax.ppermute(corner, PLANE, self.cross)
        main = self.block(self.main_row + c, 1, self.main_part, [(self.main_in, c)])
        self.kept_got = lax.ppermute(main, PLANE, self.along)
        return corner, main

    def forward(self):
        extras = [(self.main_in, 1 - self.c), (self.corner_got, None)]
        main = self.block(self.main_row + 1 - self.c, 1, self.main_part, extras)
        self.passed_got = lax.ppermute(main, PLANE, self.along)
        return main

    def hand_over(self):
        home = self.block(2 * self.x + 1 - self.c, 1, self.y, [(self.passed_got, None)])
        self.home_in = lax.ppermute(home, "c", SWAP)
        return home

    def finish(self):
        home = self.block(2 * self.x + self.c, 1, self.y, [(self.kept_got, None), (self.home_in, None)])
        return home, lax.psum_scatter(home, "z", scatter_dimension=0, tiled=True)


def sequence_parallel(
    layer_input,
    segment_ids,
    qkv_weight,
    qv_bias,
    out_weight,
    up_weight,
    up_bias,
    down_weight,
    norm_gains,
    row_biases,
    cotangent,
):
    low = jnp.bfloat16
    parts = lax.axis_size("y")
    grid = tuple(lax.axis_size(name) for name in ("x", "c", "z"))
    dp_count = grid[0] * grid[1] * grid[2]
    mine = lax.axis_index("y")
    coords = tuple(lax.axis_index(name) for name in ("x", "c", "y", "z"))
    half, width = layer_input.shape[1:]
    heads_local = qv_bias.shape[1]
    width_local = heads_local * HEAD_DIM
    hidden_local = up_weight.shape[1]
    wide = 3 * width_local
    span = range(parts)

    source = jnp.arange(width).reshape(grid[2], grid[0], grid[1], -1)
    source = source.transpose(1, 2, 0, 3).reshape(-1)
    chosen = lax.broadcasted_iota(jnp.int32, (width, width), 0) == source[None, :]
    order = chosen.astype(low)

    def own_sequence(rows):
        kept = lax.dynamic_index_in_dim(rows, mine, 0, keepdims=False)
        sent = lax.dynamic_index_in_dim(rows, 1 - mine, 0, keepdims=False)
        return jnp.concatenate([kept, lax.ppermute(sent, "y", SWAP)], axis=0)

    def own_rows(rows):
        rows = dot_nt(rows.astype(low), order).astype(low)
        received = lax.ppermute(rows[half:], "y", SWAP)
        first = jnp.where(mine == 0, rows[:half], received)
        second = jnp.where(mine == 0, received, rows[:half])
        return jnp.stack([first, second])

    small = jnp.concatenate(
        [
            qv_bias.astype(jnp.float32).reshape(-1),
            up_bias.astype(jnp.float32).reshape(-1),
            norm_gains.reshape(-1),
            row_biases.reshape(-1),
        ]
    )
    packed = jnp.concatenate(
        [
            qkv_weight[0],
            qkv_weight[1],
            qkv_weight[2],
            out_weight.T,
            three_parts(small, up_weight.shape[0]),
        ],
        axis=1,
    )

    def lane_of(piece):
        return lax.all_gather(piece, "z", axis=0, tiled=True)

    along, _, back = plane_permutes()

    def start_plane(lane):
        other = lax.ppermute(lane, "c", SWAP)
        main_other = lax.ppermute(other, PLANE, along)
        return [lane, other, lax.ppermute(lane, PLANE, along), main_other]

    lane = lane_of(packed)
    lane_up = lane_of(after(up_weight, packed))
    lane_down = lane_of(after(down_weight.T, packed))
    layer_input, cotangent = after((layer_input, cotangent), packed)
    rows_in, grad_output = own_sequence(layer_input), own_sequence(cotangent)
    lane, rows_in, grad_output = barrier(lane, rows_in, grad_output)
    pieces = start_plane(lane)
    rows_in, grad_output = after((rows_in, grad_output), pieces[1])
    rows_in, grad_output = (dot_nn(item, order).astype(low) for item in (rows_in, grad_output))
    pieces[2], pieces[3], rows_in, grad_output = barrier(
        pieces[2], pieces[3], rows_in, grad_output
    )
    pieces.append(lax.ppermute(pieces[2], PLANE, back))
    up_pieces = start_plane(after(lane_up, pieces[2]))
    pieces[4], up_pieces[1] = barrier(pieces[4], up_pieces[1])
    qkv_full, out_full, small_all = gather_weight(pieces, coords, (wide, width_local, LANES))
    segments = lax.dynamic_index_in_dim(segment_ids, mine, 0, keepdims=False)
    segments = jnp.where(mine == 0, segments, jnp.roll(segments, -half))

    small_all = small_all.reshape(grid + (-1, parts, LANES))[:, :, :, : 3 * small.size // LANES]
    small_all = small_all.astype(jnp.float32).transpose(4, 0, 1, 2, 3, 5)
    small_all = small_all.reshape((parts,) + grid + (3, small.size))
    small_all = small_all[..., 0, :] + small_all[..., 1, :] + small_all[..., 2, :]
    sizes = [qv_bias.size, up_bias.size, norm_gains.size, row_biases.size]
    starts = [0, sizes[0], sum(sizes[:2]), sum(sizes[:3])]

    def section(i, shard):
        values = small_all[..., starts[i] : starts[i] + sizes[i]]
        return values.reshape((parts,) + grid + shard.shape)

    qv_all = section(0, qv_bias).transpose(4, 0, 5, 3, 1, 2, 6).reshape(2, parts, width_local)
    upb_all = section(1, up_bias).transpose(0, 3, 1, 2, 4, 5).reshape(-1)

    def whole_rows(i, shard):
        values = section(i, shard).transpose(4, 1, 2, 3, 0, 5)
        return values.reshape(shard.shape[0], width)

    gains_all, biases_all = whole_rows(2, norm_gains), whole_rows(3, row_biases)
    none = jnp.zeros((width_local,), jnp.float32)
    qkv_bias = jnp.concatenate(
        [item for t in span for item in (qv_all[0, t], none, qv_all[1, t])]
    )

    up_pieces[2], qkv_full = barrier(up_pieces[2], qkv_full)
    projected = (dot_nn(rows_in, qkv_full) + qkv_bias).astype(low)
    up_pieces[3], projected = barrier(up_pieces[3], projected)
    up_pieces.append(lax.ppermute(after(up_pieces[2], projected), PLANE, back))
    down_pieces = start_plane(after(lane_down, projected))
    context, stats = attend_call(after(projected, down_pieces[1]), segments, parts)
    down_pieces[2], down_pieces[3], up_pieces[4], context = barrier(
        down_pieces[2], down_pieces[3], up_pieces[4], context
    )
    down_pieces.append(lax.ppermute(down_pieces[2], PLANE, back))
    attention = dot_nt(context, out_full)
    residual_one = rows_in.astype(jnp.float32) + attention + biases_all[0]
    hidden, normed_one, inverse_one = normalize(residual_one, gains_all[0], biases_all[1])
    hidden_low = hidden.astype(low)
    (up_full,) = gather_weight(up_pieces, coords, (hidden_local,))
    activated, slope = gelu_pair(
        dot_nn(hidden_low, up_full) + upb_all
    )
    activated, slope = activated.astype(low), slope.astype(low)
    down_pieces[4], activated = barrier(down_pieces[4], activated)
    (down_full,) = gather_weight(down_pieces, coords, (hidden_local,))
    branch = dot_nt(activated, down_full)
    residual_two = hidden + branch + biases_all[2]
    result, normed_two, inverse_two = normalize(residual_two, gains_all[1], biases_all[3])

    result_low = barrier(result.astype(low))[0]
    grad_output = grad_output.astype(jnp.float32)
    grad_two = norm_back(grad_output, normed_two, inverse_two, gains_all[1])
    branch_grad = grad_two.astype(low)

    down = Reduction([(branch_grad, activated)], coords)
    sent = down.send()
    columns = [slice(t * hidden_local, (t + 1) * hidden_local) for t in span]
    branch_late = after(branch_grad, *sent)
    grad_first = (dot_nn(branch_late, down_full[:, columns[0]]) * slope[:, columns[0]]).astype(low)
    down.corner_in = after(down.corner_in, grad_first)
    moved = down.spread()
    branch_late = after(branch_grad, *moved)
    grad_second = (dot_nn(branch_late, down_full[:, columns[1]]) * slope[:, columns[1]]).astype(low)
    grad_upper = jnp.concatenate([grad_first, grad_second], axis=1)
    up = Reduction([(hidden_low, grad_upper)], coords)
    sent = up.send()
    down.corner_got = after(down.corner_got, *sent)
    moved = down.forward()
    grad_hidden = grad_two + dot_nt(after(grad_upper, moved), up_full)
    grad_one = norm_back(grad_hidden, normed_one, inverse_one, gains_all[0])
    attention_grad = grad_one.astype(low)
    grad_context = dot_nn(attention_grad, out_full).astype(low)
    up.corner_in = after(up.corner_in, grad_context, down.kept_got)
    moved = up.spread()
    grad_projected = attend_back_call(
        projected, after(grad_context, *moved), segments, stats, parts, 0
    )
    down.passed_got = after(down.passed_got, grad_projected)
    moved = down.hand_over()
    up.corner_got = after(up.corner_got, moved)
    moved = up.forward()
    down.home_in = after(down.home_in, moved)
    moved, down_sum = down.finish()
    grad_projected = attend_back_call(
        projected, after(grad_context, moved), segments, stats, parts, 1, grad_projected
    )
    last = Reduction([(rows_in, grad_projected), (attention_grad, context)], coords)
    sent = last.send()
    up.passed_got = after(up.passed_got, *sent)
    moved = up.hand_over()
    last.corner_in = after(last.corner_in, moved, up.kept_got)
    moved = last.spread()
    up.home_in = after(up.home_in, *moved)
    moved, up_sum = up.finish()
    input_grad = grad_one + dot_nt(after(grad_projected, moved), qkv_full)
    last.corner_got = after(last.corner_got, input_grad)
    moved = last.forward()
    grad_output, grad_two, grad_hidden, grad_one, grad_upper, grad_projected = after(
        (grad_output, grad_two, grad_hidden, grad_one, grad_upper, grad_projected), moved
    )
    gain_two_grad = jnp.sum(grad_output * normed_two, axis=0)
    shift_two_grad = jnp.sum(grad_output, axis=0)
    down_bias_grad = jnp.sum(grad_two, axis=0)
    gain_one_grad = jnp.sum(grad_hidden * normed_one, axis=0)
    shift_one_grad = jnp.sum(grad_hidden, axis=0)
    out_bias_grad = jnp.sum(grad_one, axis=0)
    upb_grad = jnp.sum(grad_upper.astype(jnp.float32), axis=0)
    qkv_sums = jnp.sum(grad_projected.astype(jnp.float32), axis=0)
    last.passed_got = after(
        last.passed_got,
        *(gain_two_grad, shift_two_grad, down_bias_grad, gain_one_grad),
        *(shift_one_grad, out_bias_grad, upb_grad, qkv_sums, last.kept_got),
    )
    moved = last.hand_over()
    moved, last_sum = last.finish()
    input_grads = own_rows(after(input_grad, moved))
    outputs = own_rows(after(result_low, moved))

    qkv_sums = qkv_sums.reshape(parts, 3, width_local)
    dp_order = (grid[2], grid[0], grid[1])
    qv_grads = jnp.stack([qkv_sums[:, 0], qkv_sums[:, 2]], axis=1)
    qv_grads = qv_grads.reshape((parts, 2, heads_local) + dp_order + (-1,))
    qv_grads = qv_grads.transpose(0, 4, 5, 3, 1, 2, 6).reshape(parts * dp_count, -1)
    upb_grad = upb_grad.reshape((parts,) + dp_order + (-1,))
    upb_grad = upb_grad.transpose(0, 2, 3, 1, 4).reshape(parts * dp_count, -1)

    def split_rows(rows):
        count = len(rows)
        rows = jnp.stack(rows).reshape((count,) + grid + (parts, -1))
        return rows.transpose(4, 1, 2, 3, 0, 5).reshape(parts * dp_count, -1)

    small_grad = jnp.concatenate(
        [
            qv_grads,
            upb_grad,
            split_rows([gain_one_grad, gain_two_grad]),
            split_rows([out_bias_grad, shift_one_grad, down_bias_grad, shift_two_grad]),
        ],
        axis=1,
    )
    small_grad = after(small_grad, moved)
    exchanged = lax.all_to_all(small_grad, EVERY, 0, 0, tiled=True)
    small_sum = jnp.sum(exchanged, axis=0)
    qv_sum, upb_sum, gains_sum, biases_sum = (
        small_sum[a : a + n] for a, n in zip(starts, sizes)
    )
    last_sum = last_sum.astype(jnp.float32)
    qkv_sum = last_sum[:, :wide].reshape(-1, 3, width_local).transpose(1, 0, 2)
    return (
        outputs,
        input_grads,
        qkv_sum,
        qv_sum.reshape(qv_bias.shape),
        last_sum[:, wide:].T,
        up_sum.astype(jnp.float32),
        upb_sum.reshape(up_bias.shape),
        down_sum.astype(jnp.float32).T,
        gains_sum.reshape(norm_gains.shape),
        biases_sum.reshape(row_biases.shape),
    )


def solution(mesh):
    groups = mesh.shape["dp"]
    parts = mesh.shape["tensor"]

    def program(*arrays):
        micro, width = arrays[0].shape[0], arrays[0].shape[2]
        fits = micro == 2 and parts == 2 and groups % 4 == 0 and width % (groups * 16) == 0
        if fits:
            dp, place = ("z", "x", "c"), "y"
            shape = (groups // 4, 2, 2, 2)
            used = Mesh(mesh.devices.reshape(shape), dp + (place,))
        else:
            dp, place, used = ("dp",), "tensor", mesh
        whole = dp + (place,)
        rows, vectors = P(None, whole, None), P(None, whole)
        weights = (
            P(None, dp, place),
            P(None, place, dp),
            P(place, dp),
            P(dp, place),
            P(place, dp),
            P(place, dp),
            vectors,
            vectors,
        )
        return jax.shard_map(
            sequence_parallel if fits else tensor_split,
            mesh=used,
            in_specs=(rows, P(None, dp)) + weights + (rows,),
            out_specs=(rows, rows) + weights,
            check_vma=False,
        )(*arrays)

    return program
```

```python
import functools

import jax
import jax.numpy as jnp
from jax import lax
from jax.experimental import pallas as pl
from jax.experimental.pallas import tpu as pltpu
from jax.sharding import Mesh
from jax.sharding import PartitionSpec as P

HEAD_DIM = 64


def gelu_exact(values):
    return jax.nn.gelu(values, approximate=False)


def normalize(rows, gain, shift):
    centered = rows - jnp.mean(rows, axis=-1, keepdims=True)
    variance = jnp.mean(centered * centered, axis=-1, keepdims=True)
    inverse = lax.rsqrt(variance + 1e-05)
    normed = centered * inverse
    return (normed * gain + shift, normed, inverse)


def norm_back(grad, normed, inverse, gain):
    scaled = grad * gain
    return inverse * (
        scaled
        - jnp.mean(scaled, axis=-1, keepdims=True)
        - normed * jnp.mean(scaled * normed, axis=-1, keepdims=True)
    )


def attend(query, keys, values, keep_mask, scale):
    scores = jnp.einsum("qhd,khd->hqk", query, keys, preferred_element_type=jnp.float32) * scale
    masked = jnp.where(keep_mask[None], scores, -1e30)
    highest = jnp.max(masked, axis=-1, keepdims=True)
    shifted = jnp.exp(masked - highest)
    totals = jnp.sum(shifted, axis=-1, keepdims=True)
    probs = (shifted / totals).astype(jnp.bfloat16)
    context = jnp.einsum("hqk,khd->qhd", probs, values, preferred_element_type=jnp.float32)
    return (context, highest + jnp.log(totals))


def attend_back(query, keys, values, keep_mask, logsumexp, grad_context, scale):
    scores = jnp.einsum("qhd,khd->hqk", query, keys, preferred_element_type=jnp.float32) * scale
    masked = jnp.where(keep_mask[None], scores, -1e30)
    probs = jnp.exp(masked - logsumexp)
    probs_low = probs.astype(jnp.bfloat16)
    grad_values = jnp.einsum(
        "hqk,qhd->khd", probs_low, grad_context, preferred_element_type=jnp.float32
    )
    grad_probs = jnp.einsum(
        "qhd,khd->hqk", grad_context, values, preferred_element_type=jnp.float32
    )
    grad_scores = probs * (grad_probs - jnp.sum(probs * grad_probs, axis=-1, keepdims=True))
    grad_low = grad_scores.astype(jnp.bfloat16)
    grad_query = (
        jnp.einsum("hqk,khd->qhd", grad_low, keys, preferred_element_type=jnp.float32) * scale
    )
    grad_keys = (
        jnp.einsum("hqk,qhd->khd", grad_low, query, preferred_element_type=jnp.float32) * scale
    )
    return (grad_query, grad_keys, grad_values)


def tensor_split(
    layer_input,
    segment_ids,
    qkv_weight,
    qv_bias,
    out_weight,
    up_weight,
    up_bias,
    down_weight,
    norm_gains,
    row_biases,
    cotangent,
):
    gains_all, biases_all = (
        lax.all_gather(norm_gains, ("dp", "tensor"), axis=1, tiled=True),
        lax.all_gather(row_biases, ("dp", "tensor"), axis=1, tiled=True),
    )
    shards = (qkv_weight, qv_bias, out_weight, up_weight, up_bias, down_weight)
    dp_count = lax.axis_size("dp")
    seq_len = segment_ids.shape[1]
    heads_local = qv_bias.shape[1]
    width_local = heads_local * HEAD_DIM
    scale = HEAD_DIM ** (-0.5)

    def micro_step(carry, inputs):
        rows_in, segments, grad_rows = inputs
        qkv_full, qv_full, out_full, up_full, upb_full, down_full = (
            lax.all_gather(shards[0], "dp", axis=1, tiled=True),
            lax.all_gather(shards[1], "dp", axis=2, tiled=True),
            lax.all_gather(shards[2], "dp", axis=1, tiled=True),
            lax.all_gather(shards[3], "dp", axis=0, tiled=True),
            lax.all_gather(shards[4], "dp", axis=1, tiled=True),
            lax.all_gather(shards[5], "dp", axis=1, tiled=True),
        )
        gathered = lax.all_gather(rows_in, "tensor", axis=0, tiled=True)
        projected = jnp.einsum(
            "rd,kdc->krc", gathered, qkv_full, preferred_element_type=jnp.float32
        )
        bias_flat = qv_full.reshape(2, width_local).astype(jnp.float32)
        split = (seq_len, heads_local, HEAD_DIM)
        query = (projected[0] + bias_flat[0]).astype(jnp.bfloat16).reshape(split)
        keys = projected[1].astype(jnp.bfloat16).reshape(split)
        values = (projected[2] + bias_flat[1]).astype(jnp.bfloat16).reshape(split)
        keep_mask = segments[:, None] == segments[None, :]
        attended, logsumexp = attend(query, keys, values, keep_mask, scale)
        context = attended.reshape(seq_len, width_local).astype(jnp.bfloat16)
        attention = lax.psum_scatter(
            jnp.dot(context, out_full, preferred_element_type=jnp.float32).astype(jnp.bfloat16),
            "tensor",
            scatter_dimension=0,
            tiled=True,
        ).astype(jnp.float32)
        residual_one = rows_in.astype(jnp.float32) + attention + biases_all[0]
        hidden, normed_one, inverse_one = normalize(residual_one, gains_all[0], biases_all[1])
        hidden_rows = lax.all_gather(hidden.astype(jnp.bfloat16), "tensor", axis=0, tiled=True)
        upper = jnp.dot(
            hidden_rows, up_full, preferred_element_type=jnp.float32
        ) + upb_full.reshape(-1).astype(jnp.float32)
        activated = gelu_exact(upper).astype(jnp.bfloat16)
        branch = lax.psum_scatter(
            jnp.dot(activated, down_full, preferred_element_type=jnp.float32).astype(jnp.bfloat16),
            "tensor",
            scatter_dimension=0,
            tiled=True,
        ).astype(jnp.float32)
        residual_two = hidden + branch + biases_all[2]
        result, normed_two, inverse_two = normalize(residual_two, gains_all[1], biases_all[3])
        qkv_back, qv_back, out_back, up_back, upb_back, down_back = (
            lax.all_gather(shards[0], "dp", axis=1, tiled=True),
            lax.all_gather(shards[1], "dp", axis=2, tiled=True),
            lax.all_gather(shards[2], "dp", axis=1, tiled=True),
            lax.all_gather(shards[3], "dp", axis=0, tiled=True),
            lax.all_gather(shards[4], "dp", axis=1, tiled=True),
            lax.all_gather(shards[5], "dp", axis=1, tiled=True),
        )
        grad_output = grad_rows.astype(jnp.float32)
        gain_two_grad = jnp.sum(grad_output * normed_two, axis=0)
        shift_two_grad = jnp.sum(grad_output, axis=0)
        grad_two = norm_back(grad_output, normed_two, inverse_two, gains_all[1])
        down_bias_grad = jnp.sum(grad_two, axis=0)
        branch_rows = lax.all_gather(grad_two.astype(jnp.bfloat16), "tensor", axis=0, tiled=True)
        down_grad = jnp.einsum(
            "rf,rd->fd", activated, branch_rows, preferred_element_type=jnp.float32
        )
        grad_active = jnp.einsum(
            "rd,fd->rf", branch_rows, down_back, preferred_element_type=jnp.float32
        )
        gelu_pull = jax.vjp(gelu_exact, upper)[1]
        grad_upper = gelu_pull(grad_active)[0].astype(jnp.bfloat16)
        up_bias_grad = jnp.sum(grad_upper.astype(jnp.float32), axis=0).reshape(1, -1)
        up_grad = jnp.einsum(
            "rd,rf->df", hidden_rows, grad_upper, preferred_element_type=jnp.float32
        )
        grad_hidden = grad_two + lax.psum_scatter(
            jnp.einsum("rf,df->rd", grad_upper, up_back, preferred_element_type=jnp.float32).astype(
                jnp.bfloat16
            ),
            "tensor",
            scatter_dimension=0,
            tiled=True,
        ).astype(jnp.float32)
        gain_one_grad = jnp.sum(grad_hidden * normed_one, axis=0)
        shift_one_grad = jnp.sum(grad_hidden, axis=0)
        grad_one = norm_back(grad_hidden, normed_one, inverse_one, gains_all[0])
        out_bias_grad = jnp.sum(grad_one, axis=0)
        attention_rows = lax.all_gather(grad_one.astype(jnp.bfloat16), "tensor", axis=0, tiled=True)
        out_grad = jnp.einsum(
            "rc,rd->cd", context, attention_rows, preferred_element_type=jnp.float32
        )
        grad_context = (
            jnp.einsum("rd,cd->rc", attention_rows, out_back, preferred_element_type=jnp.float32)
            .astype(jnp.bfloat16)
            .reshape(split)
        )
        grad_query, grad_keys, grad_values = attend_back(
            query, keys, values, keep_mask, logsumexp, grad_context, scale
        )
        grad_qkv = (
            jnp.stack([grad_query, grad_keys, grad_values])
            .reshape(3, seq_len, width_local)
            .astype(jnp.bfloat16)
        )
        bias_sums = jnp.sum(jnp.stack([grad_qkv[0], grad_qkv[2]]).astype(jnp.float32), axis=1)
        qv_grad = bias_sums.reshape(2, heads_local, HEAD_DIM)
        qkv_grad = jnp.einsum("rd,krc->kdc", gathered, grad_qkv, preferred_element_type=jnp.float32)
        input_grad = (
            grad_one
            + lax.psum_scatter(
                jnp.einsum(
                    "krc,kdc->rd", grad_qkv, qkv_back, preferred_element_type=jnp.float32
                ).astype(jnp.bfloat16),
                "tensor",
                scatter_dimension=0,
                tiled=True,
            ).astype(jnp.float32)
        ).astype(jnp.bfloat16)
        gains_grad = jnp.stack([gain_one_grad, gain_two_grad])
        biases_grad = jnp.stack([out_bias_grad, shift_one_grad, down_bias_grad, shift_two_grad])
        updates = (
            qkv_grad,
            qv_grad,
            out_grad,
            up_grad,
            up_bias_grad,
            down_grad,
            gains_grad,
            biases_grad,
        )
        carry = tuple((total + update for total, update in zip(carry, updates)))
        return (carry, (result.astype(jnp.bfloat16), input_grad))

    initial = (
        jnp.zeros((3, qkv_weight.shape[1] * dp_count, qkv_weight.shape[2]), jnp.float32),
        jnp.zeros((2, qv_bias.shape[1], qv_bias.shape[2] * dp_count), jnp.float32),
        jnp.zeros((out_weight.shape[0], out_weight.shape[1] * dp_count), jnp.float32),
        jnp.zeros((up_weight.shape[0] * dp_count, up_weight.shape[1]), jnp.float32),
        jnp.zeros((1, up_bias.shape[1] * dp_count), jnp.float32),
        jnp.zeros((down_weight.shape[0], down_weight.shape[1] * dp_count), jnp.float32),
        jnp.zeros(gains_all.shape, jnp.float32),
        jnp.zeros(biases_all.shape, jnp.float32),
    )
    totals, (outputs, input_grads) = lax.scan(
        micro_step, initial, (layer_input, segment_ids, cotangent)
    )
    qkv_sum, qv_sum, out_sum, up_sum, upb_sum, down_sum = (
        lax.psum_scatter(
            totals[0].astype(jnp.bfloat16), "dp", scatter_dimension=1, tiled=True
        ).astype(jnp.float32),
        lax.psum_scatter(
            totals[1].astype(jnp.bfloat16), "dp", scatter_dimension=2, tiled=True
        ).astype(jnp.float32),
        lax.psum_scatter(
            totals[2].astype(jnp.bfloat16), "dp", scatter_dimension=1, tiled=True
        ).astype(jnp.float32),
        lax.psum_scatter(
            totals[3].astype(jnp.bfloat16), "dp", scatter_dimension=0, tiled=True
        ).astype(jnp.float32),
        lax.psum_scatter(
            totals[4].astype(jnp.bfloat16), "dp", scatter_dimension=1, tiled=True
        ).astype(jnp.float32),
        lax.psum_scatter(
            totals[5].astype(jnp.bfloat16), "dp", scatter_dimension=1, tiled=True
        ).astype(jnp.float32),
    )
    gains_sum, biases_sum = (
        lax.psum_scatter(totals[6], ("dp", "tensor"), scatter_dimension=1, tiled=True),
        lax.psum_scatter(totals[7], ("dp", "tensor"), scatter_dimension=1, tiled=True),
    )
    return (
        outputs,
        input_grads,
        qkv_sum,
        qv_sum,
        out_sum,
        up_sum,
        upb_sum,
        down_sum,
        gains_sum,
        biases_sum,
    )


NEGATIVE = -1e30
LANES = 2 * HEAD_DIM


def half_mask(shape, half):
    lane = lax.broadcasted_iota(jnp.int32, shape, 1)
    return (lane // HEAD_DIM) == half


def attend_kernel(q_ref, k_ref, v_ref, row_ref, col_ref, context_ref, stats_ref):
    query, keys, values = q_ref[...], k_ref[...], v_ref[...]
    keep = col_ref[...] == row_ref[...]
    total = jnp.zeros(context_ref.shape, jnp.float32)
    for half in range(2):
        own = half_mask(query.shape, half)
        masked_query = jnp.where(own, query, 0) * jnp.asarray(HEAD_DIM**-0.5, query.dtype)
        scores = lax.dot_general(
            keys, masked_query, (((1,), (1,)), ((), ())), preferred_element_type=jnp.float32
        )
        scores = jnp.where(keep, scores, NEGATIVE)
        highest = jnp.max(scores, axis=0, keepdims=True)
        shifted = jnp.exp(scores - highest)
        sums = jnp.sum(shifted, axis=0, keepdims=True)
        probs = (shifted * (1.0 / sums)).astype(jnp.bfloat16)
        own_values = jnp.where(own, values, 0)
        total += lax.dot_general(
            probs, own_values, (((0,), (0,)), ((), ())), preferred_element_type=jnp.float32
        )
        stats_ref[0, half : half + 1, :] = highest + jnp.log(sums)
    context_ref[...] = total.astype(context_ref.dtype)


def attend_back_kernel(
    q_ref, k_ref, v_ref, grad_ref, row_ref, col_ref, stats_ref, *rest
):
    query, keys, values, grad = q_ref[...], k_ref[...], v_ref[...], grad_ref[...]
    scale = jnp.asarray(HEAD_DIM**-0.5, query.dtype)
    keep = col_ref[...] == row_ref[...]
    zero = jnp.zeros(query.shape, jnp.float32)
    grad_query, grad_keys, grad_values = zero, zero, zero
    for half in range(2):
        own = half_mask(query.shape, half)
        own_query = jnp.where(own, query, 0) * scale
        own_keys = jnp.where(own, keys, 0) * scale
        own_grad = jnp.where(own, grad, 0)
        contract_last = (((1,), (1,)), ((), ()))
        scores = lax.dot_general(
            keys, own_query, contract_last, preferred_element_type=jnp.float32
        )
        scores = jnp.where(keep, scores, NEGATIVE)
        probs = jnp.exp(scores - stats_ref[0, half : half + 1, :])
        grad_values += jnp.dot(
            probs.astype(jnp.bfloat16), own_grad, preferred_element_type=jnp.float32
        )
        grad_probs = lax.dot_general(
            values, own_grad, contract_last, preferred_element_type=jnp.float32
        )
        weighted = probs * grad_probs
        grad_scores = (weighted - probs * jnp.sum(weighted, axis=0, keepdims=True)).astype(
            jnp.bfloat16
        )
        grad_keys += jnp.dot(grad_scores, own_query, preferred_element_type=jnp.float32)
        grad_query += lax.dot_general(
            grad_scores, own_keys, (((0,), (0,)), ((), ())), preferred_element_type=jnp.float32
        )
    pair, out_ref = pl.program_id(0), rest[-1]
    width = out_ref.shape[1] // 3
    for place, value in enumerate((grad_query, grad_keys, grad_values)):
        start = pl.multiple_of(place * width + pair * LANES, LANES)
        out_ref[:, pl.ds(start, LANES)] = value.astype(out_ref.dtype)


def attention_specs(rows, pairs, parts):
    inner = pairs // parts

    def column(place):
        return pl.BlockSpec(
            (rows, LANES),
            lambda i: (0, (i // inner) * (3 * inner) + place * inner + lax.rem(i, inner)),
        )

    plain = pl.BlockSpec((rows, LANES), lambda i: (0, i))
    row_ids = pl.BlockSpec((1, rows), lambda i: (0, 0))
    column_ids = pl.BlockSpec((rows, 1), lambda i: (0, 0))
    stats = pl.BlockSpec((1, 2, rows), lambda i: (i, 0, 0))
    return [column(place) for place in range(3)], plain, [row_ids, column_ids], stats


def attend_call(projected, segments, parts):
    rows, width = projected.shape[0], projected.shape[1] // 3
    pairs = width // LANES
    columns, plain, ids, stats = attention_specs(rows, pairs, parts)
    return pl.pallas_call(
        attend_kernel,
        grid=(pairs,),
        in_specs=columns + ids,
        out_specs=[plain, stats],
        out_shape=[
            jax.ShapeDtypeStruct((rows, width), jnp.bfloat16),
            jax.ShapeDtypeStruct((pairs, 2, rows), jnp.float32),
        ],
        compiler_params=pltpu.CompilerParams(vmem_limit_bytes=14 * 1024 * 1024),
        cost_estimate=pl.CostEstimate(
            flops=16 * pairs * rows * rows * LANES,
            bytes_accessed=8 * rows * width,
            transcendentals=2 * pairs * rows * rows,
        ),
        name="attend",
    )(projected, projected, projected, segments[None, :], segments[:, None])


def attend_back_call(projected, grad, segments, stats_in, parts, part, others=None):
    rows, width = grad.shape
    inner = width // LANES // parts

    def column(place):
        return pl.BlockSpec(
            (rows, LANES), lambda i: (0, part * (3 * inner) + place * inner + i)
        )

    ids = [pl.BlockSpec((1, rows), lambda i: (0, 0)), pl.BlockSpec((rows, 1), lambda i: (0, 0))]
    stats = pl.BlockSpec((1, 2, rows), lambda i: (part * inner + i, 0, 0))
    plain = pl.BlockSpec((rows, LANES), lambda i: (0, part * inner + i))
    rest = [] if others is None else [others]
    return pl.pallas_call(
        attend_back_kernel,
        grid=(inner,),
        in_specs=[column(place) for place in range(3)]
        + [plain]
        + ids
        + [stats]
        + [pl.BlockSpec(memory_space=pl.ANY)] * len(rest),
        out_specs=pl.BlockSpec((rows, 3 * width // parts), lambda i: (0, part)),
        out_shape=jax.ShapeDtypeStruct((rows, 3 * width), jnp.bfloat16),
        input_output_aliases={7: 0} if rest else {},
        compiler_params=pltpu.CompilerParams(vmem_limit_bytes=14 * 1024 * 1024),
        cost_estimate=pl.CostEstimate(
            flops=40 * inner * rows * rows * LANES,
            bytes_accessed=14 * rows * width // parts,
            transcendentals=2 * inner * rows * rows,
        ),
        name="attend_back",
    )(
        projected,
        projected,
        projected,
        grad,
        segments[None, :],
        segments[:, None],
        stats_in,
        *rest,
    )


def dot_nn(a, b):
    return jnp.dot(a, b, preferred_element_type=jnp.float32)


def dot_nt(a, b):
    return lax.dot_general(a, b, (((1,), (1,)), ((), ())), preferred_element_type=jnp.float32)


def dot_tn(a, b):
    return lax.dot_general(a, b, (((0,), (0,)), ((), ())), preferred_element_type=jnp.float32)


def gelu_pair(values):
    cdf = 0.5 * (1.0 + lax.erf(values * (0.5**0.5)))
    density = jnp.exp(-0.5 * values * values) * (0.5 / jnp.pi) ** 0.5
    return values * cdf, cdf + values * density


PLANE = ("x", "c", "y")
EVERY = ("y", "x", "c", "z")
SWAP = [(0, 1), (1, 0)]


def plane_permutes():
    def index(x, c, y):
        return (x * 2 + c) * 2 + y

    cells = [(x, y) for x in range(2) for y in range(2)]
    along = [(index(x, 0, y), index(1 - x, 0, y)) for x, y in cells]
    along += [(index(x, 1, y), index(x, 1, 1 - y)) for x, y in cells]
    cross = [(index(x, 0, y), index(1 - x, 1, y)) for x, y in cells]
    cross += [(index(x, 1, y), index(x, 0, 1 - y)) for x, y in cells]
    return along, cross, [(target, source) for source, target in cross]


def after(value, *done):
    return lax.optimization_barrier((value,) + done)[0]


def barrier(*values):
    return lax.optimization_barrier(values)


def place_kernel(table_ref, *refs, widths):
    pieces = refs[:8]
    outs, held, arrived, left = refs[8:-3], refs[-3], refs[-2], refs[-1]
    loads, stores = [], []
    for i, piece in enumerate(pieces):
        loads.append(pltpu.make_async_copy(piece, held.at[i], arrived.at[i]))
        loads[-1].start()
    for i, piece in enumerate(pieces):
        size, start = piece.shape[0], 0
        row = pl.multiple_of(table_ref[i] * size, size)
        loads[i].wait()
        for j, (out, width) in enumerate(zip(outs, widths)):
            column = pl.multiple_of(table_ref[8 + i] * width, width)
            stores.append(
                pltpu.make_async_copy(
                    held.at[i, :, pl.ds(start, width)],
                    out.at[pl.ds(row, size), pl.ds(column, width)],
                    left.at[i, j],
                )
            )
            stores[-1].start()
            start += width
    for store in stores:
        store.wait()


def place(pieces, table, widths):
    size = pieces[0].shape[0]
    anywhere = pl.BlockSpec(memory_space=pl.ANY)
    return pl.pallas_call(
        functools.partial(place_kernel, widths=widths),
        grid_spec=pltpu.PrefetchScalarGridSpec(
            num_scalar_prefetch=1,
            grid=(1,),
            in_specs=[anywhere] * 8,
            out_specs=[anywhere] * len(widths),
            scratch_shapes=[
                pltpu.VMEM((8, size, sum(widths)), jnp.bfloat16),
                pltpu.SemaphoreType.DMA((8,)),
                pltpu.SemaphoreType.DMA((8, len(widths))),
            ],
        ),
        out_shape=[jax.ShapeDtypeStruct((4 * size, 2 * w), jnp.bfloat16) for w in widths],
        compiler_params=pltpu.CompilerParams(vmem_limit_bytes=16 * 1024 * 1024),
        cost_estimate=pl.CostEstimate(
            flops=0, bytes_accessed=32 * size * sum(widths), transcendentals=0
        ),
        name="place",
    )(table, *pieces)


def plane_spots(core, x, y):
    main = jnp.where(core == 0, 2 - 2 * x, 2 * x)
    part = jnp.where(core == 0, y, 1 - y)
    rows = [2 * x + core, main + core, main + 1 - core, 3 - 2 * x - core]
    return rows, [y, part, part, 1 - y]


def gather_weight(pieces, coords, widths):
    x, c, y, _ = coords
    pieces = pieces + [lax.ppermute(item, "c", SWAP) for item in pieces[2:]]
    (rows, parts), (partner_rows, partner_parts) = (plane_spots(k, x, y) for k in (c, 1 - c))
    order = [rows[0], partner_rows[0]] + rows[1:] + partner_rows[1:]
    order += [parts[0], partner_parts[0]] + parts[1:] + partner_parts[1:]
    return place(pieces, jnp.stack(order).astype(jnp.int32), widths)


def pack_kernel(qkv_ref, out_ref, tile_ref, packed_ref):
    count, _, width = qkv_ref.shape
    for i in range(count):
        packed_ref[:, i * width : (i + 1) * width] = qkv_ref[i]
    start = count * width
    packed_ref[:, start : start + width] = out_ref[...]
    packed_ref[:, start + width :] = tile_ref[...]


def pack(qkv, out, tile):
    count, rows, width = qkv.shape
    shape = (rows, (count + 1) * width + tile.shape[1])
    return pl.pallas_call(
        pack_kernel,
        out_shape=jax.ShapeDtypeStruct(shape, qkv.dtype),
        cost_estimate=pl.CostEstimate(
            flops=0, bytes_accessed=4 * shape[0] * shape[1], transcendentals=0
        ),
        name="pack",
    )(qkv, out, tile)


def three_parts(values, rows):
    parts = []
    for _ in range(3):
        parts.append(lax.reduce_precision(values, exponent_bits=8, mantissa_bits=7))
        values = values - parts[-1]
    tile = jnp.concatenate(parts).astype(jnp.bfloat16).reshape(-1, LANES)
    return jnp.pad(tile, ((0, rows - tile.shape[0]), (0, 0)))


class Reduction:
    def __init__(self, pairs, coords):
        self.pairs = pairs
        self.x, self.c, self.y, _ = coords
        self.along, self.cross, _ = plane_permutes()
        x, c, y = self.x, self.c, self.y
        self.main_row = jnp.where(c == 0, 2 - 2 * x, 2 * x)
        self.main_part = jnp.where(c == 0, y, 1 - y)
        self.partner_row = jnp.where(c == 0, 2 * x, 2 - 2 * x)
        self.partner_part = 1 - self.main_part

    def block(self, row, count, part, extras=()):
        pieces, start = [], 0
        pairs, extras = barrier(self.pairs, list(extras))
        for left, right in pairs:
            size, width = left.shape[1] // 4, right.shape[1] // 2
            picked = lax.dynamic_slice_in_dim(left, row * size, count * size, 1)
            total = dot_tn(picked, lax.dynamic_slice_in_dim(right, part * width, width, 1))
            for extra, at in extras:
                if at is not None:
                    extra = lax.dynamic_slice_in_dim(extra, at * size, count * size, 0)
                total = total + extra[:, start : start + width].astype(jnp.float32)
            pieces.append(total.astype(jnp.bfloat16))
            start += width
        return pieces[0] if len(pieces) == 1 else jnp.concatenate(pieces, axis=1)

    def send(self):
        corner = self.block(3 - 2 * self.x - self.c, 1, 1 - self.y)
        main = self.block(self.partner_row, 2, self.partner_part)
        self.corner_in = lax.ppermute(corner, "c", SWAP)
        self.main_in = lax.ppermute(main, "c", SWAP)
        return corner, main

    def spread(self):
        x, c, y = self.x, self.c, self.y
        corner = self.block(2 - 2 * x + c, 1, 1 - y, [(self.corner_in, None)])
        self.corner_got = lax.ppermute(corner, PLANE, self.cross)
        main = self.block(self.main_row + c, 1, self.main_part, [(self.main_in, c)])
        self.kept_got = lax.ppermute(main, PLANE, self.along)
        return corner, main

    def forward(self):
        extras = [(self.main_in, 1 - self.c), (self.corner_got, None)]
        main = self.block(self.main_row + 1 - self.c, 1, self.main_part, extras)
        self.passed_got = lax.ppermute(main, PLANE, self.along)
        return main

    def hand_over(self):
        home = self.block(2 * self.x + 1 - self.c, 1, self.y, [(self.passed_got, None)])
        self.home_in = lax.ppermute(home, "c", SWAP)
        return home

    def finish(self):
        home = self.block(2 * self.x + self.c, 1, self.y, [(self.kept_got, None), (self.home_in, None)])
        return home, lax.psum_scatter(home, "z", scatter_dimension=0, tiled=True)


def sequence_parallel(
    layer_input,
    segment_ids,
    qkv_weight,
    qv_bias,
    out_weight,
    up_weight,
    up_bias,
    down_weight,
    norm_gains,
    row_biases,
    cotangent,
):
    low = jnp.bfloat16
    parts = lax.axis_size("y")
    grid = tuple(lax.axis_size(name) for name in ("x", "c", "z"))
    dp_count = grid[0] * grid[1] * grid[2]
    mine = lax.axis_index("y")
    coords = tuple(lax.axis_index(name) for name in ("x", "c", "y", "z"))
    half, width = layer_input.shape[1:]
    heads_local = qv_bias.shape[1]
    width_local = heads_local * HEAD_DIM
    hidden_local = up_weight.shape[1]
    wide = 3 * width_local
    span = range(parts)

    source = jnp.arange(width).reshape(grid[2], grid[0], grid[1], -1)
    source = source.transpose(1, 2, 0, 3).reshape(-1)
    chosen = lax.broadcasted_iota(jnp.int32, (width, width), 0) == source[None, :]
    order = chosen.astype(low)

    def own_sequence(rows):
        kept = lax.dynamic_index_in_dim(rows, mine, 0, keepdims=False)
        sent = lax.dynamic_index_in_dim(rows, 1 - mine, 0, keepdims=False)
        return jnp.concatenate([kept, lax.ppermute(sent, "y", SWAP)], axis=0)

    def own_rows(rows):
        rows = dot_nt(rows.astype(low), order).astype(low)
        received = lax.ppermute(rows[half:], "y", SWAP)
        first = jnp.where(mine == 0, rows[:half], received)
        second = jnp.where(mine == 0, received, rows[:half])
        return jnp.stack([first, second])

    small = jnp.concatenate(
        [
            qv_bias.astype(jnp.float32).reshape(-1),
            up_bias.astype(jnp.float32).reshape(-1),
            norm_gains.reshape(-1),
            row_biases.reshape(-1),
        ]
    )
    packed = pack(qkv_weight, out_weight.T, three_parts(small, up_weight.shape[0]))

    def lane_of(piece):
        return lax.all_gather(piece, "z", axis=0, tiled=True)

    along, _, back = plane_permutes()

    def start_plane(lane):
        other = lax.ppermute(lane, "c", SWAP)
        main_other = lax.ppermute(other, PLANE, along)
        return [lane, other, lax.ppermute(lane, PLANE, along), main_other]

    lane = lane_of(packed)
    lane_up = lane_of(after(up_weight, packed))
    lane_down = lane_of(after(down_weight.T, packed))
    layer_input, cotangent = after((layer_input, cotangent), packed)
    rows_in, grad_output = own_sequence(layer_input), own_sequence(cotangent)
    lane, rows_in, grad_output = barrier(lane, rows_in, grad_output)
    pieces = start_plane(lane)
    rows_in, grad_output = after((rows_in, grad_output), pieces[1])
    rows_in, grad_output = (dot_nn(item, order).astype(low) for item in (rows_in, grad_output))
    pieces[2], pieces[3], rows_in, grad_output = barrier(
        pieces[2], pieces[3], rows_in, grad_output
    )
    pieces.append(lax.ppermute(pieces[2], PLANE, back))
    up_pieces = start_plane(after(lane_up, pieces[2]))
    pieces[4], up_pieces[1] = barrier(pieces[4], up_pieces[1])
    qkv_full, out_full, small_all = gather_weight(pieces, coords, (wide, width_local, LANES))
    segments = lax.dynamic_index_in_dim(segment_ids, mine, 0, keepdims=False)
    segments = jnp.where(mine == 0, segments, jnp.roll(segments, -half))

    small_all = small_all.reshape(grid + (-1, parts, LANES))[:, :, :, : 3 * small.size // LANES]
    small_all = small_all.astype(jnp.float32).transpose(4, 0, 1, 2, 3, 5)
    small_all = small_all.reshape((parts,) + grid + (3, small.size))
    small_all = small_all[..., 0, :] + small_all[..., 1, :] + small_all[..., 2, :]
    sizes = [qv_bias.size, up_bias.size, norm_gains.size, row_biases.size]
    starts = [0, sizes[0], sum(sizes[:2]), sum(sizes[:3])]

    def section(i, shard):
        values = small_all[..., starts[i] : starts[i] + sizes[i]]
        return values.reshape((parts,) + grid + shard.shape)

    qv_all = section(0, qv_bias).transpose(4, 0, 5, 3, 1, 2, 6).reshape(2, parts, width_local)
    upb_all = section(1, up_bias).transpose(0, 3, 1, 2, 4, 5).reshape(-1)

    def whole_rows(i, shard):
        values = section(i, shard).transpose(4, 1, 2, 3, 0, 5)
        return values.reshape(shard.shape[0], width)

    gains_all, biases_all = whole_rows(2, norm_gains), whole_rows(3, row_biases)
    none = jnp.zeros((width_local,), jnp.float32)
    qkv_bias = jnp.concatenate(
        [item for t in span for item in (qv_all[0, t], none, qv_all[1, t])]
    )

    up_pieces[2], qkv_full = barrier(up_pieces[2], qkv_full)
    projected = (dot_nn(rows_in, qkv_full) + qkv_bias).astype(low)
    up_pieces[3], projected = barrier(up_pieces[3], projected)
    up_pieces.append(lax.ppermute(after(up_pieces[2], projected), PLANE, back))
    down_pieces = start_plane(after(lane_down, projected))
    context, stats = attend_call(after(projected, down_pieces[1]), segments, parts)
    down_pieces[2], down_pieces[3], up_pieces[4], context = barrier(
        down_pieces[2], down_pieces[3], up_pieces[4], context
    )
    down_pieces.append(lax.ppermute(down_pieces[2], PLANE, back))
    attention = dot_nt(context, out_full)
    residual_one = rows_in.astype(jnp.float32) + attention + biases_all[0]
    hidden, normed_one, inverse_one = normalize(residual_one, gains_all[0], biases_all[1])
    hidden_low = hidden.astype(low)
    (up_full,) = gather_weight(up_pieces, coords, (hidden_local,))
    activated, slope = gelu_pair(
        dot_nn(hidden_low, up_full) + upb_all
    )
    activated, slope = activated.astype(low), slope.astype(low)
    down_pieces[4], activated = barrier(down_pieces[4], activated)
    (down_full,) = gather_weight(down_pieces, coords, (hidden_local,))
    branch = dot_nt(activated, down_full)
    residual_two = hidden + branch + biases_all[2]
    result, normed_two, inverse_two = normalize(residual_two, gains_all[1], biases_all[3])

    result_low = barrier(result.astype(low))[0]
    grad_output = grad_output.astype(jnp.float32)
    grad_two = norm_back(grad_output, normed_two, inverse_two, gains_all[1])
    branch_grad = grad_two.astype(low)

    down = Reduction([(branch_grad, activated)], coords)
    sent = down.send()
    columns = [slice(t * hidden_local, (t + 1) * hidden_local) for t in span]
    branch_late = after(branch_grad, *sent)
    grad_first = (dot_nn(branch_late, down_full[:, columns[0]]) * slope[:, columns[0]]).astype(low)
    down.corner_in = after(down.corner_in, grad_first)
    moved = down.spread()
    branch_late = after(branch_grad, *moved)
    grad_second = (dot_nn(branch_late, down_full[:, columns[1]]) * slope[:, columns[1]]).astype(low)
    grad_upper = jnp.concatenate([grad_first, grad_second], axis=1)
    up = Reduction([(hidden_low, grad_upper)], coords)
    sent = up.send()
    down.corner_got = after(down.corner_got, *sent)
    moved = down.forward()
    grad_hidden = grad_two + dot_nt(after(grad_upper, moved), up_full)
    grad_one = norm_back(grad_hidden, normed_one, inverse_one, gains_all[0])
    attention_grad = grad_one.astype(low)
    grad_context = dot_nn(attention_grad, out_full).astype(low)
    up.corner_in = after(up.corner_in, grad_context, down.kept_got)
    moved = up.spread()
    grad_projected = attend_back_call(
        projected, after(grad_context, *moved), segments, stats, parts, 0
    )
    down.passed_got = after(down.passed_got, grad_projected)
    moved = down.hand_over()
    up.corner_got = after(up.corner_got, moved)
    moved = up.forward()
    down.home_in = after(down.home_in, moved)
    moved, down_sum = down.finish()
    grad_projected = attend_back_call(
        projected, after(grad_context, moved), segments, stats, parts, 1, grad_projected
    )
    last = Reduction([(rows_in, grad_projected), (attention_grad, context)], coords)
    sent = last.send()
    up.passed_got = after(up.passed_got, *sent)
    moved = up.hand_over()
    last.corner_in = after(last.corner_in, moved, up.kept_got)
    moved = last.spread()
    up.home_in = after(up.home_in, *moved)
    moved, up_sum = up.finish()
    input_grad = grad_one + dot_nt(after(grad_projected, moved), qkv_full)
    last.corner_got = after(last.corner_got, input_grad)
    moved = last.forward()
    grad_output, grad_two, grad_hidden, grad_one, grad_upper, grad_projected = after(
        (grad_output, grad_two, grad_hidden, grad_one, grad_upper, grad_projected), moved
    )
    gain_two_grad = jnp.sum(grad_output * normed_two, axis=0)
    shift_two_grad = jnp.sum(grad_output, axis=0)
    down_bias_grad = jnp.sum(grad_two, axis=0)
    gain_one_grad = jnp.sum(grad_hidden * normed_one, axis=0)
    shift_one_grad = jnp.sum(grad_hidden, axis=0)
    out_bias_grad = jnp.sum(grad_one, axis=0)
    upb_grad = jnp.sum(grad_upper.astype(jnp.float32), axis=0)
    qkv_sums = jnp.sum(grad_projected.astype(jnp.float32), axis=0)
    last.passed_got = after(
        last.passed_got,
        *(gain_two_grad, shift_two_grad, down_bias_grad, gain_one_grad),
        *(shift_one_grad, out_bias_grad, upb_grad, qkv_sums, last.kept_got),
    )
    moved = last.hand_over()
    moved, last_sum = last.finish()
    input_grads = own_rows(after(input_grad, moved))
    outputs = own_rows(after(result_low, moved))

    qkv_sums = qkv_sums.reshape(parts, 3, width_local)
    dp_order = (grid[2], grid[0], grid[1])
    qv_grads = jnp.stack([qkv_sums[:, 0], qkv_sums[:, 2]], axis=1)
    qv_grads = qv_grads.reshape((parts, 2, heads_local) + dp_order + (-1,))
    qv_grads = qv_grads.transpose(0, 4, 5, 3, 1, 2, 6).reshape(parts * dp_count, -1)
    upb_grad = upb_grad.reshape((parts,) + dp_order + (-1,))
    upb_grad = upb_grad.transpose(0, 2, 3, 1, 4).reshape(parts * dp_count, -1)

    def split_rows(rows):
        count = len(rows)
        rows = jnp.stack(rows).reshape((count,) + grid + (parts, -1))
        return rows.transpose(4, 1, 2, 3, 0, 5).reshape(parts * dp_count, -1)

    small_grad = jnp.concatenate(
        [
            qv_grads,
            upb_grad,
            split_rows([gain_one_grad, gain_two_grad]),
            split_rows([out_bias_grad, shift_one_grad, down_bias_grad, shift_two_grad]),
        ],
        axis=1,
    )
    small_grad = after(small_grad, moved)
    exchanged = lax.all_to_all(small_grad, EVERY, 0, 0, tiled=True)
    small_sum = jnp.sum(exchanged, axis=0)
    qv_sum, upb_sum, gains_sum, biases_sum = (
        small_sum[a : a + n] for a, n in zip(starts, sizes)
    )
    last_sum = last_sum.astype(jnp.float32)
    qkv_sum = last_sum[:, :wide].reshape(-1, 3, width_local).transpose(1, 0, 2)
    return (
        outputs,
        input_grads,
        qkv_sum,
        qv_sum.reshape(qv_bias.shape),
        last_sum[:, wide:].T,
        up_sum.astype(jnp.float32),
        upb_sum.reshape(up_bias.shape),
        down_sum.astype(jnp.float32).T,
        gains_sum.reshape(norm_gains.shape),
        biases_sum.reshape(row_biases.shape),
    )


def solution(mesh):
    groups = mesh.shape["dp"]
    parts = mesh.shape["tensor"]

    def program(*arrays):
        micro, width = arrays[0].shape[0], arrays[0].shape[2]
        fits = micro == 2 and parts == 2 and groups % 4 == 0 and width % (groups * 16) == 0
        if fits:
            dp, place = ("z", "x", "c"), "y"
            shape = (groups // 4, 2, 2, 2)
            used = Mesh(mesh.devices.reshape(shape), dp + (place,))
        else:
            dp, place, used = ("dp",), "tensor", mesh
        whole = dp + (place,)
        rows, vectors = P(None, whole, None), P(None, whole)
        weights = (
            P(None, dp, place),
            P(None, place, dp),
            P(place, dp),
            P(dp, place),
            P(place, dp),
            P(place, dp),
            vectors,
            vectors,
        )
        return jax.shard_map(
            sequence_parallel if fits else tensor_split,
            mesh=used,
            in_specs=(rows, P(None, dp)) + weights + (rows,),
            out_specs=(rows, rows) + weights,
            check_vma=False,
        )(*arrays)

    return program
```

```python
import functools

import jax
import jax.numpy as jnp
from jax import lax
from jax.experimental import pallas as pl
from jax.experimental.pallas import tpu as pltpu
from jax.sharding import Mesh
from jax.sharding import PartitionSpec as P

HEAD_DIM = 64


def gelu_exact(values):
    return jax.nn.gelu(values, approximate=False)


def normalize(rows, gain, shift):
    centered = rows - jnp.mean(rows, axis=-1, keepdims=True)
    variance = jnp.mean(centered * centered, axis=-1, keepdims=True)
    inverse = lax.rsqrt(variance + 1e-05)
    normed = centered * inverse
    return (normed * gain + shift, normed, inverse)


def norm_back(grad, normed, inverse, gain):
    scaled = grad * gain
    return inverse * (
        scaled
        - jnp.mean(scaled, axis=-1, keepdims=True)
        - normed * jnp.mean(scaled * normed, axis=-1, keepdims=True)
    )


def attend(query, keys, values, keep_mask, scale):
    scores = jnp.einsum("qhd,khd->hqk", query, keys, preferred_element_type=jnp.float32) * scale
    masked = jnp.where(keep_mask[None], scores, -1e30)
    highest = jnp.max(masked, axis=-1, keepdims=True)
    shifted = jnp.exp(masked - highest)
    totals = jnp.sum(shifted, axis=-1, keepdims=True)
    probs = (shifted / totals).astype(jnp.bfloat16)
    context = jnp.einsum("hqk,khd->qhd", probs, values, preferred_element_type=jnp.float32)
    return (context, highest + jnp.log(totals))


def attend_back(query, keys, values, keep_mask, logsumexp, grad_context, scale):
    scores = jnp.einsum("qhd,khd->hqk", query, keys, preferred_element_type=jnp.float32) * scale
    masked = jnp.where(keep_mask[None], scores, -1e30)
    probs = jnp.exp(masked - logsumexp)
    probs_low = probs.astype(jnp.bfloat16)
    grad_values = jnp.einsum(
        "hqk,qhd->khd", probs_low, grad_context, preferred_element_type=jnp.float32
    )
    grad_probs = jnp.einsum(
        "qhd,khd->hqk", grad_context, values, preferred_element_type=jnp.float32
    )
    grad_scores = probs * (grad_probs - jnp.sum(probs * grad_probs, axis=-1, keepdims=True))
    grad_low = grad_scores.astype(jnp.bfloat16)
    grad_query = (
        jnp.einsum("hqk,khd->qhd", grad_low, keys, preferred_element_type=jnp.float32) * scale
    )
    grad_keys = (
        jnp.einsum("hqk,qhd->khd", grad_low, query, preferred_element_type=jnp.float32) * scale
    )
    return (grad_query, grad_keys, grad_values)


def tensor_split(
    layer_input,
    segment_ids,
    qkv_weight,
    qv_bias,
    out_weight,
    up_weight,
    up_bias,
    down_weight,
    norm_gains,
    row_biases,
    cotangent,
):
    gains_all, biases_all = (
        lax.all_gather(norm_gains, ("dp", "tensor"), axis=1, tiled=True),
        lax.all_gather(row_biases, ("dp", "tensor"), axis=1, tiled=True),
    )
    shards = (qkv_weight, qv_bias, out_weight, up_weight, up_bias, down_weight)
    dp_count = lax.axis_size("dp")
    seq_len = segment_ids.shape[1]
    heads_local = qv_bias.shape[1]
    width_local = heads_local * HEAD_DIM
    scale = HEAD_DIM ** (-0.5)

    def micro_step(carry, inputs):
        rows_in, segments, grad_rows = inputs
        qkv_full, qv_full, out_full, up_full, upb_full, down_full = (
            lax.all_gather(shards[0], "dp", axis=1, tiled=True),
            lax.all_gather(shards[1], "dp", axis=2, tiled=True),
            lax.all_gather(shards[2], "dp", axis=1, tiled=True),
            lax.all_gather(shards[3], "dp", axis=0, tiled=True),
            lax.all_gather(shards[4], "dp", axis=1, tiled=True),
            lax.all_gather(shards[5], "dp", axis=1, tiled=True),
        )
        gathered = lax.all_gather(rows_in, "tensor", axis=0, tiled=True)
        projected = jnp.einsum(
            "rd,kdc->krc", gathered, qkv_full, preferred_element_type=jnp.float32
        )
        bias_flat = qv_full.reshape(2, width_local).astype(jnp.float32)
        split = (seq_len, heads_local, HEAD_DIM)
        query = (projected[0] + bias_flat[0]).astype(jnp.bfloat16).reshape(split)
        keys = projected[1].astype(jnp.bfloat16).reshape(split)
        values = (projected[2] + bias_flat[1]).astype(jnp.bfloat16).reshape(split)
        keep_mask = segments[:, None] == segments[None, :]
        attended, logsumexp = attend(query, keys, values, keep_mask, scale)
        context = attended.reshape(seq_len, width_local).astype(jnp.bfloat16)
        attention = lax.psum_scatter(
            jnp.dot(context, out_full, preferred_element_type=jnp.float32).astype(jnp.bfloat16),
            "tensor",
            scatter_dimension=0,
            tiled=True,
        ).astype(jnp.float32)
        residual_one = rows_in.astype(jnp.float32) + attention + biases_all[0]
        hidden, normed_one, inverse_one = normalize(residual_one, gains_all[0], biases_all[1])
        hidden_rows = lax.all_gather(hidden.astype(jnp.bfloat16), "tensor", axis=0, tiled=True)
        upper = jnp.dot(
            hidden_rows, up_full, preferred_element_type=jnp.float32
        ) + upb_full.reshape(-1).astype(jnp.float32)
        activated = gelu_exact(upper).astype(jnp.bfloat16)
        branch = lax.psum_scatter(
            jnp.dot(activated, down_full, preferred_element_type=jnp.float32).astype(jnp.bfloat16),
            "tensor",
            scatter_dimension=0,
            tiled=True,
        ).astype(jnp.float32)
        residual_two = hidden + branch + biases_all[2]
        result, normed_two, inverse_two = normalize(residual_two, gains_all[1], biases_all[3])
        qkv_back, qv_back, out_back, up_back, upb_back, down_back = (
            lax.all_gather(shards[0], "dp", axis=1, tiled=True),
            lax.all_gather(shards[1], "dp", axis=2, tiled=True),
            lax.all_gather(shards[2], "dp", axis=1, tiled=True),
            lax.all_gather(shards[3], "dp", axis=0, tiled=True),
            lax.all_gather(shards[4], "dp", axis=1, tiled=True),
            lax.all_gather(shards[5], "dp", axis=1, tiled=True),
        )
        grad_output = grad_rows.astype(jnp.float32)
        gain_two_grad = jnp.sum(grad_output * normed_two, axis=0)
        shift_two_grad = jnp.sum(grad_output, axis=0)
        grad_two = norm_back(grad_output, normed_two, inverse_two, gains_all[1])
        down_bias_grad = jnp.sum(grad_two, axis=0)
        branch_rows = lax.all_gather(grad_two.astype(jnp.bfloat16), "tensor", axis=0, tiled=True)
        down_grad = jnp.einsum(
            "rf,rd->fd", activated, branch_rows, preferred_element_type=jnp.float32
        )
        grad_active = jnp.einsum(
            "rd,fd->rf", branch_rows, down_back, preferred_element_type=jnp.float32
        )
        gelu_pull = jax.vjp(gelu_exact, upper)[1]
        grad_upper = gelu_pull(grad_active)[0].astype(jnp.bfloat16)
        up_bias_grad = jnp.sum(grad_upper.astype(jnp.float32), axis=0).reshape(1, -1)
        up_grad = jnp.einsum(
            "rd,rf->df", hidden_rows, grad_upper, preferred_element_type=jnp.float32
        )
        grad_hidden = grad_two + lax.psum_scatter(
            jnp.einsum("rf,df->rd", grad_upper, up_back, preferred_element_type=jnp.float32).astype(
                jnp.bfloat16
            ),
            "tensor",
            scatter_dimension=0,
            tiled=True,
        ).astype(jnp.float32)
        gain_one_grad = jnp.sum(grad_hidden * normed_one, axis=0)
        shift_one_grad = jnp.sum(grad_hidden, axis=0)
        grad_one = norm_back(grad_hidden, normed_one, inverse_one, gains_all[0])
        out_bias_grad = jnp.sum(grad_one, axis=0)
        attention_rows = lax.all_gather(grad_one.astype(jnp.bfloat16), "tensor", axis=0, tiled=True)
        out_grad = jnp.einsum(
            "rc,rd->cd", context, attention_rows, preferred_element_type=jnp.float32
        )
        grad_context = (
            jnp.einsum("rd,cd->rc", attention_rows, out_back, preferred_element_type=jnp.float32)
            .astype(jnp.bfloat16)
            .reshape(split)
        )
        grad_query, grad_keys, grad_values = attend_back(
            query, keys, values, keep_mask, logsumexp, grad_context, scale
        )
        grad_qkv = (
            jnp.stack([grad_query, grad_keys, grad_values])
            .reshape(3, seq_len, width_local)
            .astype(jnp.bfloat16)
        )
        bias_sums = jnp.sum(jnp.stack([grad_qkv[0], grad_qkv[2]]).astype(jnp.float32), axis=1)
        qv_grad = bias_sums.reshape(2, heads_local, HEAD_DIM)
        qkv_grad = jnp.einsum("rd,krc->kdc", gathered, grad_qkv, preferred_element_type=jnp.float32)
        input_grad = (
            grad_one
            + lax.psum_scatter(
                jnp.einsum(
                    "krc,kdc->rd", grad_qkv, qkv_back, preferred_element_type=jnp.float32
                ).astype(jnp.bfloat16),
                "tensor",
                scatter_dimension=0,
                tiled=True,
            ).astype(jnp.float32)
        ).astype(jnp.bfloat16)
        gains_grad = jnp.stack([gain_one_grad, gain_two_grad])
        biases_grad = jnp.stack([out_bias_grad, shift_one_grad, down_bias_grad, shift_two_grad])
        updates = (
            qkv_grad,
            qv_grad,
            out_grad,
            up_grad,
            up_bias_grad,
            down_grad,
            gains_grad,
            biases_grad,
        )
        carry = tuple((total + update for total, update in zip(carry, updates)))
        return (carry, (result.astype(jnp.bfloat16), input_grad))

    initial = (
        jnp.zeros((3, qkv_weight.shape[1] * dp_count, qkv_weight.shape[2]), jnp.float32),
        jnp.zeros((2, qv_bias.shape[1], qv_bias.shape[2] * dp_count), jnp.float32),
        jnp.zeros((out_weight.shape[0], out_weight.shape[1] * dp_count), jnp.float32),
        jnp.zeros((up_weight.shape[0] * dp_count, up_weight.shape[1]), jnp.float32),
        jnp.zeros((1, up_bias.shape[1] * dp_count), jnp.float32),
        jnp.zeros((down_weight.shape[0], down_weight.shape[1] * dp_count), jnp.float32),
        jnp.zeros(gains_all.shape, jnp.float32),
        jnp.zeros(biases_all.shape, jnp.float32),
    )
    totals, (outputs, input_grads) = lax.scan(
        micro_step, initial, (layer_input, segment_ids, cotangent)
    )
    qkv_sum, qv_sum, out_sum, up_sum, upb_sum, down_sum = (
        lax.psum_scatter(
            totals[0].astype(jnp.bfloat16), "dp", scatter_dimension=1, tiled=True
        ).astype(jnp.float32),
        lax.psum_scatter(
            totals[1].astype(jnp.bfloat16), "dp", scatter_dimension=2, tiled=True
        ).astype(jnp.float32),
        lax.psum_scatter(
            totals[2].astype(jnp.bfloat16), "dp", scatter_dimension=1, tiled=True
        ).astype(jnp.float32),
        lax.psum_scatter(
            totals[3].astype(jnp.bfloat16), "dp", scatter_dimension=0, tiled=True
        ).astype(jnp.float32),
        lax.psum_scatter(
            totals[4].astype(jnp.bfloat16), "dp", scatter_dimension=1, tiled=True
        ).astype(jnp.float32),
        lax.psum_scatter(
            totals[5].astype(jnp.bfloat16), "dp", scatter_dimension=1, tiled=True
        ).astype(jnp.float32),
    )
    gains_sum, biases_sum = (
        lax.psum_scatter(totals[6], ("dp", "tensor"), scatter_dimension=1, tiled=True),
        lax.psum_scatter(totals[7], ("dp", "tensor"), scatter_dimension=1, tiled=True),
    )
    return (
        outputs,
        input_grads,
        qkv_sum,
        qv_sum,
        out_sum,
        up_sum,
        upb_sum,
        down_sum,
        gains_sum,
        biases_sum,
    )


NEGATIVE = -1e30
LANES = 2 * HEAD_DIM


def half_mask(shape, half):
    lane = lax.broadcasted_iota(jnp.int32, shape, 1)
    return (lane // HEAD_DIM) == half


def attend_kernel(q_ref, k_ref, v_ref, row_ref, col_ref, context_ref, stats_ref):
    query, keys, values = q_ref[...], k_ref[...], v_ref[...]
    keep = col_ref[...] == row_ref[...]
    total = jnp.zeros(context_ref.shape, jnp.float32)
    for half in range(2):
        own = half_mask(query.shape, half)
        masked_query = jnp.where(own, query, 0) * jnp.asarray(HEAD_DIM**-0.5, query.dtype)
        scores = lax.dot_general(
            keys, masked_query, (((1,), (1,)), ((), ())), preferred_element_type=jnp.float32
        )
        scores = jnp.where(keep, scores, NEGATIVE)
        highest = jnp.max(scores, axis=0, keepdims=True)
        shifted = jnp.exp(scores - highest)
        sums = jnp.sum(shifted, axis=0, keepdims=True)
        probs = (shifted * (1.0 / sums)).astype(jnp.bfloat16)
        own_values = jnp.where(own, values, 0)
        total += lax.dot_general(
            probs, own_values, (((0,), (0,)), ((), ())), preferred_element_type=jnp.float32
        )
        stats_ref[0, half : half + 1, :] = highest + jnp.log(sums)
    context_ref[...] = total.astype(context_ref.dtype)


def attend_back_kernel(
    q_ref, k_ref, v_ref, grad_ref, row_ref, col_ref, stats_ref, *rest
):
    query, keys, values, grad = q_ref[...], k_ref[...], v_ref[...], grad_ref[...]
    scale = jnp.asarray(HEAD_DIM**-0.5, query.dtype)
    keep = col_ref[...] == row_ref[...]
    zero = jnp.zeros(query.shape, jnp.float32)
    grad_query, grad_keys, grad_values = zero, zero, zero
    for half in range(2):
        own = half_mask(query.shape, half)
        own_query = jnp.where(own, query, 0) * scale
        own_keys = jnp.where(own, keys, 0) * scale
        own_grad = jnp.where(own, grad, 0)
        contract_last = (((1,), (1,)), ((), ()))
        scores = lax.dot_general(
            keys, own_query, contract_last, preferred_element_type=jnp.float32
        )
        scores = jnp.where(keep, scores, NEGATIVE)
        probs = jnp.exp(scores - stats_ref[0, half : half + 1, :])
        grad_values += jnp.dot(
            probs.astype(jnp.bfloat16), own_grad, preferred_element_type=jnp.float32
        )
        grad_probs = lax.dot_general(
            values, own_grad, contract_last, preferred_element_type=jnp.float32
        )
        weighted = probs * grad_probs
        grad_scores = (weighted - probs * jnp.sum(weighted, axis=0, keepdims=True)).astype(
            jnp.bfloat16
        )
        grad_keys += jnp.dot(grad_scores, own_query, preferred_element_type=jnp.float32)
        grad_query += lax.dot_general(
            grad_scores, own_keys, (((0,), (0,)), ((), ())), preferred_element_type=jnp.float32
        )
    pair, out_ref = pl.program_id(0), rest[-1]
    width = out_ref.shape[1] // 3
    for place, value in enumerate((grad_query, grad_keys, grad_values)):
        start = pl.multiple_of(place * width + pair * LANES, LANES)
        out_ref[:, pl.ds(start, LANES)] = value.astype(out_ref.dtype)


def attention_specs(rows, pairs, parts):
    inner = pairs // parts

    def column(place):
        return pl.BlockSpec(
            (rows, LANES),
            lambda i: (0, (i // inner) * (3 * inner) + place * inner + lax.rem(i, inner)),
        )

    plain = pl.BlockSpec((rows, LANES), lambda i: (0, i))
    row_ids = pl.BlockSpec((1, rows), lambda i: (0, 0))
    column_ids = pl.BlockSpec((rows, 1), lambda i: (0, 0))
    stats = pl.BlockSpec((1, 2, rows), lambda i: (i, 0, 0))
    return [column(place) for place in range(3)], plain, [row_ids, column_ids], stats


def attend_call(projected, segments, parts):
    rows, width = projected.shape[0], projected.shape[1] // 3
    pairs = width // LANES
    columns, plain, ids, stats = attention_specs(rows, pairs, parts)
    return pl.pallas_call(
        attend_kernel,
        grid=(pairs,),
        in_specs=columns + ids,
        out_specs=[plain, stats],
        out_shape=[
            jax.ShapeDtypeStruct((rows, width), jnp.bfloat16),
            jax.ShapeDtypeStruct((pairs, 2, rows), jnp.float32),
        ],
        compiler_params=pltpu.CompilerParams(vmem_limit_bytes=14 * 1024 * 1024),
        cost_estimate=pl.CostEstimate(
            flops=56 * pairs * rows * rows * LANES,
            bytes_accessed=8 * rows * width,
            transcendentals=2 * pairs * rows * rows,
        ),
        name="attend",
    )(projected, projected, projected, segments[None, :], segments[:, None])


def attend_back_call(projected, grad, segments, stats_in, parts, part, others=None):
    rows, width = grad.shape
    inner = width // LANES // parts

    def column(place):
        return pl.BlockSpec(
            (rows, LANES), lambda i: (0, part * (3 * inner) + place * inner + i)
        )

    ids = [pl.BlockSpec((1, rows), lambda i: (0, 0)), pl.BlockSpec((rows, 1), lambda i: (0, 0))]
    stats = pl.BlockSpec((1, 2, rows), lambda i: (part * inner + i, 0, 0))
    plain = pl.BlockSpec((rows, LANES), lambda i: (0, part * inner + i))
    rest = [] if others is None else [others]
    return pl.pallas_call(
        attend_back_kernel,
        grid=(inner,),
        in_specs=[column(place) for place in range(3)]
        + [plain]
        + ids
        + [stats]
        + [pl.BlockSpec(memory_space=pl.ANY)] * len(rest),
        out_specs=pl.BlockSpec((rows, 3 * width // parts), lambda i: (0, part)),
        out_shape=jax.ShapeDtypeStruct((rows, 3 * width), jnp.bfloat16),
        input_output_aliases={7: 0} if rest else {},
        compiler_params=pltpu.CompilerParams(vmem_limit_bytes=14 * 1024 * 1024),
        cost_estimate=pl.CostEstimate(
            flops=136 * inner * rows * rows * LANES,
            bytes_accessed=14 * rows * width // parts,
            transcendentals=2 * inner * rows * rows,
        ),
        name="attend_back",
    )(
        projected,
        projected,
        projected,
        grad,
        segments[None, :],
        segments[:, None],
        stats_in,
        *rest,
    )


def dot_nn(a, b):
    return jnp.dot(a, b, preferred_element_type=jnp.float32)


def dot_nt(a, b):
    return lax.dot_general(a, b, (((1,), (1,)), ((), ())), preferred_element_type=jnp.float32)


def dot_tn(a, b):
    return lax.dot_general(a, b, (((0,), (0,)), ((), ())), preferred_element_type=jnp.float32)


def gelu_pair(values):
    cdf = 0.5 * (1.0 + lax.erf(values * (0.5**0.5)))
    density = jnp.exp(-0.5 * values * values) * (0.5 / jnp.pi) ** 0.5
    return values * cdf, cdf + values * density


PLANE = ("x", "c", "y")
EVERY = ("y", "x", "c", "z")
SWAP = [(0, 1), (1, 0)]


def plane_permutes():
    def index(x, c, y):
        return (x * 2 + c) * 2 + y

    cells = [(x, y) for x in range(2) for y in range(2)]
    along = [(index(x, 0, y), index(1 - x, 0, y)) for x, y in cells]
    along += [(index(x, 1, y), index(x, 1, 1 - y)) for x, y in cells]
    cross = [(index(x, 0, y), index(1 - x, 1, y)) for x, y in cells]
    cross += [(index(x, 1, y), index(x, 0, 1 - y)) for x, y in cells]
    return along, cross, [(target, source) for source, target in cross]


def after(value, *done):
    return lax.optimization_barrier((value,) + done)[0]


def barrier(*values):
    return lax.optimization_barrier(values)


def place_kernel(table_ref, *refs, widths):
    pieces = refs[:8]
    outs, held, arrived, left = refs[8:-3], refs[-3], refs[-2], refs[-1]
    loads, stores = [], []
    for i, piece in enumerate(pieces):
        loads.append(pltpu.make_async_copy(piece, held.at[i], arrived.at[i]))
        loads[-1].start()
    for i, piece in enumerate(pieces):
        size, start = piece.shape[0], 0
        row = pl.multiple_of(table_ref[i] * size, size)
        loads[i].wait()
        for j, (out, width) in enumerate(zip(outs, widths)):
            column = pl.multiple_of(table_ref[8 + i] * width, width)
            stores.append(
                pltpu.make_async_copy(
                    held.at[i, :, pl.ds(start, width)],
                    out.at[pl.ds(row, size), pl.ds(column, width)],
                    left.at[i, j],
                )
            )
            stores[-1].start()
            start += width
    for store in stores:
        store.wait()


def place(pieces, table, widths):
    size = pieces[0].shape[0]
    anywhere = pl.BlockSpec(memory_space=pl.ANY)
    return pl.pallas_call(
        functools.partial(place_kernel, widths=widths),
        grid_spec=pltpu.PrefetchScalarGridSpec(
            num_scalar_prefetch=1,
            grid=(1,),
            in_specs=[anywhere] * 8,
            out_specs=[anywhere] * len(widths),
            scratch_shapes=[
                pltpu.VMEM((8, size, sum(widths)), jnp.bfloat16),
                pltpu.SemaphoreType.DMA((8,)),
                pltpu.SemaphoreType.DMA((8, len(widths))),
            ],
        ),
        out_shape=[jax.ShapeDtypeStruct((4 * size, 2 * w), jnp.bfloat16) for w in widths],
        compiler_params=pltpu.CompilerParams(vmem_limit_bytes=16 * 1024 * 1024),
        cost_estimate=pl.CostEstimate(
            flops=0, bytes_accessed=32 * size * sum(widths), transcendentals=0
        ),
        name="place",
    )(table, *pieces)


def plane_spots(core, x, y):
    main = jnp.where(core == 0, 2 - 2 * x, 2 * x)
    part = jnp.where(core == 0, y, 1 - y)
    rows = [2 * x + core, main + core, main + 1 - core, 3 - 2 * x - core]
    return rows, [y, part, part, 1 - y]


def gather_weight(pieces, coords, widths):
    x, c, y, _ = coords
    pieces = pieces + [lax.ppermute(item, "c", SWAP) for item in pieces[2:]]
    (rows, parts), (partner_rows, partner_parts) = (plane_spots(k, x, y) for k in (c, 1 - c))
    order = [rows[0], partner_rows[0]] + rows[1:] + partner_rows[1:]
    order += [parts[0], partner_parts[0]] + parts[1:] + partner_parts[1:]
    return place(pieces, jnp.stack(order).astype(jnp.int32), widths)


def pack_kernel(qkv_ref, out_ref, tile_ref, packed_ref):
    count, _, width = qkv_ref.shape
    for i in range(count):
        packed_ref[:, i * width : (i + 1) * width] = qkv_ref[i]
    start = count * width
    packed_ref[:, start : start + width] = out_ref[...]
    packed_ref[:, start + width :] = tile_ref[...]


def pack(qkv, out, tile):
    count, rows, width = qkv.shape
    shape = (rows, (count + 1) * width + tile.shape[1])
    return pl.pallas_call(
        pack_kernel,
        out_shape=jax.ShapeDtypeStruct(shape, qkv.dtype),
        cost_estimate=pl.CostEstimate(
            flops=0, bytes_accessed=4 * shape[0] * shape[1], transcendentals=0
        ),
        name="pack",
    )(qkv, out, tile)


def three_parts(values, rows):
    parts = []
    for _ in range(3):
        parts.append(lax.reduce_precision(values, exponent_bits=8, mantissa_bits=7))
        values = values - parts[-1]
    tile = jnp.concatenate(parts).astype(jnp.bfloat16).reshape(-1, LANES)
    return jnp.pad(tile, ((0, rows - tile.shape[0]), (0, 0)))


class Reduction:
    def __init__(self, pairs, coords):
        self.pairs = pairs
        self.x, self.c, self.y, _ = coords
        self.along, self.cross, _ = plane_permutes()
        x, c, y = self.x, self.c, self.y
        self.main_row = jnp.where(c == 0, 2 - 2 * x, 2 * x)
        self.main_part = jnp.where(c == 0, y, 1 - y)
        self.partner_row = jnp.where(c == 0, 2 * x, 2 - 2 * x)
        self.partner_part = 1 - self.main_part

    def block(self, row, count, part, extras=()):
        pieces, start = [], 0
        pairs, extras = barrier(self.pairs, list(extras))
        for left, right in pairs:
            size, width = left.shape[1] // 4, right.shape[1] // 2
            picked = lax.dynamic_slice_in_dim(left, row * size, count * size, 1)
            total = dot_tn(picked, lax.dynamic_slice_in_dim(right, part * width, width, 1))
            for extra, at in extras:
                if at is not None:
                    extra = lax.dynamic_slice_in_dim(extra, at * size, count * size, 0)
                total = total + extra[:, start : start + width].astype(jnp.float32)
            pieces.append(total.astype(jnp.bfloat16))
            start += width
        return pieces[0] if len(pieces) == 1 else jnp.concatenate(pieces, axis=1)

    def send(self):
        corner = self.block(3 - 2 * self.x - self.c, 1, 1 - self.y)
        main = self.block(self.partner_row, 2, self.partner_part)
        self.corner_in = lax.ppermute(corner, "c", SWAP)
        self.main_in = lax.ppermute(main, "c", SWAP)
        return corner, main

    def spread(self):
        x, c, y = self.x, self.c, self.y
        corner = self.block(2 - 2 * x + c, 1, 1 - y, [(self.corner_in, None)])
        self.corner_got = lax.ppermute(corner, PLANE, self.cross)
        main = self.block(self.main_row + c, 1, self.main_part, [(self.main_in, c)])
        self.kept_got = lax.ppermute(main, PLANE, self.along)
        return corner, main

    def forward(self):
        extras = [(self.main_in, 1 - self.c), (self.corner_got, None)]
        main = self.block(self.main_row + 1 - self.c, 1, self.main_part, extras)
        self.passed_got = lax.ppermute(main, PLANE, self.along)
        return main

    def hand_over(self):
        home = self.block(2 * self.x + 1 - self.c, 1, self.y, [(self.passed_got, None)])
        self.home_in = lax.ppermute(home, "c", SWAP)
        return home

    def finish(self):
        home = self.block(2 * self.x + self.c, 1, self.y, [(self.kept_got, None), (self.home_in, None)])
        return home, lax.psum_scatter(home, "z", scatter_dimension=0, tiled=True)


def sequence_parallel(
    layer_input,
    segment_ids,
    qkv_weight,
    qv_bias,
    out_weight,
    up_weight,
    up_bias,
    down_weight,
    norm_gains,
    row_biases,
    cotangent,
):
    low = jnp.bfloat16
    parts = lax.axis_size("y")
    grid = tuple(lax.axis_size(name) for name in ("x", "c", "z"))
    dp_count = grid[0] * grid[1] * grid[2]
    mine = lax.axis_index("y")
    coords = tuple(lax.axis_index(name) for name in ("x", "c", "y", "z"))
    half, width = layer_input.shape[1:]
    heads_local = qv_bias.shape[1]
    width_local = heads_local * HEAD_DIM
    hidden_local = up_weight.shape[1]
    wide = 3 * width_local
    span = range(parts)

    source = jnp.arange(width).reshape(grid[2], grid[0], grid[1], -1)
    source = source.transpose(1, 2, 0, 3).reshape(-1)
    chosen = lax.broadcasted_iota(jnp.int32, (width, width), 0) == source[None, :]
    order = chosen.astype(low)

    def own_sequence(rows):
        kept = lax.dynamic_index_in_dim(rows, mine, 0, keepdims=False)
        sent = lax.dynamic_index_in_dim(rows, 1 - mine, 0, keepdims=False)
        return jnp.concatenate([kept, lax.ppermute(sent, "y", SWAP)], axis=0)

    def own_rows(rows):
        rows = dot_nt(rows.astype(low), order).astype(low)
        received = lax.ppermute(rows[half:], "y", SWAP)
        first = jnp.where(mine == 0, rows[:half], received)
        second = jnp.where(mine == 0, received, rows[:half])
        return jnp.stack([first, second])

    small = jnp.concatenate(
        [
            qv_bias.astype(jnp.float32).reshape(-1),
            up_bias.astype(jnp.float32).reshape(-1),
            norm_gains.reshape(-1),
            row_biases.reshape(-1),
        ]
    )
    packed = pack(qkv_weight, out_weight.T, three_parts(small, up_weight.shape[0]))

    def lane_of(piece):
        return lax.all_gather(piece, "z", axis=0, tiled=True)

    along, _, back = plane_permutes()

    def start_plane(lane):
        other = lax.ppermute(lane, "c", SWAP)
        main_other = lax.ppermute(other, PLANE, along)
        return [lane, other, lax.ppermute(lane, PLANE, along), main_other]

    lane = lane_of(packed)
    lane_up = lane_of(after(up_weight, packed))
    lane_down = lane_of(after(down_weight.T, packed))
    layer_input, cotangent = after((layer_input, cotangent), packed)
    rows_in, grad_output = own_sequence(layer_input), own_sequence(cotangent)
    lane, rows_in, grad_output = barrier(lane, rows_in, grad_output)
    pieces = start_plane(lane)
    rows_in, grad_output = after((rows_in, grad_output), pieces[1])
    rows_in, grad_output = (dot_nn(item, order).astype(low) for item in (rows_in, grad_output))
    pieces[2], pieces[3], rows_in, grad_output = barrier(
        pieces[2], pieces[3], rows_in, grad_output
    )
    pieces.append(lax.ppermute(pieces[2], PLANE, back))
    up_pieces = start_plane(after(lane_up, pieces[2]))
    pieces[4], up_pieces[1] = barrier(pieces[4], up_pieces[1])
    qkv_full, out_full, small_all = gather_weight(pieces, coords, (wide, width_local, LANES))
    segments = lax.dynamic_index_in_dim(segment_ids, mine, 0, keepdims=False)
    segments = jnp.where(mine == 0, segments, jnp.roll(segments, -half))

    small_all = small_all.reshape(grid + (-1, parts, LANES))[:, :, :, : 3 * small.size // LANES]
    small_all = small_all.astype(jnp.float32).transpose(4, 0, 1, 2, 3, 5)
    small_all = small_all.reshape((parts,) + grid + (3, small.size))
    small_all = small_all[..., 0, :] + small_all[..., 1, :] + small_all[..., 2, :]
    sizes = [qv_bias.size, up_bias.size, norm_gains.size, row_biases.size]
    starts = [0, sizes[0], sum(sizes[:2]), sum(sizes[:3])]

    def section(i, shard):
        values = small_all[..., starts[i] : starts[i] + sizes[i]]
        return values.reshape((parts,) + grid + shard.shape)

    qv_all = section(0, qv_bias).transpose(4, 0, 5, 3, 1, 2, 6).reshape(2, parts, width_local)
    upb_all = section(1, up_bias).transpose(0, 3, 1, 2, 4, 5).reshape(-1)

    def whole_rows(i, shard):
        values = section(i, shard).transpose(4, 1, 2, 3, 0, 5)
        return values.reshape(shard.shape[0], width)

    gains_all, biases_all = whole_rows(2, norm_gains), whole_rows(3, row_biases)
    none = jnp.zeros((width_local,), jnp.float32)
    qkv_bias = jnp.concatenate(
        [item for t in span for item in (qv_all[0, t], none, qv_all[1, t])]
    )

    up_pieces[2], qkv_full = barrier(up_pieces[2], qkv_full)
    projected = (dot_nn(rows_in, qkv_full) + qkv_bias).astype(low)
    up_pieces[3], projected = barrier(up_pieces[3], projected)
    up_pieces.append(lax.ppermute(after(up_pieces[2], projected), PLANE, back))
    down_pieces = start_plane(after(lane_down, projected))
    context, stats = attend_call(after(projected, down_pieces[1]), segments, parts)
    down_pieces[2], down_pieces[3], up_pieces[4], context = barrier(
        down_pieces[2], down_pieces[3], up_pieces[4], context
    )
    down_pieces.append(lax.ppermute(down_pieces[2], PLANE, back))
    attention = dot_nt(context, out_full)
    residual_one = rows_in.astype(jnp.float32) + attention + biases_all[0]
    hidden, normed_one, inverse_one = normalize(residual_one, gains_all[0], biases_all[1])
    hidden_low = hidden.astype(low)
    (up_full,) = gather_weight(up_pieces, coords, (hidden_local,))
    activated, slope = gelu_pair(
        dot_nn(hidden_low, up_full) + upb_all
    )
    activated, slope = activated.astype(low), slope.astype(low)
    down_pieces[4], activated = barrier(down_pieces[4], activated)
    (down_full,) = gather_weight(down_pieces, coords, (hidden_local,))
    branch = dot_nt(activated, down_full)
    residual_two = hidden + branch + biases_all[2]
    result, normed_two, inverse_two = normalize(residual_two, gains_all[1], biases_all[3])

    result_low = barrier(result.astype(low))[0]
    grad_output = grad_output.astype(jnp.float32)
    grad_two = norm_back(grad_output, normed_two, inverse_two, gains_all[1])
    branch_grad = grad_two.astype(low)

    down = Reduction([(branch_grad, activated)], coords)
    sent = down.send()
    columns = [slice(t * hidden_local, (t + 1) * hidden_local) for t in span]
    branch_late = after(branch_grad, *sent)
    grad_first = (dot_nn(branch_late, down_full[:, columns[0]]) * slope[:, columns[0]]).astype(low)
    down.corner_in = after(down.corner_in, grad_first)
    moved = down.spread()
    branch_late = after(branch_grad, *moved)
    grad_second = (dot_nn(branch_late, down_full[:, columns[1]]) * slope[:, columns[1]]).astype(low)
    grad_upper = jnp.concatenate([grad_first, grad_second], axis=1)
    up = Reduction([(hidden_low, grad_upper)], coords)
    sent = up.send()
    down.corner_got = after(down.corner_got, *sent)
    moved = down.forward()
    grad_hidden = grad_two + dot_nt(after(grad_upper, moved), up_full)
    grad_one = norm_back(grad_hidden, normed_one, inverse_one, gains_all[0])
    attention_grad = grad_one.astype(low)
    grad_context = dot_nn(attention_grad, out_full).astype(low)
    up.corner_in = after(up.corner_in, grad_context, down.kept_got)
    moved = up.spread()
    grad_projected = attend_back_call(
        projected, after(grad_context, *moved), segments, stats, parts, 0
    )
    down.passed_got = after(down.passed_got, grad_projected)
    moved = down.hand_over()
    up.corner_got = after(up.corner_got, moved)
    moved = up.forward()
    down.home_in = after(down.home_in, moved)
    moved, down_sum = down.finish()
    grad_projected = attend_back_call(
        projected, after(grad_context, moved), segments, stats, parts, 1, grad_projected
    )
    last = Reduction([(rows_in, grad_projected), (attention_grad, context)], coords)
    sent = last.send()
    up.passed_got = after(up.passed_got, *sent)
    moved = up.hand_over()
    last.corner_in = after(last.corner_in, moved, up.kept_got)
    moved = last.spread()
    up.home_in = after(up.home_in, *moved)
    moved, up_sum = up.finish()
    input_grad = grad_one + dot_nt(after(grad_projected, moved), qkv_full)
    last.corner_got = after(last.corner_got, input_grad)
    moved = last.forward()
    grad_output, grad_two, grad_hidden, grad_one, grad_upper, grad_projected = after(
        (grad_output, grad_two, grad_hidden, grad_one, grad_upper, grad_projected), moved
    )
    gain_two_grad = jnp.sum(grad_output * normed_two, axis=0)
    shift_two_grad = jnp.sum(grad_output, axis=0)
    down_bias_grad = jnp.sum(grad_two, axis=0)
    gain_one_grad = jnp.sum(grad_hidden * normed_one, axis=0)
    shift_one_grad = jnp.sum(grad_hidden, axis=0)
    out_bias_grad = jnp.sum(grad_one, axis=0)
    upb_grad = jnp.sum(grad_upper.astype(jnp.float32), axis=0)
    qkv_sums = jnp.sum(grad_projected.astype(jnp.float32), axis=0)
    last.passed_got = after(
        last.passed_got,
        *(gain_two_grad, shift_two_grad, down_bias_grad, gain_one_grad),
        *(shift_one_grad, out_bias_grad, upb_grad, qkv_sums, last.kept_got),
    )
    moved = last.hand_over()
    moved, last_sum = last.finish()
    input_grads = own_rows(after(input_grad, moved))
    outputs = own_rows(after(result_low, moved))

    qkv_sums = qkv_sums.reshape(parts, 3, width_local)
    dp_order = (grid[2], grid[0], grid[1])
    qv_grads = jnp.stack([qkv_sums[:, 0], qkv_sums[:, 2]], axis=1)
    qv_grads = qv_grads.reshape((parts, 2, heads_local) + dp_order + (-1,))
    qv_grads = qv_grads.transpose(0, 4, 5, 3, 1, 2, 6).reshape(parts * dp_count, -1)
    upb_grad = upb_grad.reshape((parts,) + dp_order + (-1,))
    upb_grad = upb_grad.transpose(0, 2, 3, 1, 4).reshape(parts * dp_count, -1)

    def split_rows(rows):
        count = len(rows)
        rows = jnp.stack(rows).reshape((count,) + grid + (parts, -1))
        return rows.transpose(4, 1, 2, 3, 0, 5).reshape(parts * dp_count, -1)

    small_grad = jnp.concatenate(
        [
            qv_grads,
            upb_grad,
            split_rows([gain_one_grad, gain_two_grad]),
            split_rows([out_bias_grad, shift_one_grad, down_bias_grad, shift_two_grad]),
        ],
        axis=1,
    )
    small_grad = after(small_grad, moved)
    exchanged = lax.all_to_all(small_grad, EVERY, 0, 0, tiled=True)
    small_sum = jnp.sum(exchanged, axis=0)
    qv_sum, upb_sum, gains_sum, biases_sum = (
        small_sum[a : a + n] for a, n in zip(starts, sizes)
    )
    last_sum = last_sum.astype(jnp.float32)
    qkv_sum = last_sum[:, :wide].reshape(-1, 3, width_local).transpose(1, 0, 2)
    return (
        outputs,
        input_grads,
        qkv_sum,
        qv_sum.reshape(qv_bias.shape),
        last_sum[:, wide:].T,
        up_sum.astype(jnp.float32),
        upb_sum.reshape(up_bias.shape),
        down_sum.astype(jnp.float32).T,
        gains_sum.reshape(norm_gains.shape),
        biases_sum.reshape(row_biases.shape),
    )


def solution(mesh):
    groups = mesh.shape["dp"]
    parts = mesh.shape["tensor"]

    def program(*arrays):
        micro, width = arrays[0].shape[0], arrays[0].shape[2]
        fits = micro == 2 and parts == 2 and groups % 4 == 0 and width % (groups * 16) == 0
        if fits:
            dp, place = ("z", "x", "c"), "y"
            shape = (groups // 4, 2, 2, 2)
            used = Mesh(mesh.devices.reshape(shape), dp + (place,))
        else:
            dp, place, used = ("dp",), "tensor", mesh
        whole = dp + (place,)
        rows, vectors = P(None, whole, None), P(None, whole)
        weights = (
            P(None, dp, place),
            P(None, place, dp),
            P(place, dp),
            P(dp, place),
            P(place, dp),
            P(place, dp),
            vectors,
            vectors,
        )
        return jax.shard_map(
            sequence_parallel if fits else tensor_split,
            mesh=used,
            in_specs=(rows, P(None, dp)) + weights + (rows,),
            out_specs=(rows, rows) + weights,
            check_vma=False,
        )(*arrays)

    return program
```
